32 devices in a mesh: ctx: 8 (over z, y), fsdp: 4 (over x, core).
Axes of the slice: x: 2, y: 2, z: 4, core: 2. Of those that a mesh axis runs over, the one named last changes fastest.
Arguments:
- tokens: bfloat16 [8192, 1024], P(('fsdp', 'ctx')), may hold values from -6 to 6
- cotangent: bfloat16 [8192, 1024], P(('fsdp', 'ctx')), may hold values from -6 to 6
- gain_attn: bfloat16 [1024], P('fsdp'), may hold values from 0.5 to 1.5
- w_qkv: bfloat16 [1024, 3072], P('fsdp'), may hold values from -0.25 to 0.25
- w_out: bfloat16 [1024, 1024], P('fsdp'), may hold values from -0.75 to 0.75
- gain_ffn: bfloat16 [1024], P('fsdp'), may hold values from 0.5 to 1.5
- w_gate_up: bfloat16 [1024, 5632], P('fsdp'), may hold values from -0.1875 to 0.1875
- w_down: bfloat16 [2816, 1024], P('fsdp'), may hold values from -0.109375 to 0.109375
- lengths: int32 [4, 4], P('fsdp'), may hold values from 1 to 1024, 2048 in all within a row
- block_order: int32 [4, 32], P('fsdp'), may hold values from 0 to 31, each once within a row
Outputs:
- output: bfloat16 [8192, 1024], P(('fsdp', 'ctx'))
- grad_tokens: bfloat16 [8192, 1024], P(('fsdp', 'ctx'))
- grad_gain_attn: float32 [1024], P('fsdp')
- grad_w_qkv: float32 [1024, 3072], P('fsdp')
- grad_w_out: float32 [1024, 1024], P('fsdp')
- grad_gain_ffn: float32 [1024], P('fsdp')
- grad_w_gate_up: float32 [1024, 5632], P('fsdp')
- grad_w_down: float32 [2816, 1024], P('fsdp')
The draws below stay inside these ranges and needn't reach their ends.
Inputs may be any that keep to these rules, and one draw needn't show every extreme that they name: Each row gives the lengths of the 4 sequences that fill one group's 2048 tokens, in sequence order; the longest is exactly 1024. `block_order`: each row is a permutation of the 32 blocks of one group.
All inputs are finite; a program needn't handle non-finite values.
Results may differ from the reference program's by a relative error of at most 0.024.
Values may be sent and summed in bfloat16 or wider, within the bound.
No kernel may reach another device: no remote copies, remote signals or barrier semaphores. Data moves between devices by JAX's collectives and lax.ppermute only.
A program may use at most 256 MiB of HBM per device.

```python
import math
import jax
import jax.numpy as jnp
import numpy as np
from jax import lax

D = 1024
HEADS = 16
FF = 2816
HEAD_DIM = 64
NSEQ = 4
BLOCK = 64
GROUP = 2048
TOKENS = 8192
NBLK = 32
LONGEST = 1024
N_FSDP = 4


def levels(rng, dims, cuts, smallest, high):
    level, own = 1.0, jax.random.fold_in(rng, 6)
    for position, blocks in cuts:
        draws = jnp.exp(jax.random.uniform(jax.random.fold_in(own, position), (blocks,), jnp.float32, smallest / len(cuts), high / len(cuts)))
        level = level * jnp.repeat(draws, dims[position] // blocks).reshape([-1 if axis == position else 1 for axis in range(len(dims))])
    return level


def length_profile(amount, total, most, skew):
    portions = [(1 << 20) // math.isqrt(grade ** skew) + 1 for grade in range(2, amount + 1)]
    surplus, holding = total - most - (amount - 1), [1] * (amount - 1)
    while surplus > 0:
        movable = [i for i in range(amount - 1) if holding[i] < most]
        whole, left = sum([portions[i] for i in movable]), surplus
        for i in movable:
            addition = min(most - holding[i], max(1, left * portions[i] // whole), surplus)
            holding[i] = holding[i] + addition
            surplus = surplus - addition
    return np.array([most] + holding)


def ragged_sizes(stream_key, amount, total, reach, slope):
    if amount == 2:
        one = jax.random.randint(stream_key, (), max(1, total - reach), min(reach, total - 1) + 1)
        return jnp.stack([one, total - one])
    sizes = jnp.asarray(length_profile(amount, total, reach, slope), jnp.int32)
    couples = (amount - 1) // 2
    source_of, taker = sizes[1:1 + 2 * couples:2], sizes[2:2 + 2 * couples:2]
    margin = jnp.minimum(source_of - 1, reach - taker)
    moved = jax.random.randint(jax.random.fold_in(stream_key, 1), (couples,), 0, 1 << 20) % (margin + 1)
    sizes = sizes.at[1:1 + 2 * couples:2].set(source_of - moved).at[2:2 + 2 * couples:2].set(taker + moved)
    return sizes[jax.random.permutation(jax.random.fold_in(stream_key, 2), amount)]


def scatter_about(stream_key, extent, width, limit, cuts=(), held_as=jnp.bfloat16):
    loudness = levels(stream_key, extent, cuts, -0.22, 0.18) if cuts else 1.0
    entries = jax.random.normal(stream_key, extent, jnp.float32) * width * loudness
    return jnp.minimum(jnp.maximum(entries, -limit), limit).astype(held_as)


def setup_inputs(seed: int = 0) -> dict:
    seeds = jax.random.split(jax.random.key(seed), 11)
    return {
        "tokens": scatter_about(seeds[0], (TOKENS, D), 1.0, 6.0, ((0, 32),)),
        "cotangent": scatter_about(seeds[1], (TOKENS, D), 1.0, 6.0, ((0, 32),)),
        "gain_attn": jnp.clip(1.0 + 0.1 * jax.random.normal(seeds[2], (D,), jnp.float32), 0.5, 1.5).astype(jnp.bfloat16),
        "w_qkv": scatter_about(seeds[3], (D, 3 * D), (D // 2) ** -0.5, 0.25, ((0, 4),)),
        "w_out": scatter_about(seeds[4], (D, D), (D // 16) ** -0.5, 0.75, ((0, 4),)),
        "gain_ffn": jnp.clip(1.0 + 0.1 * jax.random.normal(seeds[5], (D,), jnp.float32), 0.5, 1.5).astype(jnp.bfloat16),
        "w_gate_up": scatter_about(seeds[6], (D, 2 * FF), D ** -0.5, 0.1875, ((0, 4),)),
        "w_down": scatter_about(seeds[7], (FF, D), FF ** -0.5, 0.109375, ((0, 4),)),
        "lengths": jax.vmap(lambda own: ragged_sizes(own, NSEQ, GROUP, LONGEST, 2))(jax.random.split(seeds[8], N_FSDP)).reshape((N_FSDP, NSEQ)).astype(jnp.int32),
        "block_order": jax.vmap(lambda own: jax.random.permutation(own, NBLK))(jax.random.split(seeds[9], N_FSDP)).reshape((N_FSDP, NBLK)).astype(jnp.int32),
    }


EPS = 1e-05
HIGH = lax.Precision.HIGHEST

@jax.custom_vjp
def low(v):
    return lax.optimization_barrier(v.astype(jnp.bfloat16)).astype(jnp.float32)

@jax.custom_vjp
def low_back(v):
    return v

def low_keep(v):
    return (low(v), None)

def low_pass(kept, grad):
    return (grad,)

def back_keep(v):
    return (v, None)

def back_low(kept, grad):
    return (low(grad),)
low.defvjp(low_keep, low_pass)
low_back.defvjp(back_keep, back_low)

def mixed(left, right):
    return jnp.dot(left, right, precision=HIGH)

def rms(rows, gain):
    return rows * lax.rsqrt(lax.optimization_barrier(jnp.mean(rows * rows, axis=-1, keepdims=True)) + EPS) * gain

def order_of(order_row, length_row):
    positions = (order_row[:, None] * BLOCK + jnp.arange(BLOCK, dtype=jnp.int32)[None, :]).reshape(GROUP)
    ends = jnp.cumsum(length_row).astype(jnp.int32)
    segment = lax.optimization_barrier(jnp.sum((positions[:, None] >= ends[None, :]).astype(jnp.int32), axis=1)).astype(jnp.int32)
    return (positions, segment)

def group_attention(items):
    query, keys, values, positions, segment = items
    query_rows = min(512, GROUP)
    scale = HEAD_DIM ** (-0.5)

    def one_block(parts):
        query_block, query_pos, query_seg = parts
        scores = jnp.einsum('qhd,khd->qhk', query_block, keys, precision=HIGH) * scale
        scores = low_back(scores)
        allowed = (query_seg[:, None] == segment[None, :]) & (positions[None, :] <= query_pos[:, None])
        scores = jnp.where(allowed[:, None, :], scores, -1e+30)
        probs = low(jax.nn.softmax(scores, axis=-1))
        return jnp.einsum('qhk,khd->qhd', probs, values, precision=HIGH)
    count = GROUP // query_rows
    result = lax.map(jax.checkpoint(one_block), (query.reshape(count, query_rows, HEADS, HEAD_DIM), positions.reshape(count, query_rows), segment.reshape(count, query_rows)))
    return result.reshape(GROUP, HEADS, HEAD_DIM)

def reference(tokens, cotangent, gain_attn, w_qkv, w_out, gain_ffn, w_gate_up, w_down, lengths, block_order):
    pos_all, seg_all = jax.vmap(order_of)(block_order, lengths)

    def forward(inputs, gain_one, weight_qkv, weight_out, gain_two, weight_gu, weight_down):
        attn_in = low(rms(inputs, gain_one))
        qkv = mixed(attn_in, weight_qkv)
        query = low(low_back(qkv[:, :D]))
        keys = low(low_back(qkv[:, D:2 * D]))
        values = low(low_back(qkv[:, 2 * D:]))
        shape = (N_FSDP, GROUP, HEADS, HEAD_DIM)
        attn = lax.map(jax.checkpoint(group_attention), (query.reshape(shape), keys.reshape(shape), values.reshape(shape), pos_all, seg_all))
        attn = low(low_back(attn.reshape(TOKENS, D)))
        resid = inputs + low_back(mixed(attn, weight_out))
        ffn_in = low(rms(resid, gain_two))
        gate_up = mixed(ffn_in, weight_gu)
        gate = low_back(gate_up[:, :FF])
        upward = low_back(gate_up[:, FF:])
        hidden = low(gate * jax.nn.sigmoid(gate) * upward)
        return resid + low_back(mixed(hidden, weight_down))
    primals = (tokens.astype(jnp.float32), gain_attn.astype(jnp.float32), w_qkv.astype(jnp.float32), w_out.astype(jnp.float32), gain_ffn.astype(jnp.float32), w_gate_up.astype(jnp.float32), w_down.astype(jnp.float32))
    result, pullback = jax.vjp(forward, *primals)
    grads = pullback(cotangent.astype(jnp.float32))
    factor = 1.0 / math.sqrt(TOKENS)
    return (result.astype(jnp.bfloat16), grads[0].astype(jnp.bfloat16), grads[1] * factor, grads[2] * factor, grads[3] * factor, grads[4] * factor, grads[5] * factor, grads[6] * factor)
```

```python
import functools
import math

import jax
import jax.numpy as jnp
from jax import lax
from jax.experimental import pallas as pl
from jax.experimental.pallas import tpu as pltpu
from jax.sharding import PartitionSpec as P

HEADS = 16
TILE = 256


EPS = 1e-05
MASKED=-1e30
def nt(a,b): return lax.dot_general(a,b,(((1,),(1,)),((),())),preferred_element_type=jnp.float32)
def nn(a,b): return lax.dot_general(a,b,(((1,),(0,)),((),())),preferred_element_type=jnp.float32)

def first_tile(ends_ref, nseq, position, tile):
    start = jnp.int32(0)
    for i in range(nseq - 1):
        start = jnp.where(ends_ref[i] <= position, ends_ref[i], start)
    return start // tile

def last_tile(ends_ref, nseq, position, tile):
    end = ends_ref[nseq - 1]
    for i in range(nseq - 2, -1, -1):
        end = jnp.where(ends_ref[i] > position, ends_ref[i], end)
    return (end - 1) // tile

def seen(ends_ref, nseq, query_start, key_start, tile):
    pos_query = query_start + lax.broadcasted_iota(jnp.int32, (1, tile), 1)
    start = jnp.zeros((1, tile), jnp.int32)
    for i in range(nseq - 1):
        start = jnp.where(pos_query >= ends_ref[i], ends_ref[i], start)
    pos_key = key_start + lax.broadcasted_iota(jnp.int32, (tile, tile), 0)
    return (pos_key <= pos_query) & (pos_key >= start)

def head_lanes(x, head, heads, depth):
    if heads == 1:
        return x
    lane = lax.broadcasted_iota(jnp.int32, x.shape, 1)
    return jnp.where((lane >= head * depth) & (lane < (head + 1) * depth), x, jnp.zeros_like(x))

def fwd_kernel(meta, ends_ref, place_ref, *refs):
    n, heads, depth, tile, block, nseq = meta
    qkv_refs, out_refs = refs[:n], refs[n:2*n]
    out_t_ref, lse_ref = refs[2*n], refs[2*n+1]
    q_ref, k_ref, v_ref, o_ref = refs[2*n+2:]
    width = heads*depth
    scale = depth ** (-0.5)
    per = qkv_refs[0].shape[0] // block
    for s in range(n):
        for b in range(per):
            dst = pl.ds(pl.multiple_of(place_ref[s*per+b]*block, block), block)
            src = pl.ds(b*block, block)
            q = qkv_refs[s][src, 0:width].astype(jnp.float32)*scale
            for h in range(heads):
                q_ref[h, dst, :] = head_lanes(q, h, heads, depth).astype(jnp.bfloat16)
            k_ref[dst, :] = qkv_refs[s][src, width:2*width]
            v_ref[dst, :] = qkv_refs[s][src, 2*width:]
    tiles = q_ref.shape[1] // tile
    def one_query(t, _):
        rows = pl.ds(pl.multiple_of(t*tile, tile), tile)
        qs = [q_ref[h, rows, :] for h in range(heads)]
        def one_key(j, carry):
            keys = pl.ds(pl.multiple_of(j*tile, tile), tile)
            k = k_ref[keys, :]
            v_t = jnp.transpose(v_ref[keys, :].astype(jnp.float32)).astype(jnp.bfloat16)
            mask = seen(ends_ref, nseq, t*tile, j*tile, tile)
            new = []
            for h in range(heads):
                m, l, acc = carry[h]
                s = jnp.where(mask, nt(k, qs[h]), MASKED)
                m_new = jnp.maximum(m, jnp.max(s, axis=0, keepdims=True))
                e = jnp.exp(s - m_new)
                alpha = jnp.exp(m - m_new)
                l = l*alpha + jnp.sum(e, axis=0, keepdims=True)
                acc = acc*alpha + nn(v_t[h*depth:(h+1)*depth], e.astype(jnp.bfloat16))
                new.append((m_new, l, acc))
            return tuple(new)
        init = tuple((jnp.full((1,tile),MASKED,jnp.float32), jnp.zeros((1,tile),jnp.float32), jnp.zeros((depth,tile),jnp.float32)) for _ in range(heads))
        final = lax.fori_loop(first_tile(ends_ref, nseq, t*tile, tile), t+1, one_key, init)
        outs = []
        for h in range(heads):
            m, l, acc = final[h]
            outs.append(acc / l)
            lse_ref[h:h+1, rows] = m + jnp.log(l)
        out_t = jnp.concatenate(outs, axis=0) if heads > 1 else outs[0]
        out_t_ref[:, rows] = out_t
        o_ref[rows, :] = jnp.transpose(out_t).astype(jnp.bfloat16)
        return 0
    lax.fori_loop(0, tiles, one_query, 0)
    for s in range(n):
        for b in range(per):
            src = pl.ds(pl.multiple_of(place_ref[s*per+b]*block, block), block)
            out_refs[s][pl.ds(b*block, block), :] = o_ref[src, :]

def bwd_kernel(meta, ends_ref, place_ref, *refs):
    n, heads, depth, tile, block, nseq = meta
    qkv_refs, grad_refs = refs[:n], refs[n:2*n]
    out_t_ref, lse_ref = refs[2*n], refs[2*n+1]
    dqkv_refs = refs[2*n+2:3*n+2]
    q_ref, k_ref, v_ref, g_ref, k_t_ref, delta_ref, dq_t_ref, dq_ref, dk_ref, dv_ref = refs[3*n+2:]
    width = heads*depth
    scale = depth ** (-0.5)
    per = qkv_refs[0].shape[0] // block
    total = k_ref.shape[0]
    for s in range(n):
        for b in range(per):
            dst = pl.ds(pl.multiple_of(place_ref[s*per+b]*block, block), block)
            src = pl.ds(b*block, block)
            q = qkv_refs[s][src, 0:width].astype(jnp.float32)*scale
            g = grad_refs[s][src, :]
            for h in range(heads):
                q_ref[h, dst, :] = head_lanes(q, h, heads, depth).astype(jnp.bfloat16)
                g_ref[h, dst, :] = head_lanes(g.astype(jnp.float32), h, heads, depth).astype(jnp.bfloat16)
            k_ref[dst, :] = qkv_refs[s][src, width:2*width]
            v_ref[dst, :] = qkv_refs[s][src, 2*width:]
    tiles = total // tile
    def prepare(t, _):
        rows = pl.ds(pl.multiple_of(t*tile, tile), tile)
        k_t_ref[:, rows] = jnp.transpose(k_ref[rows, :].astype(jnp.float32)).astype(jnp.bfloat16)
        g = g_ref[0, rows, :].astype(jnp.float32)
        for h in range(1, heads):
            g = g + g_ref[h, rows, :].astype(jnp.float32)
        prod = jnp.transpose(g) * out_t_ref[:, rows]
        for h in range(heads):
            delta_ref[h:h+1, rows] = jnp.sum(prod[h*depth:(h+1)*depth], axis=0, keepdims=True)
        dq_t_ref[:, rows] = jnp.zeros((width, tile), jnp.float32)
        return 0
    lax.fori_loop(0, tiles, prepare, 0)
    def one_key(j, _):
        keys = pl.ds(pl.multiple_of(j*tile, tile), tile)
        k = k_ref[keys, :]
        v = v_ref[keys, :]
        k_t = k_t_ref[:, keys]
        dk_ref[keys, :] = jnp.zeros((tile, width), jnp.float32)
        dv_ref[keys, :] = jnp.zeros((tile, width), jnp.float32)
        def one_query(t, _):
            rows = pl.ds(pl.multiple_of(t*tile, tile), tile)
            mask = seen(ends_ref, nseq, t*tile, j*tile, tile)
            dk = dk_ref[keys, :]
            dv = dv_ref[keys, :]
            for h in range(heads):
                q = q_ref[h, rows, :]
                g = g_ref[h, rows, :]
                s = nt(k, q)
                p = jnp.where(mask, jnp.exp(s - lse_ref[h:h+1, rows]), 0.0)
                dp = nt(v, g)
                ds = (p*(dp - delta_ref[h:h+1, rows])).astype(jnp.bfloat16)
                dv = dv + nn(p.astype(jnp.bfloat16), g)
                dk = dk + nn(ds, q)
                part = pl.ds(h*depth, depth)
                dq_t_ref[part, rows] = dq_t_ref[part, rows] + nn(k_t[h*depth:(h+1)*depth], ds)
            dk_ref[keys, :] = dk
            dv_ref[keys, :] = dv
            return 0
        lax.fori_loop(j, last_tile(ends_ref, nseq, j*tile + tile - 1, tile) + 1, one_query, 0)
        return 0
    lax.fori_loop(0, tiles, one_key, 0)
    def finish(t, _):
        rows = pl.ds(pl.multiple_of(t*tile, tile), tile)
        dq_ref[rows, :] = (jnp.transpose(dq_t_ref[:, rows])*scale).astype(jnp.bfloat16)
        return 0
    lax.fori_loop(0, tiles, finish, 0)
    for s in range(n):
        for b in range(per):
            src = pl.ds(pl.multiple_of(place_ref[s*per+b]*block, block), block)
            dst = pl.ds(b*block, block)
            dqkv_refs[s][dst, 0:width] = dq_ref[src, :]
            dqkv_refs[s][dst, width:2*width] = dk_ref[src, :].astype(jnp.bfloat16)
            dqkv_refs[s][dst, 2*width:] = dv_ref[src, :].astype(jnp.bfloat16)

SM=pl.BlockSpec(memory_space=pltpu.SMEM)
VM=pl.BlockSpec(memory_space=pltpu.VMEM)
def attention_forward(ends, place, qkv, heads, depth, block, tile):
    n=len(qkv); rows=qkv[0].shape[0]; total=n*rows; width=heads*depth
    meta=(n,heads,depth,tile,block,ends.shape[0])
    pairs=total*total//4
    res=pl.pallas_call(functools.partial(fwd_kernel,meta),
        out_shape=[jax.ShapeDtypeStruct((rows,width),jnp.bfloat16)]*n+[jax.ShapeDtypeStruct((width,total),jnp.float32),jax.ShapeDtypeStruct((heads,total),jnp.float32)],
        in_specs=[SM,SM]+[VM]*n, out_specs=[VM]*(n+2),
        scratch_shapes=[pltpu.VMEM((heads,total,width),jnp.bfloat16)]+[pltpu.VMEM((total,width),jnp.bfloat16)]*3,
        cost_estimate=pl.CostEstimate(flops=4*pairs*width,bytes_accessed=10*total*width,transcendentals=pairs*heads),
        name="attention_forward")(ends,place,*qkv)
    return list(res[:n]),res[n],res[n+1]
def attention_backward(ends, place, qkv, grads, out_t, lse, heads, depth, block, tile):
    n=len(qkv); rows=qkv[0].shape[0]; total=n*rows; width=heads*depth
    meta=(n,heads,depth,tile,block,ends.shape[0])
    pairs=total*total//4
    f32=jnp.float32; b16=jnp.bfloat16
    return pl.pallas_call(functools.partial(bwd_kernel,meta),
        out_shape=[jax.ShapeDtypeStruct((rows,3*width),b16)]*n,
        in_specs=[SM,SM]+[VM]*(2*n+2), out_specs=[VM]*n,
        scratch_shapes=[pltpu.VMEM((heads,total,width),b16),pltpu.VMEM((total,width),b16),pltpu.VMEM((total,width),b16),pltpu.VMEM((heads,total,width),b16),
          pltpu.VMEM((width,total),b16),pltpu.VMEM((heads,total),f32),pltpu.VMEM((width,total),f32),pltpu.VMEM((total,width),b16),pltpu.VMEM((total,width),f32),pltpu.VMEM((total,width),f32)],
        cost_estimate=pl.CostEstimate(flops=10*pairs*width,bytes_accessed=20*total*width,transcendentals=pairs*heads),
        name="attention_backward")(ends,place,*qkv,*grads,out_t,lse)


def contract_rows(left, right):
    return lax.dot_general(
        left, right, (((0,), (0,)), ((), ())), preferred_element_type=jnp.float32
    )


def against_rows(left, right):
    return lax.dot_general(
        left, right, (((1,), (1,)), ((), ())), preferred_element_type=jnp.float32
    )


def rms_forward(rows):
    inverse = lax.rsqrt(jnp.mean(rows * rows, axis=1, keepdims=True) + EPS)
    return (rows * inverse, inverse)


def ring_of(count):
    if count % 4 or count < 8:
        return list(range(count))
    across = count // 4
    order = []
    for along in range(4):
        columns = range(1, across) if along % 2 == 0 else range(across - 1, 0, -1)
        order += [along * across + column for column in columns]
    return order + [along * across for along in reversed(range(4))]


def ring_shift(value, ring, step):
    count = len(ring)
    return lax.ppermute(
        value, "ctx", [(ring[i], ring[(i + step) % count]) for i in range(count)]
    )


def ring_gather(value, ring):
    count = len(ring)
    half = count // 2
    slots = [None] * count
    slots[0] = value
    up = down = value
    for step in range(1, half):
        up = ring_shift(up, ring, 1)
        down = ring_shift(down, ring, -1)
        slots[count - step] = up
        slots[step] = down
    cut = value.shape[0] // 2
    slots[half] = (ring_shift(up[:cut], ring, 1), ring_shift(down[cut:], ring, -1))
    return slots


def ring_scatter(chunk, ring):
    count = len(ring)
    half = count // 2
    far = chunk(half)
    cut = far.shape[0] // 2
    up = ring_shift(far[:cut], ring, 1)
    down = ring_shift(far[cut:], ring, -1)
    for step in range(half - 1, 0, -1):
        mine_up, mine_down = chunk(step), chunk(count - step)
        if step == half - 1:
            mine_up = jnp.concatenate([add_low(mine_up[:cut], up), mine_up[cut:]], axis=0)
            mine_down = jnp.concatenate([mine_down[:cut], add_low(mine_down[cut:], down)], axis=0)
        else:
            mine_up, mine_down = add_low(mine_up, up), add_low(mine_down, down)
        up = ring_shift(mine_up, ring, 1)
        down = ring_shift(mine_down, ring, -1)
    return chunk(0).astype(jnp.float32) + up.astype(jnp.float32) + down.astype(jnp.float32)


def add_low(left, right):
    return (left.astype(jnp.float32) + right.astype(jnp.float32)).astype(jnp.bfloat16)


def partner(value, fsdp_count):
    return lax.ppermute(value, "fsdp", [(i, i ^ 1) for i in range(fsdp_count)])


def chip_shift(value, fsdp_count, step):
    return lax.ppermute(
        value, "fsdp", [(i, (i + 2 * step) % fsdp_count) for i in range(fsdp_count)]
    )


def side_gather(value, fsdp_count):
    slots = []
    for step in range(fsdp_count // 2):
        near = value if step == 0 else chip_shift(value, fsdp_count, -step)
        slots += [near, partner(near, fsdp_count)]
    return slots


def side_scatter(terms, fsdp_count):
    total = None
    for step in reversed(range(fsdp_count // 2)):
        near = terms[2 * step].astype(jnp.float32) + partner(
            terms[2 * step + 1], fsdp_count
        ).astype(jnp.float32)
        if step:
            near = chip_shift(near.astype(jnp.bfloat16), fsdp_count, step).astype(jnp.float32)
        total = near if total is None else total + near
    return total


def side_exchange(pieces, fsdp_count):
    received = []
    for step in range(fsdp_count // 2):
        for flip in (0, 1):
            piece = pieces[2 * step + flip]
            if step or flip:
                piece = lax.ppermute(
                    piece,
                    "fsdp",
                    [(i, ((i + 2 * step) % fsdp_count) ^ flip) for i in range(fsdp_count)],
                )
            received.append(piece)
    chips = fsdp_count // 2
    return [received[2 * ((chips - step) % chips) + flip] for step in range(chips) for flip in (0, 1)]


def pick(array, index):
    return lax.dynamic_index_in_dim(array, index, 0, keepdims=False)


def body(
    tokens, cotangent, gain_attn, w_qkv, w_out, gain_ffn, w_gate_up, w_down, lengths, block_order
):
    rows, width = tokens.shape
    heads = HEADS
    depth = width // heads
    ctx_count = lax.axis_size("ctx")
    fsdp_count = lax.axis_size("fsdp")
    group_rows = rows * ctx_count
    factor = 1.0 / math.sqrt(rows * ctx_count * fsdp_count)
    shard = width // fsdp_count
    hidden = w_down.shape[0]
    own_heads = heads // ctx_count
    own_width = own_heads * depth
    ring = ring_of(ctx_count)
    place_in_ring = [ring.index(i) for i in range(ctx_count)]
    me = jnp.asarray(place_in_ring, jnp.int32)[lax.axis_index("ctx")]
    owner = jnp.asarray(ring, jnp.int32)[(me + jnp.arange(ctx_count, dtype=jnp.int32)) % ctx_count]
    owners = [owner[k] for k in range(ctx_count)]
    my_chip, my_core = lax.axis_index("fsdp") // 2, lax.axis_index("fsdp") % 2
    sides = [
        ((my_chip + step) % (fsdp_count // 2)) * 2 + (my_core ^ flip)
        for step in range(fsdp_count // 2)
        for flip in (0, 1)
    ]
    block_size = group_rows // block_order.shape[1]
    per_shard = rows // block_size
    ends = jnp.cumsum(lengths[0]).astype(jnp.int32)
    place = block_order[0].reshape(ctx_count, per_shard)[owner].reshape(-1)

    gains = side_gather(jnp.stack([gain_attn, gain_ffn]), fsdp_count)
    gain_pair = jnp.zeros((2, fsdp_count, shard), jnp.bfloat16)
    for slot, side in zip(gains, sides):
        gain_pair = lax.dynamic_update_slice(gain_pair, slot[:, None, :], (0, side, 0))
    gain_pair = gain_pair.reshape(2, width).astype(jnp.float32)
    gain_one, gain_two = gain_pair[0], gain_pair[1]

    inputs = tokens.astype(jnp.float32)
    normed_one, inverse_one = rms_forward(inputs)
    attn_in = (normed_one * gain_one).astype(jnp.bfloat16)
    attn_slots = ring_gather(attn_in, ring)

    def stack_sides(slots):
        whole = jnp.zeros((fsdp_count,) + slots[0].shape, slots[0].dtype)
        for slot, side in zip(slots, sides):
            whole = lax.dynamic_update_slice_in_dim(whole, slot[None], side, 0)
        return whole

    columns = w_qkv.reshape(shard, 3, ctx_count, own_width)
    slice_mine = lax.dynamic_index_in_dim(columns, owners[0], 2, keepdims=False).reshape(shard, 3 * own_width)
    weight_mine = stack_sides(side_gather(slice_mine, fsdp_count)).reshape(width, 3 * own_width)

    gate_parts = w_gate_up.reshape(shard, 2, fsdp_count, hidden)
    gate_pieces = [
        lax.dynamic_index_in_dim(gate_parts, side, 2, keepdims=False).reshape(shard, 2 * hidden)
        for side in sides
    ]
    weight_gu = stack_sides(side_exchange(gate_pieces, fsdp_count)).reshape(width, 2 * hidden)
    weight_out = stack_sides(side_gather(w_out, fsdp_count)).reshape(ctx_count, own_width, width)
    weight_out = jnp.concatenate([pick(weight_out, owners[k]) for k in range(ctx_count)], axis=0)
    cot_all = jnp.concatenate(side_gather(cotangent, fsdp_count), axis=0)
    weight_qkv = stack_sides(side_gather(w_qkv, fsdp_count)).reshape(width, 3 * width)

    def project(value):
        return jnp.dot(value, weight_mine, preferred_element_type=jnp.float32).astype(jnp.bfloat16)

    half = ctx_count // 2
    attn_slots[half] = jnp.concatenate(attn_slots[half], axis=0)
    qkv = [project(slot) for slot in attn_slots]
    out_slots, out_t, log_total = attention_forward(
        ends, place, qkv, own_heads, depth, block_size, TILE
    )
    attn_parts = [out_slots[0]] + [None] * (ctx_count - 1)
    for k in range(1, ctx_count):
        attn_parts[ctx_count - k] = ring_shift(out_slots[k], ring, k)
    attn_low = jnp.concatenate(attn_parts, axis=1)
    resid = inputs + jnp.dot(attn_low, weight_out, preferred_element_type=jnp.float32)
    normed_two, inverse_two = rms_forward(resid)
    ffn_in = (normed_two * gain_two).astype(jnp.bfloat16)
    ffn_all = jnp.concatenate(side_gather(ffn_in, fsdp_count), axis=0)

    gate_up = jnp.dot(ffn_all, weight_gu, preferred_element_type=jnp.float32)
    gate = gate_up[:, :hidden]
    upward = gate_up[:, hidden:]
    sigma = jax.nn.sigmoid(gate)
    active = gate * sigma
    hidden_low = (active * upward).astype(jnp.bfloat16)
    grad_hidden = against_rows(cot_all, w_down)
    grad_gate = grad_hidden * upward * (sigma + gate * sigma * (1.0 - sigma))
    grad_up = grad_hidden * active
    grad_gu = jnp.concatenate([grad_gate, grad_up], axis=1).astype(jnp.bfloat16)
    grad_ffn_terms = against_rows(grad_gu, weight_gu).astype(jnp.bfloat16).reshape(fsdp_count, rows, width)
    grad_ffn_in = side_scatter([grad_ffn_terms[i] for i in range(fsdp_count)], fsdp_count)
    out_terms = jnp.dot(hidden_low, w_down, preferred_element_type=jnp.float32)
    out_terms = out_terms.astype(jnp.bfloat16).reshape(fsdp_count, rows, width)
    output = (
        resid + side_scatter([out_terms[i] for i in range(fsdp_count)], fsdp_count)
    ).astype(jnp.bfloat16)

    scaled_two = grad_ffn_in * gain_two
    inner_two = jnp.mean(scaled_two * normed_two, axis=1, keepdims=True)
    grad_resid = cotangent.astype(jnp.float32) + inverse_two * (scaled_two - normed_two * inner_two)
    grad_branch = grad_resid.astype(jnp.bfloat16)
    grad_attn = against_rows(grad_branch, weight_out).astype(jnp.bfloat16)
    grad_slots = [grad_attn[:, :own_width]] + [None] * (ctx_count - 1)
    for k in range(1, ctx_count):
        grad_slots[ctx_count - k] = ring_shift(grad_attn[:, k * own_width : (k + 1) * own_width], ring, k)
    grad_qkv = attention_backward(
        ends, place, qkv, grad_slots, out_t, log_total, own_heads, depth, block_size, TILE
    )
    grad_parts = [grad_qkv[0]] + [None] * (ctx_count - 1)
    for k in range(1, ctx_count):
        grad_parts[ctx_count - k] = ring_shift(grad_qkv[k], ring, k)
    by_owner = weight_qkv.reshape(width, 3, ctx_count, own_width)
    weight_rel = jnp.concatenate(
        [
            lax.dynamic_index_in_dim(by_owner, owners[k], 2, keepdims=False).reshape(width, 3 * own_width)
            for k in range(ctx_count)
        ],
        axis=1,
    )
    grad_attn_in = against_rows(jnp.concatenate(grad_parts, axis=1), weight_rel)
    scaled_one = grad_attn_in * gain_one
    inner_one = jnp.mean(scaled_one * normed_one, axis=1, keepdims=True)
    grad_tokens = (grad_resid + inverse_one * (scaled_one - normed_one * inner_one)).astype(jnp.bfloat16)

    sub = shard // ctx_count
    terms_gu = contract_rows(ffn_all, grad_gu).astype(jnp.bfloat16).reshape(fsdp_count, ctx_count, sub, 2 * hidden)
    terms_down = contract_rows(hidden_low, cot_all).astype(jnp.bfloat16).reshape(ctx_count, hidden // ctx_count, width)
    chunk_gu = ring_scatter(
        lambda k: lax.dynamic_index_in_dim(terms_gu, owners[k], 1, keepdims=False).reshape(
            fsdp_count * sub, 2 * hidden
        ),
        ring,
    ).astype(jnp.bfloat16)
    chunk_down = ring_scatter(lambda k: pick(terms_down, owners[k]), ring).astype(jnp.bfloat16)
    chunk_gu = chunk_gu.reshape(fsdp_count, sub, 2 * hidden)
    chunk_gu = side_exchange([pick(chunk_gu, side) for side in sides], fsdp_count)
    chunk_gu = stack_sides(chunk_gu).reshape(fsdp_count, sub, 2, hidden)
    chunk_gu = chunk_gu.transpose(1, 2, 0, 3).reshape(sub, 2 * fsdp_count * hidden)

    terms_out = contract_rows(attn_low, grad_branch).astype(jnp.bfloat16).reshape(ctx_count, own_width, width)
    ordered_out = jnp.zeros_like(terms_out)
    for k in range(ctx_count):
        ordered_out = lax.dynamic_update_slice_in_dim(ordered_out, terms_out[k : k + 1], owners[k], 0)
    ordered_out = ordered_out.reshape(fsdp_count, shard, width)
    part_out = side_scatter([pick(ordered_out, side) for side in sides], fsdp_count).astype(jnp.bfloat16)
    part_out = part_out.reshape(ctx_count, sub, width)
    chunk_out = ring_scatter(lambda k: pick(part_out, owners[k]), ring).astype(jnp.bfloat16)

    attn_all = jnp.concatenate(attn_slots, axis=0)
    terms_qkv = contract_rows(attn_all, jnp.concatenate(grad_qkv, axis=0)).astype(jnp.bfloat16)
    terms_qkv = terms_qkv.reshape(fsdp_count, shard, 3 * own_width)
    chunk_qkv = side_scatter([pick(terms_qkv, side) for side in sides], fsdp_count).astype(jnp.bfloat16)

    def gather_rows(chunk):
        slots = ring_gather(chunk, ring)
        whole = jnp.zeros((ctx_count,) + chunk.shape, jnp.float32)
        cut = chunk.shape[0] // 2
        for k in range(ctx_count):
            if k == half:
                for piece, start in zip(slots[k], (0, cut)):
                    whole = lax.dynamic_update_slice(
                        whole, (piece.astype(jnp.float32) * factor)[None], (owners[k], start, 0)
                    )
            else:
                whole = lax.dynamic_update_slice(
                    whole, (slots[k].astype(jnp.float32) * factor)[None], (owners[k], 0, 0)
                )
        return whole.reshape(-1, chunk.shape[1])

    grad_w_gate_up = gather_rows(chunk_gu)
    grad_w_down = gather_rows(chunk_down)
    grad_w_out = gather_rows(chunk_out)
    qkv_slots = ring_gather(chunk_qkv, ring)
    grad_w_qkv = jnp.zeros((shard, 3, ctx_count * own_width), jnp.float32)
    cut = shard // 2
    for k in range(ctx_count):
        pieces = zip(qkv_slots[k], (0, cut)) if k == half else ((qkv_slots[k], 0),)
        for piece, start in pieces:
            piece = (piece.astype(jnp.float32) * factor).reshape(-1, 3, own_width)
            grad_w_qkv = lax.dynamic_update_slice(grad_w_qkv, piece, (start, 0, owners[k] * own_width))
    grad_w_qkv = grad_w_qkv.reshape(shard, 3 * width)

    def gain_gradient(weight, grad_weight, gain):
        return jnp.sum(weight.astype(jnp.float32) * grad_weight, axis=1) / gain.astype(jnp.float32)

    return (
        output,
        grad_tokens,
        gain_gradient(w_qkv, grad_w_qkv, gain_attn),
        grad_w_qkv,
        grad_w_out,
        gain_gradient(w_gate_up, grad_w_gate_up, gain_ffn),
        grad_w_gate_up,
        grad_w_down,
    )


def solution(mesh):
    in_specs = (
        P(("fsdp", "ctx"), None),
        P(("fsdp", "ctx"), None),
        P("fsdp"),
        P("fsdp", None),
        P("fsdp", None),
        P("fsdp"),
        P("fsdp", None),
        P("fsdp", None),
        P("fsdp", None),
        P("fsdp", None),
    )
    out_specs = (
        P(("fsdp", "ctx"), None),
        P(("fsdp", "ctx"), None),
        P("fsdp"),
        P("fsdp", None),
        P("fsdp", None),
        P("fsdp"),
        P("fsdp", None),
        P("fsdp", None),
    )
    return jax.shard_map(body, mesh=mesh, in_specs=in_specs, out_specs=out_specs, check_vma=False)
```

```python
import functools
import math

import jax
import jax.numpy as jnp
from jax import lax
from jax.experimental import pallas as pl
from jax.experimental.pallas import tpu as pltpu
from jax.sharding import PartitionSpec as P

HEADS = 16
TILE = 256


EPS = 1e-05
MASKED=-1e30
def nt(a,b): return lax.dot_general(a,b,(((1,),(1,)),((),())),preferred_element_type=jnp.float32)
def nn(a,b): return lax.dot_general(a,b,(((1,),(0,)),((),())),preferred_element_type=jnp.float32)

def ends_of(lengths_ref):
    ends = [lengths_ref[0, 0]]
    for i in range(1, lengths_ref.shape[1]):
        ends.append(ends[-1] + lengths_ref[0, i])
    return ends

def first_tile(ends, position, tile):
    start = jnp.int32(0)
    for end in ends[:-1]:
        start = jnp.where(end <= position, end, start)
    return start // tile

def last_tile(ends, position, tile):
    last = ends[-1]
    for end in reversed(ends[:-1]):
        last = jnp.where(end > position, end, last)
    return (last - 1) // tile

def seen(ends, query_start, key_start, tile):
    pos_query = query_start + lax.broadcasted_iota(jnp.int32, (1, tile), 1)
    start = jnp.zeros((1, tile), jnp.int32)
    for end in ends[:-1]:
        start = jnp.where(pos_query >= end, end, start)
    pos_key = key_start + lax.broadcasted_iota(jnp.int32, (tile, tile), 0)
    return (pos_key <= pos_query) & (pos_key >= start)

def head_lanes(x, head, heads, depth):
    if heads == 1:
        return x
    lane = lax.broadcasted_iota(jnp.int32, x.shape, 1)
    return jnp.where((lane >= head * depth) & (lane < (head + 1) * depth), x, jnp.zeros_like(x))

def placed(slots, block, table, order_ref, per):
    number = 0
    for slot in slots:
        for row in range(0, slot.shape[0], block):
            position = order_ref[0, table[0, number // per] * per + number % per] * block
            yield slot, pl.ds(row, block), pl.ds(pl.multiple_of(position, block), block)
            number += 1

def fwd_kernel(meta, table, lengths_ref, order_ref, *refs):
    given, n, heads, depth, tile, block = meta
    qkv_refs, out_refs = refs[:given], refs[given:given+n]
    out_t_ref, lse_ref = refs[given+n], refs[given+n+1]
    q_ref, k_ref, v_ref, o_ref = refs[given+n+2:]
    ends = ends_of(lengths_ref)
    width = heads*depth
    scale = depth ** (-0.5)
    per = out_refs[0].shape[0] // block
    for slot, src, dst in placed(qkv_refs, block, table, order_ref, per):
        q = slot[src, 0:width].astype(jnp.float32)*scale
        for h in range(heads):
            q_ref[h, dst, :] = head_lanes(q, h, heads, depth).astype(jnp.bfloat16)
        k_ref[dst, :] = slot[src, width:2*width]
        v_ref[dst, :] = slot[src, 2*width:]
    tiles = q_ref.shape[1] // tile
    def one_query(t, _):
        rows = pl.ds(pl.multiple_of(t*tile, tile), tile)
        qs = [q_ref[h, rows, :] for h in range(heads)]
        def one_key(j, carry):
            keys = pl.ds(pl.multiple_of(j*tile, tile), tile)
            k = k_ref[keys, :]
            v_t = jnp.transpose(v_ref[keys, :].astype(jnp.float32)).astype(jnp.bfloat16)
            mask = seen(ends, t*tile, j*tile, tile)
            new = []
            for h in range(heads):
                m, l, acc = carry[h]
                s = jnp.where(mask, nt(k, qs[h]), MASKED)
                m_new = jnp.maximum(m, jnp.max(s, axis=0, keepdims=True))
                e = jnp.exp(s - m_new)
                alpha = jnp.exp(m - m_new)
                l = l*alpha + jnp.sum(e, axis=0, keepdims=True)
                acc = acc*alpha + nn(v_t[h*depth:(h+1)*depth], e.astype(jnp.bfloat16))
                new.append((m_new, l, acc))
            return tuple(new)
        init = tuple((jnp.full((1,tile),MASKED,jnp.float32), jnp.zeros((1,tile),jnp.float32), jnp.zeros((depth,tile),jnp.float32)) for _ in range(heads))
        final = lax.fori_loop(first_tile(ends, t*tile, tile), t+1, one_key, init)
        outs = []
        for h in range(heads):
            m, l, acc = final[h]
            outs.append(acc / l)
            lse_ref[h:h+1, rows] = m + jnp.log(l)
        out_t = jnp.concatenate(outs, axis=0) if heads > 1 else outs[0]
        out_t_ref[:, rows] = out_t
        o_ref[rows, :] = jnp.transpose(out_t).astype(jnp.bfloat16)
        return 0
    lax.fori_loop(0, tiles, one_query, 0)
    for slot, dst, src in placed(out_refs, block, table, order_ref, per):
        slot[dst, :] = o_ref[src, :]

def bwd_kernel(meta, table, lengths_ref, order_ref, *refs):
    given, n, heads, depth, tile, block = meta
    qkv_refs, grad_refs = refs[:given], refs[given:given+n]
    part_out_ref = refs[given+n]
    refs = refs[given-n:]
    out_t_ref, lse_ref = refs[2*n+1], refs[2*n+2]
    dqkv_refs = refs[2*n+3:3*n+3]
    ends = ends_of(lengths_ref)
    q_ref, k_ref, v_ref, g_ref, k_t_ref, delta_ref, dq_t_ref, dq_ref, dk_ref, dv_ref = refs[3*n+3:]
    width = heads*depth
    scale = depth ** (-0.5)
    per = dqkv_refs[0].shape[0] // block
    total = k_ref.shape[0]
    for slot, src, dst in placed(qkv_refs, block, table, order_ref, per):
        q = slot[src, 0:width].astype(jnp.float32)*scale
        for h in range(heads):
            q_ref[h, dst, :] = head_lanes(q, h, heads, depth).astype(jnp.bfloat16)
        k_ref[dst, :] = slot[src, width:2*width]
        v_ref[dst, :] = slot[src, 2*width:]
    for slot, src, dst in placed(grad_refs, block, table, order_ref, per):
        g = slot[src, :].astype(jnp.float32)
        for h in range(heads):
            g_ref[h, dst, :] = head_lanes(g, h, heads, depth).astype(jnp.bfloat16)
    tiles = total // tile
    def prepare(t, _):
        rows = pl.ds(pl.multiple_of(t*tile, tile), tile)
        k_t_ref[:, rows] = jnp.transpose(k_ref[rows, :].astype(jnp.float32)).astype(jnp.bfloat16)
        g = g_ref[0, rows, :].astype(jnp.float32)
        for h in range(1, heads):
            g = g + g_ref[h, rows, :].astype(jnp.float32)
        prod = jnp.transpose(g) * out_t_ref[:, rows]
        for h in range(heads):
            delta_ref[h:h+1, rows] = jnp.sum(prod[h*depth:(h+1)*depth], axis=0, keepdims=True)
        dq_t_ref[:, rows] = jnp.zeros((width, tile), jnp.float32)
        return 0
    lax.fori_loop(0, tiles, prepare, 0)
    def one_key(j, _):
        keys = pl.ds(pl.multiple_of(j*tile, tile), tile)
        k = k_ref[keys, :]
        v = v_ref[keys, :]
        k_t = k_t_ref[:, keys]
        dk_ref[keys, :] = jnp.zeros((tile, width), jnp.float32)
        dv_ref[keys, :] = jnp.zeros((tile, width), jnp.float32)
        def one_query(t, _):
            rows = pl.ds(pl.multiple_of(t*tile, tile), tile)
            mask = seen(ends, t*tile, j*tile, tile)
            dk = dk_ref[keys, :]
            dv = dv_ref[keys, :]
            for h in range(heads):
                q = q_ref[h, rows, :]
                g = g_ref[h, rows, :]
                s = nt(k, q)
                p = jnp.where(mask, jnp.exp(s - lse_ref[h:h+1, rows]), 0.0)
                dp = nt(v, g)
                ds = (p*(dp - delta_ref[h:h+1, rows])).astype(jnp.bfloat16)
                dv = dv + nn(p.astype(jnp.bfloat16), g)
                dk = dk + nn(ds, q)
                part = pl.ds(h*depth, depth)
                dq_t_ref[part, rows] = dq_t_ref[part, rows] + nn(k_t[h*depth:(h+1)*depth], ds)
            dk_ref[keys, :] = dk
            dv_ref[keys, :] = dv
            return 0
        lax.fori_loop(j, last_tile(ends, j*tile + tile - 1, tile) + 1, one_query, 0)
        return 0
    lax.fori_loop(0, tiles, one_key, 0)
    def finish(t, _):
        rows = pl.ds(pl.multiple_of(t*tile, tile), tile)
        dq_ref[rows, :] = (jnp.transpose(dq_t_ref[:, rows])*scale).astype(jnp.bfloat16)
        return 0
    lax.fori_loop(0, tiles, finish, 0)
    for slot, dst, src in placed(dqkv_refs, block, table, order_ref, per):
        slot[dst, 0:width] = dq_ref[src, :]
        slot[dst, width:2*width] = dk_ref[src, :].astype(jnp.bfloat16)
        slot[dst, 2*width:3*width] = dv_ref[src, :].astype(jnp.bfloat16)
    shard = part_out_ref.shape[1]
    for k in range(n):
        dqkv_refs[k][0:shard, 3*width:] = part_out_ref[k]
        if shard < dqkv_refs[k].shape[0]:
            dqkv_refs[k][shard:, 3*width:] = jnp.zeros((dqkv_refs[k].shape[0]-shard, width), jnp.bfloat16)

SM=pl.BlockSpec(memory_space=pltpu.SMEM)
VM=pl.BlockSpec(memory_space=pltpu.VMEM)
def attention_forward(table, lengths, order, qkv, n, heads, depth, tile):
    total=sum(x.shape[0] for x in qkv); rows=total//n; width=heads*depth
    block=total//order.shape[1]
    meta=(len(qkv),n,heads,depth,tile,block)
    res=pl.pallas_call(functools.partial(fwd_kernel,meta),
        out_shape=[jax.ShapeDtypeStruct((rows,width),jnp.bfloat16)]*n+[jax.ShapeDtypeStruct((width,total),jnp.float32),jax.ShapeDtypeStruct((heads,total),jnp.float32)],
        in_specs=[SM,SM,SM]+[VM]*len(qkv), out_specs=[VM]*(n+2),
        scratch_shapes=[pltpu.VMEM((heads,total,width),jnp.bfloat16)]+[pltpu.VMEM((total,width),jnp.bfloat16)]*3,
        cost_estimate=cost(17),
        name="attention_forward")(table,lengths,order,*qkv)
    return list(res[:n]),res[n],res[n+1]
def attention_backward(table, lengths, order, qkv, grads, part_out, out_t, lse, heads, depth, tile):
    n=len(grads); rows=grads[0].shape[0]; total=n*rows; width=heads*depth
    block=total//order.shape[1]
    meta=(len(qkv),n,heads,depth,tile,block)
    f32=jnp.float32; b16=jnp.bfloat16
    return list(pl.pallas_call(functools.partial(bwd_kernel,meta),
        out_shape=[jax.ShapeDtypeStruct((rows,4*width),b16)]*n,
        in_specs=[SM,SM,SM]+[VM]*(len(qkv)+n+3), out_specs=[VM]*n,
        scratch_shapes=[pltpu.VMEM((heads,total,width),b16),pltpu.VMEM((total,width),b16),pltpu.VMEM((total,width),b16),pltpu.VMEM((heads,total,width),b16),
          pltpu.VMEM((width,total),b16),pltpu.VMEM((heads,total),f32),pltpu.VMEM((width,total),f32),pltpu.VMEM((total,width),b16),pltpu.VMEM((total,width),f32),pltpu.VMEM((total,width),f32)],
        cost_estimate=cost(18),
        name="attention_backward")(table,lengths,order,*qkv,*grads,part_out,out_t,lse))


def tn(left, right):
    return lax.dot_general(left, right, (((0,), (0,)), ((), ())), preferred_element_type=jnp.float32)


def low(value):
    return value.astype(jnp.bfloat16)


def wide(value):
    return value.astype(jnp.float32)


def at(start, size):
    return pl.ds(pl.multiple_of(start, size), size)


def cost(microseconds):
    return pl.CostEstimate(flops=0, bytes_accessed=int(microseconds * 3.4e6), transcendentals=0)


def call(name, kernel, out, inputs, scratch=(), time=2.0):
    return list(
        pl.pallas_call(
            kernel,
            out_shape=list(out),
            in_specs=[SM] + [VM] * (len(inputs) - 1),
            out_specs=[VM] * len(out),
            scratch_shapes=list(scratch),
            cost_estimate=cost(time),
            name=name,
        )(*inputs)
    )


def shape(dims, dtype=jnp.bfloat16):
    return jax.ShapeDtypeStruct(tuple(dims), dtype)


def slice_kernel(own_width, table, w_ref, one_ref, two_ref, out_ref):
    shard, total = w_ref.shape
    for part in range(3):
        out_ref[0:shard, part * own_width : (part + 1) * own_width] = w_ref[
            :, at(part * (total // 3) + table[0, 0] * own_width, own_width)
        ]
    out_ref[shard : shard + 8, :] = gain_rows(wide(one_ref[...]), wide(two_ref[...]), 3 * own_width)


def gain_rows(one, two, lanes):
    shard = one.shape[1]
    if lanes > shard:
        rest = jnp.zeros((1, lanes - shard), jnp.float32)
        one, two = jnp.concatenate([one, rest], axis=1), jnp.concatenate([two, rest], axis=1)
    number = lax.broadcasted_iota(jnp.int32, (8, lanes), 0)
    return low(jnp.where(number == 0, one, jnp.where(number == 1, two, 0.0)))


def full_gain(table, n, pieces, row, gain_ref):
    shard = gain_ref.shape[1] // len(pieces)
    for slot, piece in enumerate(pieces):
        lines = wide(piece[pl.ds(piece.shape[0] - 8, 8), 0:shard])
        gain_ref[0:1, at(table[0, n + slot] * shard, shard)] = lines[row : row + 1]


def split_kernel(n, table, w_ref, *refs):
    outs, parts_ref = refs[:-1], refs[-1]
    count = len(outs)
    hidden = w_ref.shape[1] // (2 * count)
    for part in range(count):
        parts_ref[part, :, 0:hidden] = w_ref[:, part * hidden : (part + 1) * hidden]
        parts_ref[part, :, hidden:] = w_ref[:, (count + part) * hidden : (count + part + 1) * hidden]
    for slot in range(count):
        outs[slot][...] = parts_ref[table[0, n + slot]]


def project_kernel(n, table, rows_ref, *refs):
    pieces, attn_ref, qkv_ref, gain_ref, weight_ref = refs[:-4], refs[-4], refs[-3], refs[-2], refs[-1]
    shard = rows_ref.shape[1] // len(pieces)
    full_gain(table, n, pieces, 0, gain_ref)
    for slot, piece in enumerate(pieces):
        weight_ref[at(table[0, n + slot] * shard, shard), :] = piece[pl.ds(0, shard), :]
    value = wide(rows_ref[...])
    inverse = lax.rsqrt(jnp.mean(value * value, axis=1, keepdims=True) + EPS)
    attn_in = low(value * inverse * gain_ref[0:1, :])
    attn_ref[...] = attn_in
    qkv_ref[...] = low(nn(attn_in, weight_ref[...]))


def stage_rows(table, n, pieces, weight_ref):
    shard = pieces[0].shape[0]
    for slot, piece in enumerate(pieces):
        weight_ref[at(table[0, n + slot] * shard, shard), :] = piece[...]


def leave_kernel(n, count, table, tokens_ref, *refs):
    parts, outs, slices = refs[:n], refs[n : n + count], refs[n + count : n + 2 * count]
    resid_ref, ffn_ref, gain_ref, weight_ref, sum_ref = refs[n + 2 * count :]
    own_width = parts[0].shape[1]
    full_gain(table, n, slices, 1, gain_ref)
    stage_rows(table, n, outs, weight_ref)
    rows = tokens_ref.shape[0]
    attn = jnp.concatenate([parts[k][...] for k in range(n)], axis=1)
    ordered = jnp.concatenate([weight_ref[at(table[0, k] * own_width, own_width), :] for k in range(n)], axis=0)
    resid = wide(tokens_ref[...]) + nn(attn, ordered)
    resid_ref[...] = resid
    inverse = lax.rsqrt(jnp.mean(resid * resid, axis=1, keepdims=True) + EPS)
    ffn_ref[...] = low(resid * inverse * gain_ref[0:1, :])


def ffn_kernel(n, count, slots, table, *refs):
    ffn, cot = refs[:slots], refs[slots : 2 * slots]
    pieces, down_ref = refs[2 * slots : 2 * slots + count], refs[2 * slots + count]
    rest = refs[2 * slots + count + 1 :]
    terms, outs, hidden_ref, grad_ref = rest[:slots], rest[slots : 2 * slots], rest[2 * slots], rest[2 * slots + 1]
    gate_ref, up_ref = rest[2 * slots + 2 :]
    hidden = down_ref.shape[0]
    shard = pieces[0].shape[0]
    rows = ffn[0].shape[0]
    for slot, piece in enumerate(pieces):
        place = at(table[0, n + slot] * shard, shard)
        gate_ref[place, :] = piece[:, 0:hidden]
        up_ref[place, :] = piece[:, hidden:]
    for slot in range(slots):
        value = ffn[slot][...]
        gate = nn(value, gate_ref[...])
        upward = nn(value, up_ref[...])
        grad_hidden = nt(cot[slot][...], down_ref[...])
        sigma = jax.nn.sigmoid(gate)
        active = gate * sigma
        hidden_low = low(active * upward)
        grad_gate = low(grad_hidden * upward * (sigma + active * (1.0 - sigma)))
        grad_up = low(grad_hidden * active)
        terms[slot][...] = low(nt(grad_gate, gate_ref[...]) + nt(grad_up, up_ref[...]))
        outs[slot][...] = low(nn(hidden_low, down_ref[...]))
        place = pl.ds(slot * rows, rows)
        hidden_ref[place, :] = hidden_low
        grad_ref[place, 0:hidden] = grad_gate
        grad_ref[place, hidden:] = grad_up


def ffn_weight_kernel(n, count, table, *refs):
    ffn, cot, rest = refs[:count], refs[count : 2 * count], refs[2 * count :]
    hiddens, grads, rest = rest[: count // 2], rest[count // 2 : count], rest[count:]
    outs, (value_ref, turned_ref) = rest[:-2], rest[-2:]
    hidden = hiddens[0].shape[1]
    half = n // 2
    shard = ffn[0].shape[1] // count
    sub = shard // n
    lines = count * sub
    cut = outs[half].shape[0]
    hidden_all = jnp.concatenate([r[...] for r in hiddens], axis=0)
    grad_all = jnp.concatenate([r[...] for r in grads], axis=0)

    def store(slot, row, lanes, value):
        if slot != half:
            outs[slot if slot < half else slot + 1][row : row + sub, lanes] = value
        elif row < cut:
            outs[half][row : row + sub, lanes] = value
        else:
            outs[half + 1][row - cut : row - cut + sub, lanes] = value

    for f in range(count):
        lanes = slice(f * shard, (f + 1) * shard)
        ffn_all = jnp.concatenate([r[:, lanes] for r in ffn], axis=0)
        value_ref[...] = low(tn(ffn_all, grad_all))
        cot_all = jnp.concatenate([r[:, lanes] for r in cot], axis=0)
        turned_ref[...] = low(tn(cot_all, hidden_all))
        side, line = f // (count // 2), lines + (f % (count // 2)) * sub
        for slot in range(n):
            mine = at(table[0, slot] * sub, sub)
            store(slot, f * sub, slice(0, 2 * hidden), value_ref[mine, :])
            store(slot, line, slice(side * hidden, (side + 1) * hidden), turned_ref[mine, :])


def branch_kernel(n, count, got, table, resid_ref, cot_ref, *refs):
    terms, outs, slices = refs[:got], refs[got : got + count], refs[got + count : got + 2 * count]
    rest = refs[got + 2 * count :]
    grad_ref, branch_ref, parts = rest[0], rest[1], rest[2 : 2 + n]
    gain_ref, weight_ref, scratch_ref = rest[2 + n :]
    own_width = parts[0].shape[1]
    full_gain(table, n, slices, 1, gain_ref)
    stage_rows(table, n, outs, weight_ref)
    resid = resid_ref[...]
    inverse = lax.rsqrt(jnp.mean(resid * resid, axis=1, keepdims=True) + EPS)
    normed = resid * inverse
    grad = wide(terms[0][...])
    for term in terms[1:]:
        grad = grad + wide(term[...])
    scaled = grad * gain_ref[0:1, :]
    inner = jnp.mean(scaled * normed, axis=1, keepdims=True)
    grad_resid = wide(cot_ref[...]) + inverse * (scaled - normed * inner)
    grad_ref[...] = grad_resid
    branch = low(grad_resid)
    branch_ref[...] = branch
    for k in range(n):
        parts[k][...] = low(nt(branch, weight_ref[at(table[0, k] * own_width, own_width), :]))


def out_weight_kernel(n, count, table, branch_ref, *refs):
    parts, outs, whole_ref = refs[:n], refs[n : n + count], refs[-1]
    own_width = parts[0].shape[1]
    shard = outs[0].shape[1]
    branch = branch_ref[...]
    for k in range(n):
        whole_ref[at(table[0, k] * own_width, own_width), :] = low(tn(parts[k][...], branch))
    for slot in range(count):
        lines = at(table[0, n + slot] * shard, shard)
        for k in range(n):
            if own_width % 128 == 0:
                outs[slot][k] = whole_ref[lines, at(table[0, k] * own_width, own_width)]
            else:
                outs[slot][k] = whole_ref[lines, k * own_width : (k + 1) * own_width]


def qkv_weight_kernel(given, n, count, table, *refs):
    attn, grads, outs = refs[:given], refs[given : given + n], refs[given + n :]
    shard = outs[0].shape[0]
    grad_all = jnp.concatenate([r[:, 0 : outs[0].shape[1]] for r in grads], axis=0)
    for slot in range(count):
        lanes = at(table[0, n + slot] * shard, shard)
        attn_all = jnp.concatenate([r[:, lanes] for r in attn], axis=0)
        outs[slot][...] = low(tn(attn_all, grad_all))


def tail_kernel(n, count, aligned, table, tokens_ref, grad_ref, *refs):
    parts, weights, slices = refs[:n], refs[n : -4 - count], refs[-4 - count : -4]
    out_ref, gain_ref, sum_ref, grads_ref = refs[-4:]
    pieces = len(weights) // count
    own_width = parts[0].shape[1] // 4
    width = tokens_ref.shape[1]
    shard = width // count
    full_gain(table, n, slices, 0, gain_ref)
    for k in range(n):
        for part in range(3):
            value = parts[k][:, part * own_width : (part + 1) * own_width]
            if aligned:
                grads_ref[:, at(part * width + table[0, k] * own_width, own_width)] = value
            else:
                start = (k * 3 + part) * own_width
                grads_ref[:, start : start + own_width] = value
    for slot in range(count):
        for piece in range(pieces):
            size = shard // pieces
            place = at(table[0, n + slot] * shard + piece * size, size)
            sum_ref[:, place] = nt(grads_ref[...], weights[slot * pieces + piece][...])
    value = wide(tokens_ref[...])
    inverse = lax.rsqrt(jnp.mean(value * value, axis=1, keepdims=True) + EPS)
    normed = value * inverse
    scaled = sum_ref[...] * gain_ref[0:1, :]
    inner = jnp.mean(scaled * normed, axis=1, keepdims=True)
    out_ref[...] = low(grad_ref[...] + inverse * (scaled - normed * inner))


def row_sums(product):
    rows, lanes = product.shape
    total = product[:, 0:128]
    for i in range(1, lanes // 128):
        total = total + product[:, i * 128 : (i + 1) * 128]
    return jnp.sum(jnp.transpose(total), axis=0, keepdims=True)


def ffn_final_kernel(n, count, factor, table, w_ref, gain_ref, *refs):
    pieces = refs[: n + 1]
    gu_ref, down_ref, gain_out_ref, turned_ref = refs[n + 1 :]
    hidden = down_ref.shape[0]
    sub = gu_ref.shape[0] // n
    half = n // 2
    for k in range(n):
        if k == half:
            piece = jnp.concatenate([wide(pieces[half][...]), wide(pieces[half + 1][...])], axis=0)
        else:
            piece = wide(pieces[k if k < half else k + 1][...])
        piece = piece * factor
        start = table[0, k] * sub
        for part in range(count):
            lines = piece[part * sub : (part + 1) * sub]
            gu_ref[at(start, sub), part * hidden : (part + 1) * hidden] = lines[:, 0:hidden]
            gu_ref[at(start, sub), (count + part) * hidden : (count + part + 1) * hidden] = lines[:, hidden:]
            side, line = part // (count // 2), (count + part % (count // 2)) * sub
            turned_ref[at(part * (n * sub) + start, sub), :] = piece[line : line + sub, side * hidden : (side + 1) * hidden]
    width = turned_ref.shape[0]
    for i in range(width // 128):
        down_ref[:, i * 128 : (i + 1) * 128] = jnp.transpose(turned_ref[i * 128 : (i + 1) * 128, :])
    gain_out_ref[...] = row_sums(wide(w_ref[...]) * gu_ref[...]) / wide(gain_ref[...])


def attn_final_kernel(n, factor, aligned, table, w_ref, gain_ref, *refs):
    pieces = refs[: n + 1]
    qkv_ref, out_ref, gain_out_ref = refs[n + 1 :]
    own_width = pieces[0].shape[1] // 4
    width = out_ref.shape[1]
    half = n // 2
    for k in range(n):
        if k == half:
            piece = jnp.concatenate([wide(pieces[half][...]), wide(pieces[half + 1][...])], axis=0)
        else:
            piece = wide(pieces[k if k < half else k + 1][...])
        piece = piece * factor
        for part in range(4):
            value = piece[:, part * own_width : (part + 1) * own_width]
            target = out_ref if part == 3 else qkv_ref
            base = 0 if part == 3 else part * width
            if aligned:
                target[:, at(base + table[0, k] * own_width, own_width)] = value
            else:
                target[:, base + k * own_width : base + (k + 1) * own_width] = value
    gain_out_ref[...] = row_sums(wide(w_ref[...]) * qkv_ref[...]) / wide(gain_ref[...])


def cut_kernel(n, table, own_ref, up_ref, down_ref, *refs):
    outs, rest_ref, sum_ref = refs[:-2], refs[-2], refs[-1]
    sum_ref[...] = low(wide(own_ref[...]) + wide(up_ref[...]) + wide(down_ref[...]))
    sub = outs[0].shape[0]
    for slot, out in enumerate(outs):
        out[...] = sum_ref[at(table[0, n + slot] * sub, sub), :]
    rest_ref[...] = sum_ref[len(outs) * sub :, :]


def pack_kernel(n, table, rest_ref, *refs):
    pieces, out_ref = refs[:-1], refs[-1]
    sub = pieces[0].shape[0]
    for slot, piece in enumerate(pieces):
        out_ref[at(table[0, n + slot] * sub, sub), :] = piece[...]
    out_ref[len(pieces) * sub :, :] = rest_ref[...]


def join_kernel(terms, table, *refs):
    qkv, back, out_ref = refs[:terms], refs[terms:-1], refs[-1]
    total = wide(qkv[0][...])
    for term in qkv[1:]:
        total = total + wide(term[...])
    start = total.shape[1]
    out_ref[:, 0:start] = low(total)
    shard = out_ref.shape[0]
    other = wide(back[0][0:shard, start:])
    for term in back[1:]:
        other = other + wide(term[0:shard, start:])
    out_ref[:, start:] = low(other)


def ring_of(count):
    if count % 4 or count < 8:
        return list(range(count))
    across = count // 4
    order = []
    for along in range(4):
        columns = range(1, across) if along % 2 == 0 else range(across - 1, 0, -1)
        order += [along * across + column for column in columns]
    return order + [along * across for along in reversed(range(4))]


def ring_shift(value, ring, step):
    count = len(ring)
    return lax.ppermute(
        value, "ctx", [(ring[i], ring[(i + step) % count]) for i in range(count)]
    )


def tie(*values):
    return lax.optimization_barrier(values)


class Gather:
    def __init__(self, value, ring):
        self.ring, self.half, self.step = ring, len(ring) // 2, 1
        self.first, self.ahead, self.behind, self.far = value, [], [], None
        self.up, self.down = tie(ring_shift(value, ring, 1), ring_shift(value, ring, -1))

    def advance(self, *others):
        self.ahead.append(self.down)
        self.behind.append(self.up)
        self.up, self.down, *others = tie(self.up, self.down, *others)
        self.step += 1
        up, down = self.up, self.down
        if self.step == self.half:
            cut = up.shape[0] // 2
            up, down = up[:cut], down[cut:]
        self.up, self.down = tie(ring_shift(up, self.ring, 1), ring_shift(down, self.ring, -1))
        return others

    def slots(self):
        while self.step < self.half:
            self.advance()
        return [self.first] + self.ahead + [self.up, self.down] + self.behind[::-1]


class Scatter:
    def __init__(self, terms, ring):
        self.ring, self.half, self.terms = ring, len(ring) // 2, terms
        self.up, self.down = terms[self.half : self.half + 2]
        self.step = self.half
        self.send()

    def send(self):
        self.up, self.down = tie(ring_shift(self.up, self.ring, 1), ring_shift(self.down, self.ring, -1))

    def advance(self, *others):
        self.up, self.down, *others = tie(self.up, self.down, *others)
        up, down, cut = self.terms[self.step - 1], self.terms[len(self.ring) + 2 - self.step], self.up.shape[0]
        if self.step == self.half:
            rows = up.shape[0]
            self.up = low(wide(up) + jnp.pad(wide(self.up), ((0, rows - cut), (0, 0))))
            self.down = low(wide(down) + jnp.pad(wide(self.down), ((rows - cut, 0), (0, 0))))
        else:
            self.up, self.down = add_low(up, self.up), add_low(down, self.down)
        self.step -= 1
        self.send()
        return others

    def sums(self):
        while self.step > 1:
            self.advance()
        return [self.terms[0], self.up, self.down]


def ring_exchange(slots, ring):
    count = len(ring)
    result = [slots[0]] + [None] * (count - 1)
    for k in range(1, count):
        result[count - k] = ring_shift(slots[k], ring, k)
    return result


def partner(value, count):
    return lax.ppermute(value, "fsdp", [(i, i ^ 1) for i in range(count)])


def chip_shift(value, count, step):
    return lax.ppermute(value, "fsdp", [(i, (i + 2 * step) % count) for i in range(count)])


def far_gather(value, count):
    return [value] + [chip_shift(value, count, -step) for step in range(1, count // 2)]


def near_gather(nears, count):
    slots = []
    for near in nears:
        slots += [near, partner(near, count)]
    return slots


def near_scatter(terms, count):
    return [add_low(terms[i], partner(terms[i + 1], count)) for i in range(0, count, 2)]


def far_scatter(nears, count):
    return [nears[0]] + [chip_shift(nears[step], count, step) for step in range(1, count // 2)]


def side_exchange(pieces, count):
    chips = count // 2
    received = [None] * count
    for step in range(chips):
        for flip in (0, 1):
            piece = pieces[2 * step + flip]
            if step or flip:
                pairs = [(i, ((i + 2 * step) % count) ^ flip) for i in range(count)]
                piece = lax.ppermute(piece, "fsdp", pairs)
            received[2 * ((chips - step) % chips) + flip] = piece
    return received


def add_low(left, right):
    return low(wide(left) + wide(right))


def total_of(terms):
    total = wide(terms[0])
    for term in terms[1:]:
        total = total + wide(term)
    return total


def body(
    tokens, cotangent, gain_attn, w_qkv, w_out, gain_ffn, w_gate_up, w_down, lengths, block_order
):
    rows, width = tokens.shape
    heads = HEADS
    depth = width // heads
    ctx = lax.axis_size("ctx")
    fsdp = lax.axis_size("fsdp")
    factor = 1.0 / math.sqrt(rows * ctx * fsdp)
    shard = width // fsdp
    hidden = w_down.shape[0]
    own_heads = heads // ctx
    own_width = own_heads * depth
    aligned = own_width % 128 == 0
    half = ctx // 2
    sub = shard // ctx
    lines = fsdp * sub
    ring = ring_of(ctx)
    chips = fsdp // 2
    entries = []
    for c in range(ctx):
        me = ring.index(c)
        for f in range(fsdp):
            owners = [ring[(me + k) % ctx] for k in range(ctx)]
            sides = [((f // 2 + s) % chips) * 2 + ((f % 2) ^ k) for s in range(chips) for k in (0, 1)]
            entries.append(owners + sides)
    device = lax.axis_index("ctx") * fsdp + lax.axis_index("fsdp")
    table = lax.dynamic_slice_in_dim(jnp.asarray(entries, jnp.int32), device, 1, 0)
    gain_one, gain_two = gain_attn.reshape(1, shard), gain_ffn.reshape(1, shard)
    f32 = jnp.float32
    gain_scratch = pltpu.VMEM((8, width), f32)
    square_scratch = pltpu.VMEM((width, width), jnp.bfloat16)

    going = Gather(tokens, ring)
    if aligned:
        (piece,) = call(
            "slice", functools.partial(slice_kernel, own_width),
            [shape((shard + 8, 3 * own_width))], [table, w_qkv, gain_one, gain_two],
            time=2.2,
        )
    else:
        mine = [
            lax.dynamic_slice(w_qkv, (0, part * width + table[0, 0] * own_width), (shard, own_width))
            for part in range(3)
        ]
        piece = jnp.concatenate(
            [jnp.concatenate(mine, axis=1), gain_rows(wide(gain_one), wide(gain_two), 3 * own_width)], axis=0
        )
    slices = far_gather(piece, fsdp)
    gate_pieces = call(
        "split", functools.partial(split_kernel, ctx),
        [shape((shard, 2 * hidden))] * fsdp, [table, w_gate_up],
        scratch=[pltpu.VMEM((fsdp, shard, 2 * hidden), jnp.bfloat16)],
        time=4,
    )
    slices, gate_pieces = going.advance(slices, gate_pieces)
    slices = near_gather(slices, fsdp)
    gate_pieces = side_exchange(gate_pieces, fsdp)

    def project(slot):
        return call(
            "project", functools.partial(project_kernel, ctx),
            [shape(slot.shape), shape((slot.shape[0], 3 * own_width))], [table, slot] + slices,
            scratch=[gain_scratch, pltpu.VMEM((width, 3 * own_width), jnp.bfloat16)],
            time=2.6,
        )

    first = project(tokens)
    ahead, behind = [project(going.ahead[0])], [project(going.behind[0])]
    first, ahead[0], behind[0], gate_pieces[1:3] = going.advance(first, ahead[0], behind[0], gate_pieces[1:3])
    for step in range(1, half - 1):
        ahead.append(project(going.ahead[step]))
        behind.append(project(going.behind[step]))
        if going.step < half:
            ahead[step], behind[step], gate_pieces[3:] = going.advance(ahead[step], behind[step], gate_pieces[3:])
    later_out, later_cot, later_qkv, unused = tie(w_out, cotangent, w_qkv, gate_pieces[-1])
    outs = far_gather(later_out, fsdp)
    *far, ahead, behind = tie(going.up, going.down, ahead, behind)
    pairs = [first] + ahead + [project(far[0]), project(far[1])] + behind[::-1]
    attn_slots, qkv = [pair[0] for pair in pairs], [pair[1] for pair in pairs]

    out_slots, out_t, log_total = attention_forward(
        table, lengths, block_order, qkv, ctx, own_heads, depth, TILE
    )
    qkv_halves = [later_qkv[: shard // 2], later_qkv[shard // 2 :]] if aligned else [relative(later_qkv, table, ctx)]
    qkv_nears = [far_gather(qkv_halves[0], fsdp)]
    out_slots, qkv_nears[0], outs = tie(out_slots, qkv_nears[0], outs)
    attn_parts = ring_exchange(out_slots, ring)
    later_cot, unused = tie(later_cot, out_slots[0])
    outs, cots = near_gather(outs, fsdp), near_gather(far_gather(later_cot, fsdp), fsdp)
    attn_parts, outs, cots[2::2] = tie(attn_parts, outs, cots[2::2])
    resid, ffn_in = call(
        "leave", functools.partial(leave_kernel, ctx, fsdp),
        [shape((rows, width), f32), shape((rows, width))],
        [table, tokens] + attn_parts + outs + slices,
        scratch=[gain_scratch, square_scratch, pltpu.VMEM((8, 128), f32)],
        time=4.1,
    )

    nears = far_gather(ffn_in, fsdp)
    ffns, grad_terms, out_terms, hiddens, grads = [], [], [], [], []
    for chip in range(chips):
        ffn_pair = [nears[chip], partner(nears[chip], fsdp)]
        result = call(
            "feed_forward", functools.partial(ffn_kernel, ctx, fsdp, 2),
            [shape((rows, width))] * 4 + [shape((2 * rows, hidden)), shape((2 * rows, 2 * hidden))],
            [table] + ffn_pair + cots[2 * chip : 2 * chip + 2] + gate_pieces + [w_down],
            scratch=[pltpu.VMEM((width, hidden), jnp.bfloat16)] * 2,
            time=9.5,
        )
        if chip == 0:
            result, nears[1:] = tie(result, nears[1:])
        ffns += ffn_pair
        grad_terms += result[0:2]
        out_terms += result[2:4]
        hiddens.append(result[4])
        grads.append(result[5])
    grad_nears = near_scatter(grad_terms, fsdp)
    hiddens, grad_nears = tie(hiddens, grad_nears)
    grad_parts = far_scatter(grad_nears, fsdp)
    terms_ffn = call(
        "feed_forward_weights", functools.partial(ffn_weight_kernel, ctx, fsdp),
        [shape((lines + lines // 2, 2 * hidden))] * half
        + [shape(((lines + lines // 2) // 2, 2 * hidden))] * 2
        + [shape((lines + lines // 2, 2 * hidden))] * (half - 1),
        [table] + ffns + cots + hiddens + grads,
        scratch=[pltpu.VMEM((shard, 2 * hidden), jnp.bfloat16), pltpu.VMEM((shard, hidden), jnp.bfloat16)],
        time=12,
    )
    terms_ffn, grad_parts = tie(terms_ffn, grad_parts)
    ffn_sums = Scatter(terms_ffn, ring)
    grad_resid, branch, *grad_attn = call(
        "branch", functools.partial(branch_kernel, ctx, fsdp, len(grad_parts)),
        [shape((rows, width), f32), shape((rows, width))] + [shape((rows, own_width))] * ctx,
        [table, resid, cotangent] + grad_parts + outs + slices,
        scratch=[gain_scratch, square_scratch, pltpu.VMEM((8, 128), f32)],
        time=5,
    )
    grad_slots = ring_exchange(grad_attn, ring)
    out_sides = call(
        "out_weights", functools.partial(out_weight_kernel, ctx, fsdp),
        [shape((ctx, shard, own_width))] * fsdp, [table, branch] + attn_parts,
        scratch=[square_scratch],
        time=3.3,
    )
    if not aligned:
        out_sides = [by_slot(array, table, ctx) for array in out_sides]
    out_nears = near_scatter(out_sides, fsdp)

    out_parts = far_scatter(out_nears, fsdp)
    part_out = low(total_of(out_parts))
    grad_slots, part_out = ffn_sums.advance(grad_slots, part_out)
    grad_qkv = attention_backward(
        table, lengths, block_order, qkv, grad_slots, part_out, out_t, log_total, own_heads, depth, TILE
    )
    (grad_qkv,) = ffn_sums.advance(grad_qkv)
    qkv_halves, unused = tie(qkv_halves, grad_qkv[0])
    qkv_nears += [far_gather(piece, fsdp) for piece in qkv_halves[1:]]
    grad_back = ring_exchange(grad_qkv, ring)
    qkv_sides = call(
        "qkv_weights", functools.partial(qkv_weight_kernel, len(attn_slots), ctx, fsdp),
        [shape((shard, 3 * own_width))] * fsdp, [table] + attn_slots + grad_qkv,
        time=6,
    )
    qkv_sum_nears = near_scatter(qkv_sides, fsdp)
    third = max(1, (ctx - 1) * 3 // 7)
    grad_back[-third:], qkv_sum_nears = ffn_sums.advance(grad_back[-third:], qkv_sum_nears)
    qkv_sum = far_scatter(qkv_sum_nears, fsdp)
    weights = [near_gather(nears, fsdp) for nears in qkv_nears]
    weights = [pieces[slot] for slot in range(fsdp) for pieces in weights]

    own_sum, ffn_up, ffn_down = ffn_sums.sums()
    second = third + max(1, (ctx - 1) * 2 // 7)
    ffn_up, ffn_down, qkv_sum, grad_back[-second:-third] = tie(ffn_up, ffn_down, qkv_sum, grad_back[-second:-third])
    *gate_sides, rest = call(
        "cut", functools.partial(cut_kernel, ctx),
        [shape((sub, 2 * hidden))] * fsdp + [shape((lines // 2, 2 * hidden))],
        [table, own_sum, ffn_up, ffn_down],
        scratch=[pltpu.VMEM((lines + lines // 2, 2 * hidden), jnp.bfloat16)],
        time=3,
    )
    gate_sides = side_exchange(gate_sides, fsdp)
    gate_sides, grad_back[1:-second], weights = tie(gate_sides, grad_back[1:-second], weights)
    (packed,) = call(
        "pack", functools.partial(pack_kernel, ctx),
        [shape((lines + lines // 2, 2 * hidden))], [table, rest] + gate_sides,
        time=2,
    )
    ffn_going = Gather(packed, ring)
    (grad_tokens,) = call(
        "tail", functools.partial(tail_kernel, ctx, fsdp, aligned),
        [shape((rows, width))], [table, tokens, grad_resid] + grad_back + weights + slices,
        scratch=[gain_scratch, pltpu.VMEM((rows, width), f32), pltpu.VMEM((rows, 3 * width), jnp.bfloat16)],
        time=8,
    )
    (joined,) = call(
        "join", functools.partial(join_kernel, len(qkv_sum)),
        [shape((shard, 4 * own_width))], [table] + qkv_sum + grad_back,
        time=2.5,
    )
    joined, grad_tokens = ffn_going.advance(joined, grad_tokens)
    ffn_going.advance()
    joined, unused = tie(joined, ffn_going.behind[-1])
    attn_going = Gather(joined, ring)
    grad_w_gate_up, grad_w_down, grad_gain_ffn = call(
        "feed_forward_final", functools.partial(ffn_final_kernel, ctx, fsdp, factor),
        [shape((shard, 2 * hidden * fsdp), f32), shape((hidden, width), f32), shape((1, shard), f32)],
        [table, w_gate_up, gain_two] + ffn_going.slots(),
        scratch=[pltpu.VMEM((width, hidden), f32)],
        time=8,
    )
    grad_w_qkv, grad_w_out, grad_gain_attn = call(
        "attention_final", functools.partial(attn_final_kernel, ctx, factor, aligned),
        [shape((shard, 3 * width), f32), shape((shard, width), f32), shape((1, shard), f32)],
        [table, w_qkv if aligned else unmixed(relative(w_qkv, table, ctx), ctx, own_width), gain_one] + attn_going.slots(),
        time=4.6,
    )
    if not aligned:
        grad_w_qkv, grad_w_out = ordered(grad_w_qkv, table, 3, ctx), ordered(grad_w_out, table, 1, ctx)
    output = low(resid + total_of(far_scatter(near_scatter(out_terms, fsdp), fsdp)))
    return (
        output,
        grad_tokens,
        grad_gain_attn.reshape(shard),
        grad_w_qkv,
        grad_w_out,
        grad_gain_ffn.reshape(shard),
        grad_w_gate_up,
        grad_w_down,
    )


def relative(weight, table, ctx):
    rows = weight.shape[0]
    parts = weight.reshape(rows, 3, ctx, -1)
    slots = [lax.dynamic_index_in_dim(parts, table[0, k], 2, keepdims=False) for k in range(ctx)]
    return jnp.concatenate([slot.reshape(rows, -1) for slot in slots], axis=1)


def by_slot(array, table, ctx):
    return jnp.stack([lax.dynamic_index_in_dim(array, table[0, k], 0, keepdims=False) for k in range(ctx)])


def unmixed(weight, ctx, own_width):
    rows = weight.shape[0]
    return weight.reshape(rows, ctx, 3, own_width).transpose(0, 2, 1, 3).reshape(rows, -1)


def ordered(array, table, parts, ctx):
    rows = array.shape[0]
    split = array.reshape(rows, parts, ctx, -1)
    result = jnp.zeros_like(split)
    for k in range(ctx):
        result = lax.dynamic_update_slice(result, split[:, :, k : k + 1], (0, 0, table[0, k], 0))
    return result.reshape(rows, -1)


def solution(mesh):
    in_specs = (
        P(("fsdp", "ctx"), None),
        P(("fsdp", "ctx"), None),
        P("fsdp"),
        P("fsdp", None),
        P("fsdp", None),
        P("fsdp"),
        P("fsdp", None),
        P("fsdp", None),
        P("fsdp", None),
        P("fsdp", None),
    )
    out_specs = (
        P(("fsdp", "ctx"), None),
        P(("fsdp", "ctx"), None),
        P("fsdp"),
        P("fsdp", None),
        P("fsdp", None),
        P("fsdp"),
        P("fsdp", None),
        P("fsdp", None),
    )
    return jax.shard_map(body, mesh=mesh, in_specs=in_specs, out_specs=out_specs, check_vma=False)
```

```python
import functools
import math

import jax
import jax.numpy as jnp
from jax import lax
from jax.experimental import pallas as pl
from jax.experimental.pallas import tpu as pltpu
from jax.sharding import PartitionSpec as P

HEADS = 16
TILE = 256
VMEM_FWD = 24 << 20
VMEM_BWD = 32 << 20


EPS = 1e-05
MASKED=-1e30
def nt(a,b): return lax.dot_general(a,b,(((1,),(1,)),((),())),preferred_element_type=jnp.float32)
def nn(a,b): return lax.dot_general(a,b,(((1,),(0,)),((),())),preferred_element_type=jnp.float32)

def ends_of(lengths_ref):
    ends = [lengths_ref[0, 0]]
    for i in range(1, lengths_ref.shape[1]):
        ends.append(ends[-1] + lengths_ref[0, i])
    return ends

def first_tile(ends, position, tile):
    start = jnp.int32(0)
    for end in ends[:-1]:
        start = jnp.where(end <= position, end, start)
    return start // tile

def last_tile(ends, position, tile):
    last = ends[-1]
    for end in reversed(ends[:-1]):
        last = jnp.where(end > position, end, last)
    return (last - 1) // tile

def seen(ends, query_start, key_start, tile):
    pos_query = query_start + lax.broadcasted_iota(jnp.int32, (1, tile), 1)
    start = jnp.zeros((1, tile), jnp.int32)
    for end in ends[:-1]:
        start = jnp.where(pos_query >= end, end, start)
    pos_key = key_start + lax.broadcasted_iota(jnp.int32, (tile, tile), 0)
    return (pos_key <= pos_query) & (pos_key >= start)

def head_lanes(x, head, heads, depth):
    if heads == 1:
        return x
    lane = lax.broadcasted_iota(jnp.int32, x.shape, 1)
    return jnp.where((lane >= head * depth) & (lane < (head + 1) * depth), x, jnp.zeros_like(x))

def placed(slots, block, table, order_ref, per):
    number = 0
    for slot in slots:
        for row in range(0, slot.shape[0], block):
            position = order_ref[0, table[0, number // per] * per + number % per] * block
            yield slot, pl.ds(row, block), pl.ds(pl.multiple_of(position, block), block)
            number += 1

def stored(owners, block, order_ref, per):
    for owner in range(owners):
        for b in range(per):
            position = order_ref[0, owner * per + b] * block
            yield owner, pl.ds(b * block, block), pl.ds(pl.multiple_of(position, block), block)

def fwd_kernel(meta, table, lengths_ref, order_ref, *refs):
    given, n, heads, depth, tile, block = meta
    qkv_refs, out_refs = refs[:given], refs[given:given+n]
    out_t_ref, lse_ref = refs[given+n], refs[given+n+1]
    q_ref, k_ref, v_ref, o_ref = refs[given+n+2:]
    ends = ends_of(lengths_ref)
    width = heads*depth
    scale = depth ** (-0.5)
    per = out_refs[0].shape[0] // block
    for slot, src, dst in placed(qkv_refs, block, table, order_ref, per):
        q = slot[src, 0:width].astype(jnp.float32)*scale
        for h in range(heads):
            q_ref[h, dst, :] = head_lanes(q, h, heads, depth).astype(jnp.bfloat16)
        k_ref[dst, :] = slot[src, width:2*width]
        v_ref[dst, :] = slot[src, 2*width:]
    tiles = q_ref.shape[1] // tile
    def one_query(t, _):
        rows = pl.ds(pl.multiple_of(t*tile, tile), tile)
        qs = [q_ref[h, rows, :] for h in range(heads)]
        def one_key(j, carry):
            keys = pl.ds(pl.multiple_of(j*tile, tile), tile)
            k = k_ref[keys, :]
            v_t = jnp.transpose(v_ref[keys, :].astype(jnp.float32)).astype(jnp.bfloat16)
            mask = seen(ends, t*tile, j*tile, tile)
            new = []
            for h in range(heads):
                m, l, acc = carry[h]
                s = jnp.where(mask, nt(k, qs[h]), MASKED)
                m_new = jnp.maximum(m, jnp.max(s, axis=0, keepdims=True))
                e = jnp.exp(s - m_new)
                alpha = jnp.exp(m - m_new)
                l = l*alpha + jnp.sum(e, axis=0, keepdims=True)
                acc = acc*alpha + nn(v_t[h*depth:(h+1)*depth], e.astype(jnp.bfloat16))
                new.append((m_new, l, acc))
            return tuple(new)
        init = tuple((jnp.full((1,tile),MASKED,jnp.float32), jnp.zeros((1,tile),jnp.float32), jnp.zeros((depth,tile),jnp.float32)) for _ in range(heads))
        final = lax.fori_loop(first_tile(ends, t*tile, tile), t+1, one_key, init)
        outs = []
        for h in range(heads):
            m, l, acc = final[h]
            outs.append(acc / l)
            lse_ref[h:h+1, rows] = m + jnp.log(l)
        out_t = jnp.concatenate(outs, axis=0) if heads > 1 else outs[0]
        out_t_ref[:, rows] = out_t
        o_ref[rows, :] = jnp.transpose(out_t).astype(jnp.bfloat16)
        return 0
    lax.fori_loop(0, tiles, one_query, 0)
    for slot, dst, src in placed(out_refs, block, table, order_ref, per):
        slot[dst, :] = o_ref[src, :]

def bwd_kernel(meta, table, lengths_ref, order_ref, *refs):
    given, n, heads, depth, tile, block = meta
    qkv_refs, grad_refs = refs[:given], refs[given:given+n]
    refs = refs[n:]
    part_out_ref, out_t_ref, lse_ref, dqkv_ref = refs[given:given+4]
    ends = ends_of(lengths_ref)
    q_ref, k_ref, v_ref, g_ref, k_t_ref, delta_ref, dq_t_ref, dq_ref, dk_ref, dv_ref = refs[given+4:]
    width = heads*depth
    scale = depth ** (-0.5)
    per = dqkv_ref.shape[1] // block
    total = k_ref.shape[0]
    for slot, src, dst in placed(qkv_refs, block, table, order_ref, per):
        q = slot[src, 0:width].astype(jnp.float32)*scale
        for h in range(heads):
            q_ref[h, dst, :] = head_lanes(q, h, heads, depth).astype(jnp.bfloat16)
        k_ref[dst, :] = slot[src, width:2*width]
        v_ref[dst, :] = slot[src, 2*width:]
    for slot, src, dst in placed(grad_refs, block, table, order_ref, per):
        g = slot[src, :].astype(jnp.float32)
        for h in range(heads):
            g_ref[h, dst, :] = head_lanes(g, h, heads, depth).astype(jnp.bfloat16)
    tiles = total // tile
    def prepare(t, _):
        rows = pl.ds(pl.multiple_of(t*tile, tile), tile)
        k_t_ref[:, rows] = jnp.transpose(k_ref[rows, :].astype(jnp.float32)).astype(jnp.bfloat16)
        g = g_ref[0, rows, :].astype(jnp.float32)
        for h in range(1, heads):
            g = g + g_ref[h, rows, :].astype(jnp.float32)
        prod = jnp.transpose(g) * out_t_ref[:, rows]
        for h in range(heads):
            delta_ref[h:h+1, rows] = jnp.sum(prod[h*depth:(h+1)*depth], axis=0, keepdims=True)
        dq_t_ref[:, rows] = jnp.zeros((width, tile), jnp.float32)
        return 0
    lax.fori_loop(0, tiles, prepare, 0)
    def one_key(j, _):
        keys = pl.ds(pl.multiple_of(j*tile, tile), tile)
        k = k_ref[keys, :]
        v = v_ref[keys, :]
        k_t = k_t_ref[:, keys]
        dk_ref[keys, :] = jnp.zeros((tile, width), jnp.float32)
        dv_ref[keys, :] = jnp.zeros((tile, width), jnp.float32)
        def one_query(t, _):
            rows = pl.ds(pl.multiple_of(t*tile, tile), tile)
            mask = seen(ends, t*tile, j*tile, tile)
            dk = dk_ref[keys, :]
            dv = dv_ref[keys, :]
            for h in range(heads):
                q = q_ref[h, rows, :]
                g = g_ref[h, rows, :]
                s = nt(k, q)
                p = jnp.where(mask, jnp.exp(s - lse_ref[h:h+1, rows]), 0.0)
                dp = nt(v, g)
                ds = (p*(dp - delta_ref[h:h+1, rows])).astype(jnp.bfloat16)
                dv = dv + nn(p.astype(jnp.bfloat16), g)
                dk = dk + nn(ds, q)
                part = pl.ds(h*depth, depth)
                dq_t_ref[part, rows] = dq_t_ref[part, rows] + nn(k_t[h*depth:(h+1)*depth], ds)
            dk_ref[keys, :] = dk
            dv_ref[keys, :] = dv
            return 0
        lax.fori_loop(j, last_tile(ends, j*tile + tile - 1, tile) + 1, one_query, 0)
        return 0
    lax.fori_loop(0, tiles, one_key, 0)
    def finish(t, _):
        rows = pl.ds(pl.multiple_of(t*tile, tile), tile)
        dq_ref[rows, :] = (jnp.transpose(dq_t_ref[:, rows])*scale).astype(jnp.bfloat16)
        return 0
    lax.fori_loop(0, tiles, finish, 0)
    for owner, dst, src in stored(n, block, order_ref, per):
        dqkv_ref[owner, dst, 0:width] = dq_ref[src, :]
        dqkv_ref[owner, dst, width:2*width] = dk_ref[src, :].astype(jnp.bfloat16)
        dqkv_ref[owner, dst, 2*width:3*width] = dv_ref[src, :].astype(jnp.bfloat16)
    shard = part_out_ref.shape[1]
    rows = dqkv_ref.shape[1]
    for owner in range(n):
        dqkv_ref[owner, 0:shard, 3*width:] = part_out_ref[owner]
        if shard < rows:
            dqkv_ref[owner, shard:, 3*width:] = jnp.zeros((rows-shard, width), jnp.bfloat16)

SM=pl.BlockSpec(memory_space=pltpu.SMEM)
VM=pl.BlockSpec(memory_space=pltpu.VMEM)
def attention_forward(table, lengths, order, qkv, n, heads, depth, tile):
    total=sum(x.shape[0] for x in qkv); rows=total//n; width=heads*depth
    block=total//order.shape[1]
    meta=(len(qkv),n,heads,depth,tile,block)
    res=pl.pallas_call(functools.partial(fwd_kernel,meta),
        out_shape=[jax.ShapeDtypeStruct((rows,width),jnp.bfloat16)]*n+[jax.ShapeDtypeStruct((width,total),jnp.float32),jax.ShapeDtypeStruct((heads,total),jnp.float32)],
        in_specs=[SM,SM,SM]+[VM]*len(qkv), out_specs=[VM]*(n+2),
        scratch_shapes=[pltpu.VMEM((heads,total,width),jnp.bfloat16)]+[pltpu.VMEM((total,width),jnp.bfloat16)]*3,
        cost_estimate=cost(17),
        compiler_params=pltpu.CompilerParams(vmem_limit_bytes=VMEM_FWD),
        name="attention_forward")(table,lengths,order,*qkv)
    return list(res[:n]),res[n],res[n+1]
def attention_backward(table, lengths, order, qkv, grads, part_out, out_t, lse, heads, depth, tile):
    n=len(grads); rows=grads[0].shape[0]; total=n*rows; width=heads*depth
    block=total//order.shape[1]
    meta=(len(qkv),n,heads,depth,tile,block)
    f32=jnp.float32; b16=jnp.bfloat16
    return pl.pallas_call(functools.partial(bwd_kernel,meta),
        out_shape=jax.ShapeDtypeStruct((n,rows,4*width),b16),
        in_specs=[SM,SM,SM]+[VM]*(len(qkv)+n+3), out_specs=VM,
        scratch_shapes=[pltpu.VMEM((heads,total,width),b16),pltpu.VMEM((total,width),b16),pltpu.VMEM((total,width),b16),pltpu.VMEM((heads,total,width),b16),
          pltpu.VMEM((width,total),b16),pltpu.VMEM((heads,total),f32),pltpu.VMEM((width,total),f32),pltpu.VMEM((total,width),b16),pltpu.VMEM((total,width),f32),pltpu.VMEM((total,width),f32)],
        cost_estimate=cost(18),
        compiler_params=pltpu.CompilerParams(vmem_limit_bytes=VMEM_BWD),
        name="attention_backward")(table,lengths,order,*qkv,*grads,part_out,out_t,lse)


def tn(left, right):
    return lax.dot_general(left, right, (((0,), (0,)), ((), ())), preferred_element_type=jnp.float32)


def low(value):
    return value.astype(jnp.bfloat16)


def wide(value):
    return value.astype(jnp.float32)


def at(start, size):
    return pl.ds(pl.multiple_of(start, size), size)


def cost(microseconds):
    return pl.CostEstimate(flops=0, bytes_accessed=int(microseconds * 3.4e6), transcendentals=0)


def room(arrays, extra):
    total = 0
    for array in arrays:
        dims = [1, 1] + list(array.shape)
        rows, lanes = -(-dims[-2] // 16) * 16, -(-dims[-1] // 128) * 128
        total += math.prod(dims[:-2]) * rows * lanes * jnp.dtype(array.dtype).itemsize
    return pltpu.CompilerParams(vmem_limit_bytes=min(60 << 20, total + (extra << 20)))


def call(name, kernel, out, inputs, scratch=(), time=2.0, extra=8):
    return list(
        pl.pallas_call(
            kernel,
            out_shape=list(out),
            in_specs=[SM] + [VM] * (len(inputs) - 1),
            out_specs=[VM] * len(out),
            scratch_shapes=list(scratch),
            cost_estimate=cost(time),
            compiler_params=room(list(inputs[1:]) + list(out) + list(scratch), extra),
            name=name,
        )(*inputs)
    )


def shape(dims, dtype=jnp.bfloat16):
    return jax.ShapeDtypeStruct(tuple(dims), dtype)


def slice_kernel(own_width, table, w_ref, one_ref, two_ref, out_ref):
    shard, total = w_ref.shape
    for part in range(3):
        out_ref[0:shard, part * own_width : (part + 1) * own_width] = w_ref[
            :, at(part * (total // 3) + table[0, 0] * own_width, own_width)
        ]
    out_ref[shard : shard + 8, :] = gain_rows(wide(one_ref[...]), wide(two_ref[...]), 3 * own_width)


def gain_rows(one, two, lanes):
    shard = one.shape[1]
    if lanes > shard:
        rest = jnp.zeros((1, lanes - shard), jnp.float32)
        one, two = jnp.concatenate([one, rest], axis=1), jnp.concatenate([two, rest], axis=1)
    number = lax.broadcasted_iota(jnp.int32, (8, lanes), 0)
    return low(jnp.where(number == 0, one, jnp.where(number == 1, two, 0.0)))


def full_gain(table, n, pieces, row, gain_ref):
    shard = gain_ref.shape[1] // len(pieces)
    for slot, piece in enumerate(pieces):
        lines = wide(piece[pl.ds(piece.shape[0] - 8, 8), 0:shard])
        gain_ref[0:1, at(table[0, n + slot] * shard, shard)] = lines[row : row + 1]


def split_kernel(n, table, w_ref, *refs):
    outs, parts_ref = refs[:-1], refs[-1]
    count = len(outs)
    hidden = w_ref.shape[1] // (2 * count)
    for part in range(count):
        parts_ref[part, :, 0:hidden] = w_ref[:, part * hidden : (part + 1) * hidden]
        parts_ref[part, :, hidden:] = w_ref[:, (count + part) * hidden : (count + part + 1) * hidden]
    for slot in range(count):
        outs[slot][...] = parts_ref[table[0, n + slot]]


def project_kernel(n, table, rows_ref, *refs):
    pieces, attn_ref, qkv_ref, gain_ref, weight_ref = refs[:-4], refs[-4], refs[-3], refs[-2], refs[-1]
    shard = rows_ref.shape[1] // len(pieces)
    full_gain(table, n, pieces, 0, gain_ref)
    for slot, piece in enumerate(pieces):
        weight_ref[at(table[0, n + slot] * shard, shard), :] = piece[pl.ds(0, shard), :]
    value = wide(rows_ref[...])
    inverse = lax.rsqrt(jnp.mean(value * value, axis=1, keepdims=True) + EPS)
    attn_in = low(value * inverse * gain_ref[0:1, :])
    attn_ref[...] = attn_in
    qkv_ref[...] = low(nn(attn_in, weight_ref[...]))


def stage_rows(table, n, pieces, weight_ref):
    shard = pieces[0].shape[0]
    for slot, piece in enumerate(pieces):
        weight_ref[at(table[0, n + slot] * shard, shard), :] = piece[...]


def leave_kernel(n, count, table, tokens_ref, *refs):
    parts, outs, slices = refs[:n], refs[n : n + count], refs[n + count : n + 2 * count]
    resid_ref, ffn_ref, gain_ref, weight_ref = refs[n + 2 * count :]
    own_width = parts[0].shape[1]
    full_gain(table, n, slices, 1, gain_ref)
    stage_rows(table, n, outs, weight_ref)
    rows = tokens_ref.shape[0]
    attn = jnp.concatenate([parts[k][...] for k in range(n)], axis=1)
    ordered = jnp.concatenate([weight_ref[at(table[0, k] * own_width, own_width), :] for k in range(n)], axis=0)
    resid = wide(tokens_ref[...]) + nn(attn, ordered)
    resid_ref[...] = resid
    inverse = lax.rsqrt(jnp.mean(resid * resid, axis=1, keepdims=True) + EPS)
    ffn_ref[...] = low(resid * inverse * gain_ref[0:1, :])


def ffn_kernel(n, count, slots, table, *refs):
    ffn, cot = refs[:slots], refs[slots : 2 * slots]
    pieces, down_ref = refs[2 * slots : 2 * slots + count], refs[2 * slots + count]
    rest = refs[2 * slots + count + 1 :]
    terms, outs, hidden_ref, grad_ref = rest[:slots], rest[slots : 2 * slots], rest[2 * slots], rest[2 * slots + 1]
    gate_ref, up_ref = rest[2 * slots + 2 :]
    hidden = down_ref.shape[0]
    shard = pieces[0].shape[0]
    rows = ffn[0].shape[0]
    for slot, piece in enumerate(pieces):
        place = at(table[0, n + slot] * shard, shard)
        gate_ref[place, :] = piece[:, 0:hidden]
        up_ref[place, :] = piece[:, hidden:]
    for slot in range(slots):
        value = ffn[slot][...]
        gate = nn(value, gate_ref[...])
        upward = nn(value, up_ref[...])
        grad_hidden = nt(cot[slot][...], down_ref[...])
        sigma = jax.nn.sigmoid(gate)
        active = gate * sigma
        hidden_low = low(active * upward)
        grad_gate = low(grad_hidden * upward * (sigma + active * (1.0 - sigma)))
        grad_up = low(grad_hidden * active)
        terms[slot][...] = low(nt(grad_gate, gate_ref[...]) + nt(grad_up, up_ref[...]))
        outs[slot][...] = low(nn(hidden_low, down_ref[...]))
        place = pl.ds(slot * rows, rows)
        hidden_ref[place, :] = hidden_low
        grad_ref[place, 0:hidden] = grad_gate
        grad_ref[place, hidden:] = grad_up


def ffn_weight_kernel(n, count, table, *refs):
    ffn, cot, rest = refs[:count], refs[count : 2 * count], refs[2 * count :]
    hiddens, grads, rest = rest[: count // 2], rest[count // 2 : count], rest[count:]
    outs, (value_ref, turned_ref) = rest[:-2], rest[-2:]
    hidden = hiddens[0].shape[1]
    half = n // 2
    shard = ffn[0].shape[1] // count
    sub = shard // n
    lines = count * sub
    cut = outs[half].shape[0]
    hidden_all = jnp.concatenate([r[...] for r in hiddens], axis=0)
    grad_all = jnp.concatenate([r[...] for r in grads], axis=0)

    def store(slot, row, lanes, value):
        if slot != half:
            outs[slot if slot < half else slot + 1][row : row + sub, lanes] = value
        elif row < cut:
            outs[half][row : row + sub, lanes] = value
        else:
            outs[half + 1][row - cut : row - cut + sub, lanes] = value

    for f in range(count):
        lanes = slice(f * shard, (f + 1) * shard)
        ffn_all = jnp.concatenate([r[:, lanes] for r in ffn], axis=0)
        value_ref[...] = low(tn(ffn_all, grad_all))
        cot_all = jnp.concatenate([r[:, lanes] for r in cot], axis=0)
        turned_ref[...] = low(tn(cot_all, hidden_all))
        side, line = f // (count // 2), lines + (f % (count // 2)) * sub
        for slot in range(n):
            mine = at(table[0, slot] * sub, sub)
            store(slot, f * sub, slice(0, 2 * hidden), value_ref[mine, :])
            store(slot, line, slice(side * hidden, (side + 1) * hidden), turned_ref[mine, :])


def branch_kernel(n, count, got, table, resid_ref, cot_ref, *refs):
    terms, outs, slices = refs[:got], refs[got : got + count], refs[got + count : got + 2 * count]
    rest = refs[got + 2 * count :]
    grad_ref, branch_ref, parts = rest[0], rest[1], rest[2 : 2 + n]
    gain_ref, weight_ref = rest[2 + n :]
    own_width = parts[0].shape[1]
    full_gain(table, n, slices, 1, gain_ref)
    stage_rows(table, n, outs, weight_ref)
    resid = resid_ref[...]
    inverse = lax.rsqrt(jnp.mean(resid * resid, axis=1, keepdims=True) + EPS)
    normed = resid * inverse
    grad = wide(terms[0][...])
    for term in terms[1:]:
        grad = grad + wide(term[...])
    scaled = grad * gain_ref[0:1, :]
    inner = jnp.mean(scaled * normed, axis=1, keepdims=True)
    grad_resid = wide(cot_ref[...]) + inverse * (scaled - normed * inner)
    grad_ref[...] = grad_resid
    branch = low(grad_resid)
    branch_ref[...] = branch
    for k in range(n):
        parts[k][...] = low(nt(branch, weight_ref[at(table[0, k] * own_width, own_width), :]))


def out_weight_kernel(n, count, table, branch_ref, *refs):
    parts, outs, whole_ref = refs[:n], refs[n : n + count], refs[-1]
    own_width = parts[0].shape[1]
    shard = outs[0].shape[1]
    branch = branch_ref[...]
    for k in range(n):
        whole_ref[at(table[0, k] * own_width, own_width), :] = low(tn(parts[k][...], branch))
    for slot in range(count):
        lines = whole_ref[at(table[0, n + slot] * shard, shard), :]
        for owner in range(n):
            outs[slot][owner] = lines[:, owner * own_width : (owner + 1) * own_width]


def qkv_weight_kernel(given, n, count, table, *refs):
    attn, grads_ref, outs = refs[:given], refs[given], refs[given + 1 :]
    shard = outs[0].shape[0]
    used = outs[0].shape[1]
    grad_all = jnp.concatenate([grads_ref[table[0, k], :, 0:used] for k in range(n)], axis=0)
    for slot in range(count):
        lanes = at(table[0, n + slot] * shard, shard)
        attn_all = jnp.concatenate([r[:, lanes] for r in attn], axis=0)
        outs[slot][...] = low(tn(attn_all, grad_all))


def tail_kernel(n, count, table, tokens_ref, grad_ref, parts_ref, *refs):
    weights, slices = refs[:count], refs[count : 2 * count]
    out_ref, gain_ref, sum_ref, grads_ref = refs[2 * count :]
    own_width = parts_ref.shape[2] // 4
    width = tokens_ref.shape[1]
    shard = width // count
    full_gain(table, n, slices, 0, gain_ref)
    for owner in range(n):
        for part in range(3):
            start = part * width + owner * own_width
            grads_ref[:, start : start + own_width] = parts_ref[owner, :, part * own_width : (part + 1) * own_width]
    for slot in range(count):
        sum_ref[:, at(table[0, n + slot] * shard, shard)] = nt(grads_ref[...], weights[slot][...])
    value = wide(tokens_ref[...])
    inverse = lax.rsqrt(jnp.mean(value * value, axis=1, keepdims=True) + EPS)
    normed = value * inverse
    scaled = sum_ref[...] * gain_ref[0:1, :]
    inner = jnp.mean(scaled * normed, axis=1, keepdims=True)
    out_ref[...] = low(grad_ref[...] + inverse * (scaled - normed * inner))


def row_sums(product):
    rows, lanes = product.shape
    total = product[:, 0:128]
    for i in range(1, lanes // 128):
        total = total + product[:, i * 128 : (i + 1) * 128]
    return jnp.sum(jnp.transpose(total), axis=0, keepdims=True)


def ffn_final_kernel(n, count, factor, table, w_ref, gain_ref, *refs):
    pieces = refs[: n + 1]
    gu_ref, down_ref, gain_out_ref, turned_ref = refs[n + 1 :]
    hidden = down_ref.shape[0]
    sub = gu_ref.shape[0] // n
    half = n // 2
    for k in range(n):
        if k == half:
            piece = jnp.concatenate([wide(pieces[half][...]), wide(pieces[half + 1][...])], axis=0)
        else:
            piece = wide(pieces[k if k < half else k + 1][...])
        piece = piece * factor
        start = table[0, k] * sub
        for part in range(count):
            lines = piece[part * sub : (part + 1) * sub]
            gu_ref[at(start, sub), part * hidden : (part + 1) * hidden] = lines[:, 0:hidden]
            gu_ref[at(start, sub), (count + part) * hidden : (count + part + 1) * hidden] = lines[:, hidden:]
            side, line = part // (count // 2), (count + part % (count // 2)) * sub
            turned_ref[at(part * (n * sub) + start, sub), :] = piece[line : line + sub, side * hidden : (side + 1) * hidden]
    width = turned_ref.shape[0]
    for i in range(width // 128):
        down_ref[:, i * 128 : (i + 1) * 128] = jnp.transpose(turned_ref[i * 128 : (i + 1) * 128, :])
    gain_out_ref[...] = row_sums(wide(w_ref[...]) * gu_ref[...]) / wide(gain_ref[...])


def attn_final_kernel(n, factor, aligned, table, w_ref, gain_ref, *refs):
    pieces = refs[: n + 1]
    qkv_ref, out_ref, gain_out_ref = refs[n + 1 :]
    own_width = pieces[0].shape[1] // 4
    width = out_ref.shape[1]
    half = n // 2
    for k in range(n):
        if k == half:
            piece = jnp.concatenate([wide(pieces[half][...]), wide(pieces[half + 1][...])], axis=0)
        else:
            piece = wide(pieces[k if k < half else k + 1][...])
        piece = piece * factor
        for part in range(4):
            value = piece[:, part * own_width : (part + 1) * own_width]
            target = out_ref if part == 3 else qkv_ref
            base = 0 if part == 3 else part * width
            if aligned:
                target[:, at(base + table[0, k] * own_width, own_width)] = value
            else:
                target[:, base + k * own_width : base + (k + 1) * own_width] = value
    gain_out_ref[...] = row_sums(wide(w_ref[...]) * qkv_ref[...]) / wide(gain_ref[...])


def cut_kernel(n, table, own_ref, up_ref, down_ref, *refs):
    outs, rest_ref, sum_ref = refs[:-2], refs[-2], refs[-1]
    sum_ref[...] = low(wide(own_ref[...]) + wide(up_ref[...]) + wide(down_ref[...]))
    sub = outs[0].shape[0]
    for slot, out in enumerate(outs):
        out[...] = sum_ref[at(table[0, n + slot] * sub, sub), :]
    rest_ref[...] = sum_ref[len(outs) * sub :, :]


def pack_kernel(n, table, rest_ref, *refs):
    pieces, out_ref = refs[:-1], refs[-1]
    sub = pieces[0].shape[0]
    for slot, piece in enumerate(pieces):
        out_ref[at(table[0, n + slot] * sub, sub), :] = piece[...]
    out_ref[len(pieces) * sub :, :] = rest_ref[...]


def join_kernel(terms, table, *refs):
    qkv, back_ref, out_ref = refs[:terms], refs[terms], refs[-1]
    total = wide(qkv[0][...])
    for term in qkv[1:]:
        total = total + wide(term[...])
    start = total.shape[1]
    out_ref[:, 0:start] = low(total)
    shard = out_ref.shape[0]
    other = wide(back_ref[0, 0:shard, start:])
    for owner in range(1, back_ref.shape[0]):
        other = other + wide(back_ref[owner, 0:shard, start:])
    out_ref[:, start:] = low(other)


def ring_of(count):
    if count % 4 or count < 8:
        return list(range(count))
    across = count // 4
    order = []
    for along in range(4):
        columns = range(1, across) if along % 2 == 0 else range(across - 1, 0, -1)
        order += [along * across + column for column in columns]
    return order + [along * across for along in reversed(range(4))]


def ring_shift(value, ring, step):
    count = len(ring)
    return lax.ppermute(
        value, "ctx", [(ring[i], ring[(i + step) % count]) for i in range(count)]
    )


def tie(*values):
    return lax.optimization_barrier(values)


class Gather:
    def __init__(self, value, ring):
        self.ring, self.half, self.step = ring, len(ring) // 2, 1
        self.first, self.ahead, self.behind, self.far = value, [], [], None
        self.up, self.down = tie(ring_shift(value, ring, 1), ring_shift(value, ring, -1))

    def advance(self, *others):
        self.ahead.append(self.down)
        self.behind.append(self.up)
        self.up, self.down, *others = tie(self.up, self.down, *others)
        self.step += 1
        up, down = self.up, self.down
        if self.step == self.half:
            cut = up.shape[0] // 2
            up, down = up[:cut], down[cut:]
        self.up, self.down = tie(ring_shift(up, self.ring, 1), ring_shift(down, self.ring, -1))
        return others

    def slots(self):
        while self.step < self.half:
            self.advance()
        return [self.first] + self.ahead + [self.up, self.down] + self.behind[::-1]


class Scatter:
    def __init__(self, terms, ring):
        self.ring, self.half, self.terms = ring, len(ring) // 2, terms
        self.up, self.down = terms[self.half : self.half + 2]
        self.step = self.half
        self.send()

    def send(self):
        self.up, self.down = tie(ring_shift(self.up, self.ring, 1), ring_shift(self.down, self.ring, -1))

    def advance(self, *others):
        self.up, self.down, *others = tie(self.up, self.down, *others)
        up, down, cut = self.terms[self.step - 1], self.terms[len(self.ring) + 2 - self.step], self.up.shape[0]
        if self.step == self.half:
            rows = up.shape[0]
            self.up = low(wide(up) + jnp.pad(wide(self.up), ((0, rows - cut), (0, 0))))
            self.down = low(wide(down) + jnp.pad(wide(self.down), ((rows - cut, 0), (0, 0))))
        else:
            self.up, self.down = add_low(up, self.up), add_low(down, self.down)
        self.step -= 1
        self.send()
        return others

    def sums(self):
        while self.step > 1:
            self.advance()
        return [self.terms[0], self.up, self.down]


def ring_exchange(slots, ring):
    count = len(ring)
    result = [slots[0]] + [None] * (count - 1)
    for k in range(1, count):
        result[count - k] = ring_shift(slots[k], ring, k)
    return result


def exchange(array):
    return lax.all_to_all(array, "ctx", 0, 0, tiled=True)


def partner(value, count):
    return lax.ppermute(value, "fsdp", [(i, i ^ 1) for i in range(count)])


def chip_shift(value, count, step):
    return lax.ppermute(value, "fsdp", [(i, (i + 2 * step) % count) for i in range(count)])


def far_gather(value, count):
    return [value] + [chip_shift(value, count, -step) for step in range(1, count // 2)]


def near_gather(nears, count):
    slots = []
    for near in nears:
        slots += [near, partner(near, count)]
    return slots


def near_scatter(terms, count):
    return [add_low(terms[i], partner(terms[i + 1], count)) for i in range(0, count, 2)]


def far_scatter(nears, count):
    return [nears[0]] + [chip_shift(nears[step], count, step) for step in range(1, count // 2)]


def side_exchange(pieces, count):
    chips = count // 2
    received = [None] * count
    for step in range(chips):
        for flip in (0, 1):
            piece = pieces[2 * step + flip]
            if step or flip:
                pairs = [(i, ((i + 2 * step) % count) ^ flip) for i in range(count)]
                piece = lax.ppermute(piece, "fsdp", pairs)
            received[2 * ((chips - step) % chips) + flip] = piece
    return received


def add_low(left, right):
    return low(wide(left) + wide(right))


def total_of(terms):
    total = wide(terms[0])
    for term in terms[1:]:
        total = total + wide(term)
    return total


def body(
    tokens, cotangent, gain_attn, w_qkv, w_out, gain_ffn, w_gate_up, w_down, lengths, block_order
):
    rows, width = tokens.shape
    heads = HEADS
    depth = width // heads
    ctx = lax.axis_size("ctx")
    fsdp = lax.axis_size("fsdp")
    factor = 1.0 / math.sqrt(rows * ctx * fsdp)
    shard = width // fsdp
    hidden = w_down.shape[0]
    own_heads = heads // ctx
    own_width = own_heads * depth
    aligned = own_width % 128 == 0
    half = ctx // 2
    sub = shard // ctx
    lines = fsdp * sub
    ring = ring_of(ctx)
    chips = fsdp // 2
    entries = []
    for c in range(ctx):
        me = ring.index(c)
        for f in range(fsdp):
            owners = [ring[(me + k) % ctx] for k in range(ctx)]
            sides = [((f // 2 + s) % chips) * 2 + ((f % 2) ^ k) for s in range(chips) for k in (0, 1)]
            entries.append(owners + sides)
    device = lax.axis_index("ctx") * fsdp + lax.axis_index("fsdp")
    table = lax.dynamic_slice_in_dim(jnp.asarray(entries, jnp.int32), device, 1, 0)
    gain_one, gain_two = gain_attn.reshape(1, shard), gain_ffn.reshape(1, shard)
    f32 = jnp.float32
    gain_scratch = pltpu.VMEM((8, width), f32)
    square_scratch = pltpu.VMEM((width, width), jnp.bfloat16)

    going = Gather(tokens, ring)
    if aligned:
        (piece,) = call(
            "slice", functools.partial(slice_kernel, own_width),
            [shape((shard + 8, 3 * own_width))], [table, w_qkv, gain_one, gain_two],
            time=2.2,
        )
    else:
        mine = [
            lax.dynamic_slice(w_qkv, (0, part * width + table[0, 0] * own_width), (shard, own_width))
            for part in range(3)
        ]
        piece = jnp.concatenate(
            [jnp.concatenate(mine, axis=1), gain_rows(wide(gain_one), wide(gain_two), 3 * own_width)], axis=0
        )
    slices = far_gather(piece, fsdp)
    gate_pieces = call(
        "split", functools.partial(split_kernel, ctx),
        [shape((shard, 2 * hidden))] * fsdp, [table, w_gate_up],
        scratch=[pltpu.VMEM((fsdp, shard, 2 * hidden), jnp.bfloat16)],
        time=4,
    )
    slices, gate_pieces = going.advance(slices, gate_pieces)
    slices = near_gather(slices, fsdp)
    gate_pieces = side_exchange(gate_pieces, fsdp)

    def project(slot):
        return call(
            "project", functools.partial(project_kernel, ctx),
            [shape(slot.shape), shape((slot.shape[0], 3 * own_width))], [table, slot] + slices,
            scratch=[gain_scratch, pltpu.VMEM((width, 3 * own_width), jnp.bfloat16)],
            time=2.6,
        )

    first = project(tokens)
    ahead, behind = [project(going.ahead[0])], [project(going.behind[0])]
    first, ahead[0], behind[0], gate_pieces[1:3] = going.advance(first, ahead[0], behind[0], gate_pieces[1:3])
    for step in range(1, half - 1):
        ahead.append(project(going.ahead[step]))
        behind.append(project(going.behind[step]))
        if going.step < half:
            ahead[step], behind[step], gate_pieces[3:] = going.advance(ahead[step], behind[step], gate_pieces[3:])
    later_out, later_cot, unused = tie(w_out, cotangent, gate_pieces[-1])
    outs, cots = far_gather(later_out, fsdp), far_gather(later_cot, fsdp)
    *far, ahead, behind = tie(going.up, going.down, ahead, behind)
    pairs = [first] + ahead + [project(far[0]), project(far[1])] + behind[::-1]
    attn_slots, qkv = [pair[0] for pair in pairs], [pair[1] for pair in pairs]

    out_slots, out_t, log_total = attention_forward(
        table, lengths, block_order, qkv, ctx, own_heads, depth, TILE
    )
    out_slots, outs, cots = tie(out_slots, outs, cots)
    attn_parts = ring_exchange(out_slots, ring)
    outs, cots = near_gather(outs, fsdp), near_gather(cots, fsdp)
    resid, ffn_in = call(
        "leave", functools.partial(leave_kernel, ctx, fsdp),
        [shape((rows, width), f32), shape((rows, width))],
        [table, tokens] + attn_parts + outs + slices,
        scratch=[gain_scratch, square_scratch],
        time=4.1,
    )

    nears = far_gather(ffn_in, fsdp)
    ffns, grad_terms, out_terms, hiddens, grads = [], [], [], [], []
    for chip in range(chips):
        ffn_pair = [nears[chip], partner(nears[chip], fsdp)]
        result = call(
            "feed_forward", functools.partial(ffn_kernel, ctx, fsdp, 2),
            [shape((rows, width))] * 4 + [shape((2 * rows, hidden)), shape((2 * rows, 2 * hidden))],
            [table] + ffn_pair + cots[2 * chip : 2 * chip + 2] + gate_pieces + [w_down],
            scratch=[pltpu.VMEM((width, hidden), jnp.bfloat16)] * 2,
            time=9.5,
        )
        if chip == 0:
            result, nears[1:] = tie(result, nears[1:])
        ffns += ffn_pair
        grad_terms += result[0:2]
        out_terms += result[2:4]
        hiddens.append(result[4])
        grads.append(result[5])
    grad_nears = near_scatter(grad_terms, fsdp)
    hiddens, grad_nears = tie(hiddens, grad_nears)
    grad_parts = far_scatter(grad_nears, fsdp)
    terms_ffn = call(
        "feed_forward_weights", functools.partial(ffn_weight_kernel, ctx, fsdp),
        [shape((lines + lines // 2, 2 * hidden))] * half
        + [shape(((lines + lines // 2) // 2, 2 * hidden))] * 2
        + [shape((lines + lines // 2, 2 * hidden))] * (half - 1),
        [table] + ffns + cots + hiddens + grads,
        scratch=[pltpu.VMEM((shard, 2 * hidden), jnp.bfloat16), pltpu.VMEM((shard, hidden), jnp.bfloat16)],
        time=12,
    )
    terms_ffn, grad_parts = tie(terms_ffn, grad_parts)
    ffn_sums = Scatter(terms_ffn, ring)
    grad_resid, branch, *grad_attn = call(
        "branch", functools.partial(branch_kernel, ctx, fsdp, len(grad_parts)),
        [shape((rows, width), f32), shape((rows, width))] + [shape((rows, own_width))] * ctx,
        [table, resid, cotangent] + grad_parts + outs + slices,
        scratch=[gain_scratch, square_scratch],
        time=5,
    )
    grad_attn, branch, ffn_sums.up, ffn_sums.down = tie(grad_attn, branch, ffn_sums.up, ffn_sums.down)
    grad_slots = ring_exchange(grad_attn, ring)
    out_sides = call(
        "out_weights", functools.partial(out_weight_kernel, ctx, fsdp),
        [shape((ctx, shard, own_width))] * fsdp, [table, branch] + attn_parts,
        scratch=[square_scratch],
        time=3.3,
    )
    out_nears = near_scatter(out_sides, fsdp)

    out_parts = far_scatter(out_nears, fsdp)
    part_out = low(total_of(out_parts))
    grad_slots, part_out = ffn_sums.advance(grad_slots, part_out)
    grad_qkv = attention_backward(
        table, lengths, block_order, qkv, grad_slots, part_out, out_t, log_total, own_heads, depth, TILE
    )
    qkv_sides = call(
        "qkv_weights", functools.partial(qkv_weight_kernel, len(attn_slots), ctx, fsdp),
        [shape((shard, 3 * own_width))] * fsdp, [table] + attn_slots + [grad_qkv],
        time=6,
    )
    grad_qkv, qkv_sides = tie(grad_qkv, qkv_sides)
    grad_back = exchange(grad_qkv)
    qkv_sides, unused = ffn_sums.advance(qkv_sides, grad_qkv)
    later_qkv, unused = tie(w_qkv, qkv_sides[0])
    qkv_nears = far_gather(later_qkv, fsdp)
    qkv_sum = far_scatter(near_scatter(qkv_sides, fsdp), fsdp)

    qkv_sum = ffn_sums.advance(qkv_sum)[0] if ffn_sums.step > 1 else qkv_sum
    own_sum, ffn_up, ffn_down = ffn_sums.sums()
    *gate_sides, rest = call(
        "cut", functools.partial(cut_kernel, ctx),
        [shape((sub, 2 * hidden))] * fsdp + [shape((lines // 2, 2 * hidden))],
        [table, own_sum, ffn_up, ffn_down],
        scratch=[pltpu.VMEM((lines + lines // 2, 2 * hidden), jnp.bfloat16)],
        time=3,
    )
    (joined,) = call(
        "join", functools.partial(join_kernel, len(qkv_sum)),
        [shape((shard, 4 * own_width))], [table] + qkv_sum + [grad_back],
        time=2.5,
    )
    gate_sides = side_exchange(gate_sides, fsdp)
    gate_sides, joined = tie(gate_sides, joined)
    (packed,) = call(
        "pack", functools.partial(pack_kernel, ctx),
        [shape((lines + lines // 2, 2 * hidden))], [table, rest] + gate_sides,
        time=2,
    )
    ffn_going = Gather(packed, ring)
    attn_going = Gather(joined, ring)
    weights = near_gather(qkv_nears, fsdp)
    (grad_tokens,) = call(
        "tail", functools.partial(tail_kernel, ctx, fsdp),
        [shape((rows, width))], [table, tokens, grad_resid, grad_back] + weights + slices,
        scratch=[gain_scratch, pltpu.VMEM((rows, width), f32), pltpu.VMEM((rows, 3 * width), jnp.bfloat16)],
        time=8,
    )
    ffn_going.advance()
    (grad_tokens,) = ffn_going.advance(grad_tokens)
    grad_w_gate_up, grad_w_down, grad_gain_ffn = call(
        "feed_forward_final", functools.partial(ffn_final_kernel, ctx, fsdp, factor),
        [shape((shard, 2 * hidden * fsdp), f32), shape((hidden, width), f32), shape((1, shard), f32)],
        [table, w_gate_up, gain_two] + ffn_going.slots(),
        scratch=[pltpu.VMEM((width, hidden), f32)],
        time=8,
    )
    grad_w_qkv, grad_w_out, grad_gain_attn = call(
        "attention_final", functools.partial(attn_final_kernel, ctx, factor, aligned),
        [shape((shard, 3 * width), f32), shape((shard, width), f32), shape((1, shard), f32)],
        [table, w_qkv if aligned else unmixed(relative(w_qkv, table, ctx), ctx, own_width), gain_one] + attn_going.slots(),
        time=4.6,
    )
    if not aligned:
        grad_w_qkv, grad_w_out = ordered(grad_w_qkv, table, 3, ctx), ordered(grad_w_out, table, 1, ctx)
    output = low(resid + total_of(far_scatter(near_scatter(out_terms, fsdp), fsdp)))
    return (
        output,
        grad_tokens,
        grad_gain_attn.reshape(shard),
        grad_w_qkv,
        grad_w_out,
        grad_gain_ffn.reshape(shard),
        grad_w_gate_up,
        grad_w_down,
    )


def relative(weight, table, ctx):
    rows = weight.shape[0]
    parts = weight.reshape(rows, 3, ctx, -1)
    slots = [lax.dynamic_index_in_dim(parts, table[0, k], 2, keepdims=False) for k in range(ctx)]
    return jnp.concatenate([slot.reshape(rows, -1) for slot in slots], axis=1)


def unmixed(weight, ctx, own_width):
    rows = weight.shape[0]
    return weight.reshape(rows, ctx, 3, own_width).transpose(0, 2, 1, 3).reshape(rows, -1)


def ordered(array, table, parts, ctx):
    rows = array.shape[0]
    split = array.reshape(rows, parts, ctx, -1)
    result = jnp.zeros_like(split)
    for k in range(ctx):
        result = lax.dynamic_update_slice(result, split[:, :, k : k + 1], (0, 0, table[0, k], 0))
    return result.reshape(rows, -1)


def solution(mesh):
    in_specs = (
        P(("fsdp", "ctx"), None),
        P(("fsdp", "ctx"), None),
        P("fsdp"),
        P("fsdp", None),
        P("fsdp", None),
        P("fsdp"),
        P("fsdp", None),
        P("fsdp", None),
        P("fsdp", None),
        P("fsdp", None),
    )
    out_specs = (
        P(("fsdp", "ctx"), None),
        P(("fsdp", "ctx"), None),
        P("fsdp"),
        P("fsdp", None),
        P("fsdp", None),
        P("fsdp"),
        P("fsdp", None),
        P("fsdp", None),
    )
    return jax.shard_map(body, mesh=mesh, in_specs=in_specs, out_specs=out_specs, check_vma=False)
```

```python
import functools
import math

import jax
import jax.numpy as jnp
from jax import lax
from jax.experimental import pallas as pl
from jax.experimental.pallas import tpu as pltpu
from jax.sharding import PartitionSpec as P

HEADS = 16
TILE = 256
VMEM_FWD = 26 << 20
VMEM_BWD = 34 << 20


EPS = 1e-05
MASKED=-1e30
def nt(a,b): return lax.dot_general(a,b,(((1,),(1,)),((),())),preferred_element_type=jnp.float32)
def nn(a,b): return lax.dot_general(a,b,(((1,),(0,)),((),())),preferred_element_type=jnp.float32)

def ends_of(lengths_ref):
    ends = [lengths_ref[0, 0]]
    for i in range(1, lengths_ref.shape[1]):
        ends.append(ends[-1] + lengths_ref[0, i])
    return ends

def first_tile(ends, position, tile):
    start = jnp.int32(0)
    for end in ends[:-1]:
        start = jnp.where(end <= position, end, start)
    return start // tile

def last_tile(ends, position, tile):
    last = ends[-1]
    for end in reversed(ends[:-1]):
        last = jnp.where(end > position, end, last)
    return (last - 1) // tile

def seen(ends, query_start, key_start, queries, keys):
    pos_query = query_start + lax.broadcasted_iota(jnp.int32, (1, queries), 1)
    start = jnp.zeros((1, queries), jnp.int32)
    for end in ends[:-1]:
        start = jnp.where(pos_query >= end, end, start)
    pos_key = key_start + lax.broadcasted_iota(jnp.int32, (keys, queries), 0)
    return (pos_key <= pos_query) & (pos_key >= start)

def head_lanes(x, head, heads, depth):
    if heads == 1:
        return x
    lane = lax.broadcasted_iota(jnp.int32, x.shape, 1)
    return jnp.where((lane >= head * depth) & (lane < (head + 1) * depth), x, jnp.zeros_like(x))

def placed(slots, block, table, order_ref, per):
    number = 0
    for slot in slots:
        for row in range(0, slot.shape[0], block):
            position = order_ref[0, table[0, number // per] * per + number % per] * block
            yield slot, pl.ds(row, block), pl.ds(pl.multiple_of(position, block), block)
            number += 1

def stored(owners, block, order_ref, per):
    for owner in range(owners):
        for b in range(per):
            position = order_ref[0, owner * per + b] * block
            yield owner, pl.ds(b * block, block), pl.ds(pl.multiple_of(position, block), block)

def fwd_kernel(meta, table, lengths_ref, order_ref, *refs):
    given, n, heads, depth, tile, block = meta
    qkv_refs, out_refs = refs[:given], refs[given:given+n]
    out_t_ref, lse_ref = refs[given+n], refs[given+n+1]
    q_ref, k_ref, v_ref, o_ref = refs[given+n+2:]
    ends = ends_of(lengths_ref)
    width = heads*depth
    scale = depth ** (-0.5)
    per = out_refs[0].shape[0] // block
    for slot, src, dst in placed(qkv_refs, block, table, order_ref, per):
        q = slot[src, 0:width].astype(jnp.float32)*scale
        for h in range(heads):
            q_ref[h, dst, :] = head_lanes(q, h, heads, depth).astype(jnp.bfloat16)
        k_ref[dst, :] = slot[src, width:2*width]
        v_ref[dst, :] = slot[src, 2*width:]
    wide_tile = 2 * tile
    tiles = q_ref.shape[1] // wide_tile
    def one_query(t, _):
        rows = pl.ds(pl.multiple_of(t*wide_tile, wide_tile), wide_tile)
        qs = [q_ref[h, rows, :] for h in range(heads)]
        def one_key(j, carry):
            keys = pl.ds(pl.multiple_of(j*tile, tile), tile)
            k = k_ref[keys, :]
            v_t = jnp.transpose(v_ref[keys, :].astype(jnp.float32)).astype(jnp.bfloat16)
            mask = seen(ends, t*wide_tile, j*tile, wide_tile, tile)
            new = []
            for h in range(heads):
                m, l, acc = carry[h]
                s = jnp.where(mask, nt(k, qs[h]), MASKED)
                m_new = jnp.maximum(m, jnp.max(s, axis=0, keepdims=True))
                e = jnp.exp(s - m_new)
                alpha = jnp.exp(m - m_new)
                l = l*alpha + jnp.sum(e, axis=0, keepdims=True)
                acc = acc*alpha + nn(v_t[h*depth:(h+1)*depth], e.astype(jnp.bfloat16))
                new.append((m_new, l, acc))
            return tuple(new)
        init = tuple((jnp.full((1,wide_tile),MASKED,jnp.float32), jnp.zeros((1,wide_tile),jnp.float32), jnp.zeros((depth,wide_tile),jnp.float32)) for _ in range(heads))
        final = lax.fori_loop(first_tile(ends, t*wide_tile, tile), 2*t+2, one_key, init)
        outs = []
        for h in range(heads):
            m, l, acc = final[h]
            outs.append(acc / l)
            lse_ref[h:h+1, rows] = m + jnp.log(l)
        out_t = jnp.concatenate(outs, axis=0) if heads > 1 else outs[0]
        out_t_ref[:, rows] = out_t
        o_ref[rows, :] = jnp.transpose(out_t).astype(jnp.bfloat16)
        return 0
    lax.fori_loop(0, tiles, one_query, 0)
    for slot, dst, src in placed(out_refs, block, table, order_ref, per):
        slot[dst, :] = o_ref[src, :]

def bwd_kernel(meta, table, lengths_ref, order_ref, *refs):
    given, n, heads, depth, tile, block = meta
    qkv_refs, grad_refs = refs[:given], refs[given:given+n]
    refs = refs[n:]
    part_out_ref, out_t_ref, lse_ref, dqkv_ref = refs[given:given+4]
    ends = ends_of(lengths_ref)
    q_ref, k_ref, v_ref, g_ref, k_t_ref, delta_ref, dq_t_ref, dq_ref, dk_ref, dv_ref = refs[given+4:]
    width = heads*depth
    scale = depth ** (-0.5)
    per = dqkv_ref.shape[1] // block
    total = k_ref.shape[0]
    for slot, src, dst in placed(qkv_refs, block, table, order_ref, per):
        q = slot[src, 0:width].astype(jnp.float32)*scale
        for h in range(heads):
            q_ref[h, dst, :] = head_lanes(q, h, heads, depth).astype(jnp.bfloat16)
        k_ref[dst, :] = slot[src, width:2*width]
        v_ref[dst, :] = slot[src, 2*width:]
    for slot, src, dst in placed(grad_refs, block, table, order_ref, per):
        g = slot[src, :].astype(jnp.float32)
        for h in range(heads):
            g_ref[h, dst, :] = head_lanes(g, h, heads, depth).astype(jnp.bfloat16)
    tiles = total // tile
    def prepare(t, _):
        rows = pl.ds(pl.multiple_of(t*tile, tile), tile)
        k_t_ref[:, rows] = jnp.transpose(k_ref[rows, :].astype(jnp.float32)).astype(jnp.bfloat16)
        g = g_ref[0, rows, :].astype(jnp.float32)
        for h in range(1, heads):
            g = g + g_ref[h, rows, :].astype(jnp.float32)
        prod = jnp.transpose(g) * out_t_ref[:, rows]
        for h in range(heads):
            delta_ref[h:h+1, rows] = jnp.sum(prod[h*depth:(h+1)*depth], axis=0, keepdims=True)
        dq_t_ref[:, rows] = jnp.zeros((width, tile), jnp.float32)
        return 0
    lax.fori_loop(0, tiles, prepare, 0)
    wide_tile = 2 * tile
    def one_key(j, _):
        keys = pl.ds(pl.multiple_of(j*tile, tile), tile)
        k = k_ref[keys, :]
        v = v_ref[keys, :]
        k_t = k_t_ref[:, keys]
        dk_ref[keys, :] = jnp.zeros((tile, width), jnp.float32)
        dv_ref[keys, :] = jnp.zeros((tile, width), jnp.float32)
        def one_query(t, _):
            rows = pl.ds(pl.multiple_of(t*wide_tile, wide_tile), wide_tile)
            mask = seen(ends, t*wide_tile, j*tile, wide_tile, tile)
            dk = dk_ref[keys, :]
            dv = dv_ref[keys, :]
            for h in range(heads):
                q = q_ref[h, rows, :]
                g = g_ref[h, rows, :]
                s = nt(k, q)
                p = jnp.where(mask, jnp.exp(s - lse_ref[h:h+1, rows]), 0.0)
                dp = nt(v, g)
                ds = (p*(dp - delta_ref[h:h+1, rows])).astype(jnp.bfloat16)
                dv = dv + nn(p.astype(jnp.bfloat16), g)
                dk = dk + nn(ds, q)
                part = pl.ds(h*depth, depth)
                dq_t_ref[part, rows] = dq_t_ref[part, rows] + nn(k_t[h*depth:(h+1)*depth], ds)
            dk_ref[keys, :] = dk
            dv_ref[keys, :] = dv
            return 0
        lax.fori_loop(j//2, last_tile(ends, j*tile + tile - 1, wide_tile) + 1, one_query, 0)
        return 0
    lax.fori_loop(0, tiles, one_key, 0)
    def finish(t, _):
        rows = pl.ds(pl.multiple_of(t*tile, tile), tile)
        dq_ref[rows, :] = (jnp.transpose(dq_t_ref[:, rows])*scale).astype(jnp.bfloat16)
        return 0
    lax.fori_loop(0, tiles, finish, 0)
    for owner, dst, src in stored(n, block, order_ref, per):
        dqkv_ref[owner, dst, 0:width] = dq_ref[src, :]
        dqkv_ref[owner, dst, width:2*width] = dk_ref[src, :].astype(jnp.bfloat16)
        dqkv_ref[owner, dst, 2*width:3*width] = dv_ref[src, :].astype(jnp.bfloat16)
    shard = part_out_ref.shape[1]
    rows = dqkv_ref.shape[1]
    for owner in range(n):
        dqkv_ref[owner, 0:shard, 3*width:] = part_out_ref[owner]
        if shard < rows:
            dqkv_ref[owner, shard:, 3*width:] = jnp.zeros((rows-shard, width), jnp.bfloat16)

SM=pl.BlockSpec(memory_space=pltpu.SMEM)
VM=pl.BlockSpec(memory_space=pltpu.VMEM)
def attention_forward(table, lengths, order, qkv, n, heads, depth, tile):
    total=sum(x.shape[0] for x in qkv); rows=total//n; width=heads*depth
    block=total//order.shape[1]
    meta=(len(qkv),n,heads,depth,tile,block)
    res=pl.pallas_call(functools.partial(fwd_kernel,meta),
        out_shape=[jax.ShapeDtypeStruct((rows,width),jnp.bfloat16)]*n+[jax.ShapeDtypeStruct((width,total),jnp.float32),jax.ShapeDtypeStruct((heads,total),jnp.float32)],
        in_specs=[SM,SM,SM]+[VM]*len(qkv), out_specs=[VM]*(n+2),
        scratch_shapes=[pltpu.VMEM((heads,total,width),jnp.bfloat16)]+[pltpu.VMEM((total,width),jnp.bfloat16)]*3,
        cost_estimate=cost(17),
        compiler_params=pltpu.CompilerParams(vmem_limit_bytes=VMEM_FWD),
        name="attention_forward")(table,lengths,order,*qkv)
    return list(res[:n]),res[n],res[n+1]
def attention_backward(table, lengths, order, qkv, grads, part_out, out_t, lse, heads, depth, tile):
    n=len(grads); rows=grads[0].shape[0]; total=n*rows; width=heads*depth
    block=total//order.shape[1]
    meta=(len(qkv),n,heads,depth,tile,block)
    f32=jnp.float32; b16=jnp.bfloat16
    return pl.pallas_call(functools.partial(bwd_kernel,meta),
        out_shape=jax.ShapeDtypeStruct((n,rows,4*width),b16),
        in_specs=[SM,SM,SM]+[VM]*(len(qkv)+n+3), out_specs=VM,
        scratch_shapes=[pltpu.VMEM((heads,total,width),b16),pltpu.VMEM((total,width),b16),pltpu.VMEM((total,width),b16),pltpu.VMEM((heads,total,width),b16),
          pltpu.VMEM((width,total),b16),pltpu.VMEM((heads,total),f32),pltpu.VMEM((width,total),f32),pltpu.VMEM((total,width),b16),pltpu.VMEM((total,width),f32),pltpu.VMEM((total,width),f32)],
        cost_estimate=cost(18),
        compiler_params=pltpu.CompilerParams(vmem_limit_bytes=VMEM_BWD),
        name="attention_backward")(table,lengths,order,*qkv,*grads,part_out,out_t,lse)


def tn(left, right):
    return lax.dot_general(left, right, (((0,), (0,)), ((), ())), preferred_element_type=jnp.float32)


def low(value):
    return value.astype(jnp.bfloat16)


def wide(value):
    return value.astype(jnp.float32)


def at(start, size):
    return pl.ds(pl.multiple_of(start, size), size)


def cost(microseconds):
    return pl.CostEstimate(flops=0, bytes_accessed=int(microseconds * 3.4e6), transcendentals=0)


def room(arrays, extra):
    total = 0
    for array in arrays:
        dims = [1, 1] + list(array.shape)
        rows, lanes = -(-dims[-2] // 16) * 16, -(-dims[-1] // 128) * 128
        total += math.prod(dims[:-2]) * rows * lanes * jnp.dtype(array.dtype).itemsize
    return pltpu.CompilerParams(vmem_limit_bytes=min(60 << 20, total + (extra << 20)))


def call(name, kernel, out, inputs, scratch=(), time=2.0, extra=8):
    return list(
        pl.pallas_call(
            kernel,
            out_shape=list(out),
            in_specs=[SM] + [VM] * (len(inputs) - 1),
            out_specs=[VM] * len(out),
            scratch_shapes=list(scratch),
            cost_estimate=cost(time),
            compiler_params=room(list(inputs[1:]) + list(out) + list(scratch), extra),
            name=name,
        )(*inputs)
    )


def shape(dims, dtype=jnp.bfloat16):
    return jax.ShapeDtypeStruct(tuple(dims), dtype)


def slice_kernel(own_width, table, w_ref, one_ref, two_ref, out_ref):
    shard, total = w_ref.shape
    for part in range(3):
        out_ref[0:shard, part * own_width : (part + 1) * own_width] = w_ref[
            :, at(part * (total // 3) + table[0, 0] * own_width, own_width)
        ]
    out_ref[shard : shard + 8, :] = gain_rows(wide(one_ref[...]), wide(two_ref[...]), 3 * own_width)


def gain_rows(one, two, lanes):
    shard = one.shape[1]
    if lanes > shard:
        rest = jnp.zeros((1, lanes - shard), jnp.float32)
        one, two = jnp.concatenate([one, rest], axis=1), jnp.concatenate([two, rest], axis=1)
    number = lax.broadcasted_iota(jnp.int32, (8, lanes), 0)
    return low(jnp.where(number == 0, one, jnp.where(number == 1, two, 0.0)))


def full_gain(table, n, pieces, row, gain_ref):
    shard = gain_ref.shape[1] // len(pieces)
    for slot, piece in enumerate(pieces):
        lines = wide(piece[pl.ds(piece.shape[0] - 8, 8), 0:shard])
        gain_ref[0:1, at(table[0, n + slot] * shard, shard)] = lines[row : row + 1]


def split_kernel(n, table, w_ref, *refs):
    outs, parts_ref = refs[:-1], refs[-1]
    count = len(outs)
    hidden = w_ref.shape[1] // (2 * count)
    for part in range(count):
        parts_ref[part, :, 0:hidden] = w_ref[:, part * hidden : (part + 1) * hidden]
        parts_ref[part, :, hidden:] = w_ref[:, (count + part) * hidden : (count + part + 1) * hidden]
    for slot in range(count):
        outs[slot][...] = parts_ref[table[0, n + slot]]


def project_kernel(n, table, rows_ref, *refs):
    pieces, attn_ref, qkv_ref, gain_ref, weight_ref = refs[:-4], refs[-4], refs[-3], refs[-2], refs[-1]
    shard = rows_ref.shape[1] // len(pieces)
    full_gain(table, n, pieces, 0, gain_ref)
    for slot, piece in enumerate(pieces):
        weight_ref[at(table[0, n + slot] * shard, shard), :] = piece[pl.ds(0, shard), :]
    value = wide(rows_ref[...])
    inverse = lax.rsqrt(jnp.mean(value * value, axis=1, keepdims=True) + EPS)
    attn_in = low(value * inverse * gain_ref[0:1, :])
    attn_ref[...] = attn_in
    qkv_ref[...] = low(nn(attn_in, weight_ref[...]))


def stage_rows(table, n, pieces, weight_ref):
    shard = pieces[0].shape[0]
    for slot, piece in enumerate(pieces):
        weight_ref[at(table[0, n + slot] * shard, shard), :] = piece[...]


def leave_kernel(n, count, table, tokens_ref, *refs):
    parts, outs, slices = refs[:n], refs[n : n + count], refs[n + count : n + 2 * count]
    resid_ref, ffn_ref, gain_ref, weight_ref = refs[n + 2 * count :]
    own_width = parts[0].shape[1]
    full_gain(table, n, slices, 1, gain_ref)
    stage_rows(table, n, outs, weight_ref)
    rows = tokens_ref.shape[0]
    attn = jnp.concatenate([parts[k][...] for k in range(n)], axis=1)
    ordered = jnp.concatenate([weight_ref[at(table[0, k] * own_width, own_width), :] for k in range(n)], axis=0)
    resid = wide(tokens_ref[...]) + nn(attn, ordered)
    resid_ref[...] = resid
    inverse = lax.rsqrt(jnp.mean(resid * resid, axis=1, keepdims=True) + EPS)
    ffn_ref[...] = low(resid * inverse * gain_ref[0:1, :])


def ffn_kernel(n, count, slots, table, *refs):
    ffn, cot = refs[:slots], refs[slots : 2 * slots]
    pieces, down_ref = refs[2 * slots : 2 * slots + count], refs[2 * slots + count]
    rest = refs[2 * slots + count + 1 :]
    terms, outs, hidden_ref, grad_ref = rest[:slots], rest[slots : 2 * slots], rest[2 * slots], rest[2 * slots + 1]
    gate_ref, up_ref = rest[2 * slots + 2 :]
    hidden = down_ref.shape[0]
    shard = pieces[0].shape[0]
    rows = ffn[0].shape[0]
    for slot, piece in enumerate(pieces):
        place = at(table[0, n + slot] * shard, shard)
        gate_ref[place, :] = piece[:, 0:hidden]
        up_ref[place, :] = piece[:, hidden:]
    for slot in range(slots):
        value = ffn[slot][...]
        gate = nn(value, gate_ref[...])
        upward = nn(value, up_ref[...])
        grad_hidden = nt(cot[slot][...], down_ref[...])
        sigma = jax.nn.sigmoid(gate)
        active = gate * sigma
        hidden_low = low(active * upward)
        grad_gate = low(grad_hidden * upward * (sigma + active * (1.0 - sigma)))
        grad_up = low(grad_hidden * active)
        terms[slot][...] = low(nt(grad_gate, gate_ref[...]) + nt(grad_up, up_ref[...]))
        outs[slot][...] = low(nn(hidden_low, down_ref[...]))
        place = pl.ds(slot * rows, rows)
        hidden_ref[place, :] = hidden_low
        grad_ref[place, 0:hidden] = grad_gate
        grad_ref[place, hidden:] = grad_up


def ffn_weight_kernel(n, count, table, *refs):
    ffn, cot, rest = refs[:count], refs[count : 2 * count], refs[2 * count :]
    hiddens, grads, rest = rest[: count // 2], rest[count // 2 : count], rest[count:]
    outs, (value_ref, turned_ref) = rest[:-2], rest[-2:]
    hidden = hiddens[0].shape[1]
    half = n // 2
    shard = ffn[0].shape[1] // count
    sub = shard // n
    lines = count * sub
    cut = outs[half].shape[0]
    hidden_all = jnp.concatenate([r[...] for r in hiddens], axis=0)
    grad_all = jnp.concatenate([r[...] for r in grads], axis=0)

    def store(slot, row, lanes, value):
        if slot != half:
            outs[slot if slot < half else slot + 1][row : row + sub, lanes] = value
        elif row < cut:
            outs[half][row : row + sub, lanes] = value
        else:
            outs[half + 1][row - cut : row - cut + sub, lanes] = value

    for f in range(count):
        lanes = slice(f * shard, (f + 1) * shard)
        ffn_all = jnp.concatenate([r[:, lanes] for r in ffn], axis=0)
        value_ref[...] = low(tn(ffn_all, grad_all))
        cot_all = jnp.concatenate([r[:, lanes] for r in cot], axis=0)
        turned_ref[...] = low(tn(cot_all, hidden_all))
        side, line = f // (count // 2), lines + (f % (count // 2)) * sub
        for slot in range(n):
            mine = at(table[0, slot] * sub, sub)
            store(slot, f * sub, slice(0, 2 * hidden), value_ref[mine, :])
            store(slot, line, slice(side * hidden, (side + 1) * hidden), turned_ref[mine, :])


def branch_kernel(n, count, got, table, resid_ref, cot_ref, *refs):
    terms, outs, slices = refs[:got], refs[got : got + count], refs[got + count : got + 2 * count]
    rest = refs[got + 2 * count :]
    grad_ref, branch_ref, parts = rest[0], rest[1], rest[2 : 2 + n]
    gain_ref, weight_ref = rest[2 + n :]
    own_width = parts[0].shape[1]
    full_gain(table, n, slices, 1, gain_ref)
    stage_rows(table, n, outs, weight_ref)
    resid = resid_ref[...]
    inverse = lax.rsqrt(jnp.mean(resid * resid, axis=1, keepdims=True) + EPS)
    normed = resid * inverse
    grad = wide(terms[0][...])
    for term in terms[1:]:
        grad = grad + wide(term[...])
    scaled = grad * gain_ref[0:1, :]
    inner = jnp.mean(scaled * normed, axis=1, keepdims=True)
    grad_resid = wide(cot_ref[...]) + inverse * (scaled - normed * inner)
    grad_ref[...] = grad_resid
    branch = low(grad_resid)
    branch_ref[...] = branch
    for k in range(n):
        parts[k][...] = low(nt(branch, weight_ref[at(table[0, k] * own_width, own_width), :]))


def out_weight_kernel(n, count, table, branch_ref, *refs):
    parts, outs, whole_ref = refs[:n], refs[n : n + count], refs[-1]
    own_width = parts[0].shape[1]
    shard = outs[0].shape[1]
    branch = branch_ref[...]
    for k in range(n):
        whole_ref[at(table[0, k] * own_width, own_width), :] = low(tn(parts[k][...], branch))
    for slot in range(count):
        lines = whole_ref[at(table[0, n + slot] * shard, shard), :]
        for owner in range(n):
            outs[slot][owner] = lines[:, owner * own_width : (owner + 1) * own_width]


def qkv_weight_kernel(given, n, count, table, *refs):
    attn, grads_ref, outs = refs[:given], refs[given], refs[given + 1 :]
    shard = outs[0].shape[0]
    used = outs[0].shape[1]
    grad_all = jnp.concatenate([grads_ref[table[0, k], :, 0:used] for k in range(n)], axis=0)
    for slot in range(count):
        lanes = at(table[0, n + slot] * shard, shard)
        attn_all = jnp.concatenate([r[:, lanes] for r in attn], axis=0)
        outs[slot][...] = low(tn(attn_all, grad_all))


def tail_kernel(n, count, table, tokens_ref, grad_ref, parts_ref, *refs):
    weights, slices = refs[:count], refs[count : 2 * count]
    out_ref, gain_ref, sum_ref, grads_ref = refs[2 * count :]
    own_width = parts_ref.shape[2] // 4
    width = tokens_ref.shape[1]
    shard = width // count
    full_gain(table, n, slices, 0, gain_ref)
    for owner in range(n):
        for part in range(3):
            start = part * width + owner * own_width
            grads_ref[:, start : start + own_width] = parts_ref[owner, :, part * own_width : (part + 1) * own_width]
    for slot in range(count):
        sum_ref[:, at(table[0, n + slot] * shard, shard)] = nt(grads_ref[...], weights[slot][...])
    value = wide(tokens_ref[...])
    inverse = lax.rsqrt(jnp.mean(value * value, axis=1, keepdims=True) + EPS)
    normed = value * inverse
    scaled = sum_ref[...] * gain_ref[0:1, :]
    inner = jnp.mean(scaled * normed, axis=1, keepdims=True)
    out_ref[...] = low(grad_ref[...] + inverse * (scaled - normed * inner))


def row_sums(product):
    rows, lanes = product.shape
    total = product[:, 0:128]
    for i in range(1, lanes // 128):
        total = total + product[:, i * 128 : (i + 1) * 128]
    return jnp.sum(jnp.transpose(total), axis=0, keepdims=True)


def final_kernel(n, count, factor, aligned, table, gate_up_ref, gain_two_ref, w_qkv_ref, gain_one_ref, *refs):
    pieces, others = refs[: n + 1], refs[n + 1 : 2 * n + 2]
    outs, gain_outs, whole, sem = refs[2 * n + 2 : 2 * n + 6], refs[2 * n + 6 : 2 * n + 8], refs[2 * n + 8 : -1], refs[-1]
    gu_ref, down_ref, qkv_ref, out_ref, turned_ref = whole
    hidden, width = down_ref.shape
    sub = gu_ref.shape[0] // n
    own_width = others[0].shape[1] // 4
    half = n // 2
    copies = []

    def leave(number):
        copy = pltpu.make_async_copy(whole[number], outs[number], sem.at[number])
        copy.start()
        copies.append(copy)

    def shard(parts, k):
        if k == half:
            return jnp.concatenate([wide(parts[half][...]), wide(parts[half + 1][...])], axis=0) * factor
        return wide(parts[k if k < half else k + 1][...]) * factor

    for k in range(n):
        piece = shard(pieces, k)
        start = table[0, k] * sub
        for part in range(count):
            lines = piece[part * sub : (part + 1) * sub]
            gu_ref[at(start, sub), part * hidden : (part + 1) * hidden] = lines[:, 0:hidden]
            gu_ref[at(start, sub), (count + part) * hidden : (count + part + 1) * hidden] = lines[:, hidden:]
            side, line = part // (count // 2), (count + part % (count // 2)) * sub
            turned_ref[at(part * (n * sub) + start, sub), :] = piece[line : line + sub, side * hidden : (side + 1) * hidden]
    leave(0)
    for k in range(n):
        piece = shard(others, k)
        for part in range(4):
            value = piece[:, part * own_width : (part + 1) * own_width]
            target = out_ref if part == 3 else qkv_ref
            base = 0 if part == 3 else part * width
            if aligned:
                target[:, at(base + table[0, k] * own_width, own_width)] = value
            else:
                target[:, base + k * own_width : base + (k + 1) * own_width] = value
    leave(2)
    leave(3)
    for i in range(width // 128):
        down_ref[:, i * 128 : (i + 1) * 128] = jnp.transpose(turned_ref[i * 128 : (i + 1) * 128, :])
    leave(1)
    gain_outs[0][...] = row_sums(wide(gate_up_ref[...]) * gu_ref[...]) / wide(gain_two_ref[...])
    gain_outs[1][...] = row_sums(wide(w_qkv_ref[...]) * qkv_ref[...]) / wide(gain_one_ref[...])
    for copy in copies:
        copy.wait()


def cut_kernel(n, table, own_ref, up_ref, down_ref, *refs):
    outs, rest_ref, sum_ref = refs[:-2], refs[-2], refs[-1]
    sum_ref[...] = low(wide(own_ref[...]) + wide(up_ref[...]) + wide(down_ref[...]))
    sub = outs[0].shape[0]
    for slot, out in enumerate(outs):
        out[...] = sum_ref[at(table[0, n + slot] * sub, sub), :]
    rest_ref[...] = sum_ref[len(outs) * sub :, :]


def pack_kernel(n, table, rest_ref, *refs):
    pieces, out_ref = refs[:-1], refs[-1]
    sub = pieces[0].shape[0]
    for slot, piece in enumerate(pieces):
        out_ref[at(table[0, n + slot] * sub, sub), :] = piece[...]
    out_ref[len(pieces) * sub :, :] = rest_ref[...]


def join_kernel(terms, table, *refs):
    qkv, back_ref, out_ref = refs[:terms], refs[terms], refs[-1]
    total = wide(qkv[0][...])
    for term in qkv[1:]:
        total = total + wide(term[...])
    start = total.shape[1]
    out_ref[:, 0:start] = low(total)
    shard = out_ref.shape[0]
    other = wide(back_ref[0, 0:shard, start:])
    for owner in range(1, back_ref.shape[0]):
        other = other + wide(back_ref[owner, 0:shard, start:])
    out_ref[:, start:] = low(other)


def ring_of(count):
    if count % 4 or count < 8:
        return list(range(count))
    across = count // 4
    order = []
    for along in range(4):
        columns = range(1, across) if along % 2 == 0 else range(across - 1, 0, -1)
        order += [along * across + column for column in columns]
    return order + [along * across for along in reversed(range(4))]


def ring_shift(value, ring, step):
    count = len(ring)
    return lax.ppermute(
        value, "ctx", [(ring[i], ring[(i + step) % count]) for i in range(count)]
    )


def tie(*values):
    return lax.optimization_barrier(values)


class Gather:
    def __init__(self, value, ring):
        self.ring, self.half, self.step = ring, len(ring) // 2, 1
        self.first, self.ahead, self.behind, self.far = value, [], [], None
        self.up, self.down = tie(ring_shift(value, ring, 1), ring_shift(value, ring, -1))

    def advance(self, *others):
        self.ahead.append(self.down)
        self.behind.append(self.up)
        self.up, self.down, *others = tie(self.up, self.down, *others)
        self.step += 1
        up, down = self.up, self.down
        if self.step == self.half:
            cut = up.shape[0] // 2
            up, down = up[:cut], down[cut:]
        self.up, self.down = tie(ring_shift(up, self.ring, 1), ring_shift(down, self.ring, -1))
        return others

    def slots(self):
        while self.step < self.half:
            self.advance()
        return [self.first] + self.ahead + [self.up, self.down] + self.behind[::-1]


class Scatter:
    def __init__(self, terms, ring):
        self.ring, self.half, self.terms = ring, len(ring) // 2, terms
        self.up, self.down = terms[self.half : self.half + 2]
        self.step = self.half
        self.send()

    def send(self):
        self.up, self.down = tie(ring_shift(self.up, self.ring, 1), ring_shift(self.down, self.ring, -1))

    def advance(self, *others):
        self.up, self.down, *others = tie(self.up, self.down, *others)
        up, down, cut = self.terms[self.step - 1], self.terms[len(self.ring) + 2 - self.step], self.up.shape[0]
        if self.step == self.half:
            rows = up.shape[0]
            self.up = low(wide(up) + jnp.pad(wide(self.up), ((0, rows - cut), (0, 0))))
            self.down = low(wide(down) + jnp.pad(wide(self.down), ((rows - cut, 0), (0, 0))))
        else:
            self.up, self.down = add_low(up, self.up), add_low(down, self.down)
        self.up, self.down, *others = tie(self.up, self.down, *others)
        self.step -= 1
        self.send()
        return others

    def sums(self):
        while self.step > 1:
            self.advance()
        return [self.terms[0], self.up, self.down]


def ring_exchange(slots, ring):
    count = len(ring)
    result = [slots[0]] + [None] * (count - 1)
    for k in range(1, count):
        result[count - k] = ring_shift(slots[k], ring, k)
    return result


def exchange(array):
    return lax.all_to_all(array, "ctx", 0, 0, tiled=True)


def partner(value, count):
    return lax.ppermute(value, "fsdp", [(i, i ^ 1) for i in range(count)])


def chip_shift(value, count, step):
    return lax.ppermute(value, "fsdp", [(i, (i + 2 * step) % count) for i in range(count)])


def far_gather(value, count):
    return [value] + [chip_shift(value, count, -step) for step in range(1, count // 2)]


def near_gather(nears, count):
    slots = []
    for near in nears:
        slots += [near, partner(near, count)]
    return slots


def near_scatter(terms, count):
    return [add_low(terms[i], partner(terms[i + 1], count)) for i in range(0, count, 2)]


def far_scatter(nears, count):
    return [nears[0]] + [chip_shift(nears[step], count, step) for step in range(1, count // 2)]


def side_exchange(pieces, count, slots=None):
    chips = count // 2
    received = []
    for slot in range(count) if slots is None else slots:
        step, flip = (chips - slot // 2) % chips, slot % 2
        piece = pieces[2 * step + flip]
        if step or flip:
            pairs = [(i, ((i + 2 * step) % count) ^ flip) for i in range(count)]
            piece = lax.ppermute(piece, "fsdp", pairs)
        received.append(piece)
    return received


def add_low(left, right):
    return low(wide(left) + wide(right))


def total_of(terms):
    total = wide(terms[0])
    for term in terms[1:]:
        total = total + wide(term)
    return total


def body(
    tokens, cotangent, gain_attn, w_qkv, w_out, gain_ffn, w_gate_up, w_down, lengths, block_order
):
    rows, width = tokens.shape
    heads = HEADS
    depth = width // heads
    ctx = lax.axis_size("ctx")
    fsdp = lax.axis_size("fsdp")
    factor = 1.0 / math.sqrt(rows * ctx * fsdp)
    shard = width // fsdp
    hidden = w_down.shape[0]
    own_heads = heads // ctx
    own_width = own_heads * depth
    aligned = own_width % 128 == 0
    half = ctx // 2
    sub = shard // ctx
    lines = fsdp * sub
    ring = ring_of(ctx)
    chips = fsdp // 2
    entries = []
    for c in range(ctx):
        me = ring.index(c)
        for f in range(fsdp):
            owners = [ring[(me + k) % ctx] for k in range(ctx)]
            sides = [((f // 2 + s) % chips) * 2 + ((f % 2) ^ k) for s in range(chips) for k in (0, 1)]
            entries.append(owners + sides)
    device = lax.axis_index("ctx") * fsdp + lax.axis_index("fsdp")
    table = lax.dynamic_slice_in_dim(jnp.asarray(entries, jnp.int32), device, 1, 0)
    gain_one, gain_two = gain_attn.reshape(1, shard), gain_ffn.reshape(1, shard)
    f32 = jnp.float32
    gain_scratch = pltpu.VMEM((8, width), f32)
    square_scratch = pltpu.VMEM((width, width), jnp.bfloat16)

    going = Gather(tokens, ring)
    if aligned:
        (piece,) = call(
            "slice", functools.partial(slice_kernel, own_width),
            [shape((shard + 8, 3 * own_width))], [table, w_qkv, gain_one, gain_two],
            time=2.2,
        )
    else:
        mine = [
            lax.dynamic_slice(w_qkv, (0, part * width + table[0, 0] * own_width), (shard, own_width))
            for part in range(3)
        ]
        piece = jnp.concatenate(
            [jnp.concatenate(mine, axis=1), gain_rows(wide(gain_one), wide(gain_two), 3 * own_width)], axis=0
        )
    slices = far_gather(piece, fsdp)
    gate_pieces = call(
        "split", functools.partial(split_kernel, ctx),
        [shape((shard, 2 * hidden))] * fsdp, [table, w_gate_up],
        scratch=[pltpu.VMEM((fsdp, shard, 2 * hidden), jnp.bfloat16)],
        time=4,
    )
    sent = gate_pieces
    gate_pieces = [sent[0]] + side_exchange(sent, fsdp, range(1, 3)) + [None] * (fsdp - 3)
    slices, sent = going.advance(slices, sent)
    slices = near_gather(slices, fsdp)

    def project(slot):
        return call(
            "project", functools.partial(project_kernel, ctx),
            [shape(slot.shape), shape((slot.shape[0], 3 * own_width))], [table, slot] + slices,
            scratch=[gain_scratch, pltpu.VMEM((width, 3 * own_width), jnp.bfloat16)],
            time=2.6,
        )

    first = project(tokens)
    ahead, behind = [project(going.ahead[0])], [project(going.behind[0])]
    first, ahead[0], behind[0], gate_pieces[1:3] = going.advance(first, ahead[0], behind[0], gate_pieces[1:3])
    for step in range(1, half - 1):
        ahead.append(project(going.ahead[step]))
        behind.append(project(going.behind[step]))
        if step == 1:
            sent, unused = tie(sent, gate_pieces[1:3])
            gate_pieces[3:] = side_exchange(sent, fsdp, range(3, fsdp))
        if going.step < half:
            ahead[step], behind[step] = going.advance(ahead[step], behind[step])
    *far, ahead, behind, gate_pieces[3:] = tie(going.up, going.down, ahead, behind, gate_pieces[3:])
    far = [project(value) for value in far]
    later_out, far = tie(w_out, far)
    outs = far_gather(later_out, fsdp)
    pairs = [first] + ahead + far + behind[::-1]
    attn_slots, qkv = [pair[0] for pair in pairs], [pair[1] for pair in pairs]

    out_slots, out_t, log_total = attention_forward(
        table, lengths, block_order, qkv, ctx, own_heads, depth, TILE
    )
    out_slots, outs, gate_pieces = tie(out_slots, outs, gate_pieces)
    later_cot, out_slots = tie(cotangent, out_slots)
    cots = far_gather(later_cot, fsdp)
    attn_parts = ring_exchange(out_slots, ring)
    outs = near_gather(outs, fsdp)
    attn_parts, outs, cots = tie(attn_parts, outs, cots)
    cots = near_gather(cots, fsdp)
    resid, ffn_in = call(
        "leave", functools.partial(leave_kernel, ctx, fsdp),
        [shape((rows, width), f32), shape((rows, width))],
        [table, tokens] + attn_parts + outs + slices,
        scratch=[gain_scratch, square_scratch],
        time=4.1,
    )

    nears = far_gather(ffn_in, fsdp)
    ffns, grad_terms, out_terms, hiddens, grads = [], [], [], [], []
    for chip in range(chips):
        ffn_pair = [nears[chip], partner(nears[chip], fsdp)]
        result = call(
            "feed_forward", functools.partial(ffn_kernel, ctx, fsdp, 2),
            [shape((rows, width))] * 4 + [shape((2 * rows, hidden)), shape((2 * rows, 2 * hidden))],
            [table] + ffn_pair + cots[2 * chip : 2 * chip + 2] + gate_pieces + [w_down],
            scratch=[pltpu.VMEM((width, hidden), jnp.bfloat16)] * 2,
            time=9.5,
        )
        if chip == 0:
            result, nears[1:] = tie(result, nears[1:])
        ffns += ffn_pair
        grad_terms += result[0:2]
        out_terms += result[2:4]
        hiddens.append(result[4])
        grads.append(result[5])
    grad_nears = near_scatter(grad_terms, fsdp)
    hiddens, grad_nears = tie(hiddens, grad_nears)
    grad_parts = far_scatter(grad_nears, fsdp)
    terms_ffn = call(
        "feed_forward_weights", functools.partial(ffn_weight_kernel, ctx, fsdp),
        [shape((lines + lines // 2, 2 * hidden))] * half
        + [shape(((lines + lines // 2) // 2, 2 * hidden))] * 2
        + [shape((lines + lines // 2, 2 * hidden))] * (half - 1),
        [table] + ffns + cots + hiddens + grads,
        scratch=[pltpu.VMEM((shard, 2 * hidden), jnp.bfloat16), pltpu.VMEM((shard, hidden), jnp.bfloat16)],
        time=12,
    )
    grad_parts, unused = tie(grad_parts, terms_ffn[0])
    ffn_sums = Scatter(terms_ffn, ring)
    grad_resid, branch, *grad_attn = call(
        "branch", functools.partial(branch_kernel, ctx, fsdp, len(grad_parts)),
        [shape((rows, width), f32), shape((rows, width))] + [shape((rows, own_width))] * ctx,
        [table, resid, cotangent] + grad_parts + outs + slices,
        scratch=[gain_scratch, square_scratch],
        time=5,
    )
    grad_attn, branch, ffn_sums.up, ffn_sums.down = tie(grad_attn, branch, ffn_sums.up, ffn_sums.down)
    grad_slots = ring_exchange(grad_attn, ring)
    out_sides = call(
        "out_weights", functools.partial(out_weight_kernel, ctx, fsdp),
        [shape((ctx, shard, own_width))] * fsdp, [table, branch] + attn_parts,
        scratch=[square_scratch],
        time=3.3,
    )
    out_nears = near_scatter(out_sides, fsdp)

    out_parts = far_scatter(out_nears, fsdp)
    part_out = low(total_of(out_parts))
    grad_slots, part_out = ffn_sums.advance(grad_slots, part_out)
    grad_qkv = attention_backward(
        table, lengths, block_order, qkv, grad_slots, part_out, out_t, log_total, own_heads, depth, TILE
    )
    (grad_qkv,) = ffn_sums.advance(grad_qkv)
    qkv_sides = call(
        "qkv_weights", functools.partial(qkv_weight_kernel, len(attn_slots), ctx, fsdp),
        [shape((shard, 3 * own_width))] * fsdp, [table] + attn_slots + [grad_qkv],
        time=6,
    )
    if ffn_sums.step > 1:
        grad_qkv, qkv_sides = ffn_sums.advance(grad_qkv, qkv_sides)
    grad_back = exchange(grad_qkv)
    later_qkv, unused = tie(w_qkv, qkv_sides[0])
    qkv_nears = far_gather(later_qkv, fsdp)
    qkv_sum = far_scatter(near_scatter(qkv_sides, fsdp), fsdp)

    qkv_sum = ffn_sums.advance(qkv_sum)[0] if ffn_sums.step > 1 else qkv_sum
    own_sum, ffn_up, ffn_down = ffn_sums.sums()
    *gate_sides, rest = call(
        "cut", functools.partial(cut_kernel, ctx),
        [shape((sub, 2 * hidden))] * fsdp + [shape((lines // 2, 2 * hidden))],
        [table, own_sum, ffn_up, ffn_down],
        scratch=[pltpu.VMEM((lines + lines // 2, 2 * hidden), jnp.bfloat16)],
        time=3,
    )
    (joined,) = call(
        "join", functools.partial(join_kernel, len(qkv_sum)),
        [shape((shard, 4 * own_width))], [table] + qkv_sum + [grad_back],
        time=2.5,
    )
    gate_sides = side_exchange(gate_sides, fsdp)
    gate_sides, joined = tie(gate_sides, joined)
    (packed,) = call(
        "pack", functools.partial(pack_kernel, ctx),
        [shape((lines + lines // 2, 2 * hidden))], [table, rest] + gate_sides,
        time=2,
    )
    ffn_going = Gather(packed, ring)
    attn_going = Gather(joined, ring)
    weights = near_gather(qkv_nears, fsdp)
    (grad_tokens,) = call(
        "tail", functools.partial(tail_kernel, ctx, fsdp),
        [shape((rows, width))], [table, tokens, grad_resid, grad_back] + weights + slices,
        scratch=[gain_scratch, pltpu.VMEM((rows, width), f32), pltpu.VMEM((rows, 3 * width), jnp.bfloat16)],
        time=8,
    )
    ffn_going.advance()
    (grad_tokens,) = ffn_going.advance(grad_tokens)
    results = [
        shape((shard, 2 * hidden * fsdp), f32), shape((hidden, width), f32),
        shape((shard, 3 * width), f32), shape((shard, width), f32),
    ]
    inputs = [table, w_gate_up, gain_two, w_qkv if aligned else unmixed(relative(w_qkv, table, ctx), ctx, own_width), gain_one]
    inputs += ffn_going.slots() + attn_going.slots()
    scratch = [pltpu.VMEM(x.shape, f32) for x in results] + [pltpu.VMEM((width, hidden), f32)]
    *results, grad_gain_ffn, grad_gain_attn = pl.pallas_call(
        functools.partial(final_kernel, ctx, fsdp, factor, aligned),
        out_shape=results + [shape((1, shard), f32)] * 2,
        in_specs=[SM] + [VM] * (len(inputs) - 1),
        out_specs=[pl.BlockSpec(memory_space=pltpu.HBM)] * 4 + [VM] * 2,
        scratch_shapes=scratch + [pltpu.SemaphoreType.DMA((4,))],
        compiler_params=room(inputs[1:] + scratch, 8),
        cost_estimate=cost(6),
        name="final",
    )(*inputs)
    grad_w_gate_up, grad_w_down, grad_w_qkv, grad_w_out = results
    if not aligned:
        grad_w_qkv, grad_w_out = ordered(grad_w_qkv, table, 3, ctx), ordered(grad_w_out, table, 1, ctx)
    output = low(resid + total_of(far_scatter(near_scatter(out_terms, fsdp), fsdp)))
    return (
        output,
        grad_tokens,
        grad_gain_attn.reshape(shard),
        grad_w_qkv,
        grad_w_out,
        grad_gain_ffn.reshape(shard),
        grad_w_gate_up,
        grad_w_down,
    )


def relative(weight, table, ctx):
    rows = weight.shape[0]
    parts = weight.reshape(rows, 3, ctx, -1)
    slots = [lax.dynamic_index_in_dim(parts, table[0, k], 2, keepdims=False) for k in range(ctx)]
    return jnp.concatenate([slot.reshape(rows, -1) for slot in slots], axis=1)


def unmixed(weight, ctx, own_width):
    rows = weight.shape[0]
    return weight.reshape(rows, ctx, 3, own_width).transpose(0, 2, 1, 3).reshape(rows, -1)


def ordered(array, table, parts, ctx):
    rows = array.shape[0]
    split = array.reshape(rows, parts, ctx, -1)
    result = jnp.zeros_like(split)
    for k in range(ctx):
        result = lax.dynamic_update_slice(result, split[:, :, k : k + 1], (0, 0, table[0, k], 0))
    return result.reshape(rows, -1)


def solution(mesh):
    in_specs = (
        P(("fsdp", "ctx"), None),
        P(("fsdp", "ctx"), None),
        P("fsdp"),
        P("fsdp", None),
        P("fsdp", None),
        P("fsdp"),
        P("fsdp", None),
        P("fsdp", None),
        P("fsdp", None),
        P("fsdp", None),
    )
    out_specs = (
        P(("fsdp", "ctx"), None),
        P(("fsdp", "ctx"), None),
        P("fsdp"),
        P("fsdp", None),
        P("fsdp", None),
        P("fsdp"),
        P("fsdp", None),
        P("fsdp", None),
    )
    return jax.shard_map(body, mesh=mesh, in_specs=in_specs, out_specs=out_specs, check_vma=False)
```

```python
import functools
import math

import jax
import jax.numpy as jnp
from jax import lax
from jax.experimental import pallas as pl
from jax.experimental.pallas import tpu as pltpu
from jax.sharding import PartitionSpec as P

HEADS = 16
TILE = 256
VMEM_FWD = 26 << 20
VMEM_BWD = 34 << 20


EPS = 1e-05
MASKED=-1e30
def nt(a,b): return lax.dot_general(a,b,(((1,),(1,)),((),())),preferred_element_type=jnp.float32)
def nn(a,b): return lax.dot_general(a,b,(((1,),(0,)),((),())),preferred_element_type=jnp.float32)

def ends_of(lengths_ref):
    ends = [lengths_ref[0, 0]]
    for i in range(1, lengths_ref.shape[1]):
        ends.append(ends[-1] + lengths_ref[0, i])
    return ends

def first_tile(ends, position, tile):
    start = jnp.int32(0)
    for end in ends[:-1]:
        start = jnp.where(end <= position, end, start)
    return start // tile

def last_tile(ends, position, tile):
    last = ends[-1]
    for end in reversed(ends[:-1]):
        last = jnp.where(end > position, end, last)
    return (last - 1) // tile

def seen(ends, query_start, key_start, queries, keys):
    pos_query = query_start + lax.broadcasted_iota(jnp.int32, (1, queries), 1)
    start = jnp.zeros((1, queries), jnp.int32)
    for end in ends[:-1]:
        start = jnp.where(pos_query >= end, end, start)
    pos_key = key_start + lax.broadcasted_iota(jnp.int32, (keys, queries), 0)
    return (pos_key <= pos_query) & (pos_key >= start)

def head_lanes(x, head, heads, depth):
    if heads == 1:
        return x
    lane = lax.broadcasted_iota(jnp.int32, x.shape, 1)
    return jnp.where((lane >= head * depth) & (lane < (head + 1) * depth), x, jnp.zeros_like(x))

def placed(slots, block, table, order_ref, per):
    number = 0
    for slot in slots:
        for row in range(0, slot.shape[0], block):
            position = order_ref[0, table[0, number // per] * per + number % per] * block
            yield slot, pl.ds(row, block), pl.ds(pl.multiple_of(position, block), block)
            number += 1

def stored(owners, block, order_ref, per):
    for owner in range(owners):
        for b in range(per):
            position = order_ref[0, owner * per + b] * block
            yield owner, pl.ds(b * block, block), pl.ds(pl.multiple_of(position, block), block)

def fwd_kernel(meta, table, lengths_ref, order_ref, *refs):
    given, n, heads, depth, tile, block = meta
    qkv_refs, out_refs = refs[:given], refs[given:given+n]
    out_t_ref, lse_ref = refs[given+n], refs[given+n+1]
    q_ref, k_ref, v_ref, o_ref = refs[given+n+2:]
    ends = ends_of(lengths_ref)
    width = heads*depth
    scale = depth ** (-0.5)
    per = out_refs[0].shape[0] // block
    for slot, src, dst in placed(qkv_refs, block, table, order_ref, per):
        q = slot[src, 0:width].astype(jnp.float32)*scale
        for h in range(heads):
            q_ref[h, dst, :] = head_lanes(q, h, heads, depth).astype(jnp.bfloat16)
        k_ref[dst, :] = slot[src, width:2*width]
        v_ref[dst, :] = slot[src, 2*width:]
    wide_tile = 2 * tile
    tiles = q_ref.shape[1] // wide_tile
    def one_query(t, _):
        rows = pl.ds(pl.multiple_of(t*wide_tile, wide_tile), wide_tile)
        qs = [q_ref[h, rows, :] for h in range(heads)]
        def one_key(j, carry):
            keys = pl.ds(pl.multiple_of(j*tile, tile), tile)
            k = k_ref[keys, :]
            v_t = jnp.transpose(v_ref[keys, :].astype(jnp.float32)).astype(jnp.bfloat16)
            mask = seen(ends, t*wide_tile, j*tile, wide_tile, tile)
            new = []
            for h in range(heads):
                m, l, acc = carry[h]
                s = jnp.where(mask, nt(k, qs[h]), MASKED)
                m_new = jnp.maximum(m, jnp.max(s, axis=0, keepdims=True))
                e = jnp.exp(s - m_new)
                alpha = jnp.exp(m - m_new)
                l = l*alpha + jnp.sum(e, axis=0, keepdims=True)
                acc = acc*alpha + nn(v_t[h*depth:(h+1)*depth], e.astype(jnp.bfloat16))
                new.append((m_new, l, acc))
            return tuple(new)
        init = tuple((jnp.full((1,wide_tile),MASKED,jnp.float32), jnp.zeros((1,wide_tile),jnp.float32), jnp.zeros((depth,wide_tile),jnp.float32)) for _ in range(heads))
        final = lax.fori_loop(first_tile(ends, t*wide_tile, tile), 2*t+2, one_key, init)
        outs = []
        for h in range(heads):
            m, l, acc = final[h]
            outs.append(acc / l)
            lse_ref[h:h+1, rows] = m + jnp.log(l)
        out_t = jnp.concatenate(outs, axis=0) if heads > 1 else outs[0]
        out_t_ref[:, rows] = out_t
        o_ref[rows, :] = jnp.transpose(out_t).astype(jnp.bfloat16)
        return 0
    lax.fori_loop(0, tiles, one_query, 0)
    for slot, dst, src in placed(out_refs, block, table, order_ref, per):
        slot[dst, :] = o_ref[src, :]

def bwd_kernel(meta, table, lengths_ref, order_ref, *refs):
    given, n, heads, depth, tile, block = meta
    qkv_refs, grad_refs = refs[:given], refs[given:given+n]
    refs = refs[n:]
    part_out_ref, out_t_ref, lse_ref, dqkv_ref = refs[given:given+4]
    ends = ends_of(lengths_ref)
    q_ref, k_ref, v_ref, g_ref, k_t_ref, delta_ref, dq_t_ref, dq_ref, dk_ref, dv_ref = refs[given+4:]
    width = heads*depth
    scale = depth ** (-0.5)
    per = dqkv_ref.shape[1] // block
    total = k_ref.shape[0]
    for slot, src, dst in placed(qkv_refs, block, table, order_ref, per):
        q = slot[src, 0:width].astype(jnp.float32)*scale
        for h in range(heads):
            q_ref[h, dst, :] = head_lanes(q, h, heads, depth).astype(jnp.bfloat16)
        k_ref[dst, :] = slot[src, width:2*width]
        v_ref[dst, :] = slot[src, 2*width:]
    for slot, src, dst in placed(grad_refs, block, table, order_ref, per):
        g = slot[src, :].astype(jnp.float32)
        for h in range(heads):
            g_ref[h, dst, :] = head_lanes(g, h, heads, depth).astype(jnp.bfloat16)
    tiles = total // tile
    def prepare(t, _):
        rows = pl.ds(pl.multiple_of(t*tile, tile), tile)
        k_t_ref[:, rows] = jnp.transpose(k_ref[rows, :].astype(jnp.float32)).astype(jnp.bfloat16)
        g = g_ref[0, rows, :].astype(jnp.float32)
        for h in range(1, heads):
            g = g + g_ref[h, rows, :].astype(jnp.float32)
        prod = jnp.transpose(g) * out_t_ref[:, rows]
        for h in range(heads):
            delta_ref[h:h+1, rows] = jnp.sum(prod[h*depth:(h+1)*depth], axis=0, keepdims=True)
        dq_t_ref[:, rows] = jnp.zeros((width, tile), jnp.float32)
        return 0
    lax.fori_loop(0, tiles, prepare, 0)
    wide_tile = 2 * tile
    def one_key(j, _):
        keys = pl.ds(pl.multiple_of(j*tile, tile), tile)
        k = k_ref[keys, :]
        v = v_ref[keys, :]
        k_t = k_t_ref[:, keys]
        dk_ref[keys, :] = jnp.zeros((tile, width), jnp.float32)
        dv_ref[keys, :] = jnp.zeros((tile, width), jnp.float32)
        def one_query(t, _):
            rows = pl.ds(pl.multiple_of(t*wide_tile, wide_tile), wide_tile)
            mask = seen(ends, t*wide_tile, j*tile, wide_tile, tile)
            dk = dk_ref[keys, :]
            dv = dv_ref[keys, :]
            for h in range(heads):
                q = q_ref[h, rows, :]
                g = g_ref[h, rows, :]
                s = nt(k, q)
                p = jnp.where(mask, jnp.exp(s - lse_ref[h:h+1, rows]), 0.0)
                dp = nt(v, g)
                ds = (p*(dp - delta_ref[h:h+1, rows])).astype(jnp.bfloat16)
                dv = dv + nn(p.astype(jnp.bfloat16), g)
                dk = dk + nn(ds, q)
                part = pl.ds(h*depth, depth)
                dq_t_ref[part, rows] = dq_t_ref[part, rows] + nn(k_t[h*depth:(h+1)*depth], ds)
            dk_ref[keys, :] = dk
            dv_ref[keys, :] = dv
            return 0
        lax.fori_loop(j//2, last_tile(ends, j*tile + tile - 1, wide_tile) + 1, one_query, 0)
        return 0
    lax.fori_loop(0, tiles, one_key, 0)
    def finish(t, _):
        rows = pl.ds(pl.multiple_of(t*tile, tile), tile)
        dq_ref[rows, :] = (jnp.transpose(dq_t_ref[:, rows])*scale).astype(jnp.bfloat16)
        return 0
    lax.fori_loop(0, tiles, finish, 0)
    for owner, dst, src in stored(n, block, order_ref, per):
        dqkv_ref[owner, dst, 0:width] = dq_ref[src, :]
        dqkv_ref[owner, dst, width:2*width] = dk_ref[src, :].astype(jnp.bfloat16)
        dqkv_ref[owner, dst, 2*width:3*width] = dv_ref[src, :].astype(jnp.bfloat16)
    shard = part_out_ref.shape[1]
    rows = dqkv_ref.shape[1]
    for owner in range(n):
        dqkv_ref[owner, 0:shard, 3*width:] = part_out_ref[owner]
        if shard < rows:
            dqkv_ref[owner, shard:, 3*width:] = jnp.zeros((rows-shard, width), jnp.bfloat16)

SM=pl.BlockSpec(memory_space=pltpu.SMEM)
VM=pl.BlockSpec(memory_space=pltpu.VMEM)
def attention_forward(table, lengths, order, qkv, n, heads, depth, tile):
    total=sum(x.shape[0] for x in qkv); rows=total//n; width=heads*depth
    block=total//order.shape[1]
    meta=(len(qkv),n,heads,depth,tile,block)
    res=pl.pallas_call(functools.partial(fwd_kernel,meta),
        out_shape=[jax.ShapeDtypeStruct((rows,width),jnp.bfloat16)]*n+[jax.ShapeDtypeStruct((width,total),jnp.float32),jax.ShapeDtypeStruct((heads,total),jnp.float32)],
        in_specs=[SM,SM,SM]+[VM]*len(qkv), out_specs=[VM]*(n+2),
        scratch_shapes=[pltpu.VMEM((heads,total,width),jnp.bfloat16)]+[pltpu.VMEM((total,width),jnp.bfloat16)]*3,
        cost_estimate=cost(17),
        compiler_params=pltpu.CompilerParams(vmem_limit_bytes=VMEM_FWD),
        name="attention_forward")(table,lengths,order,*qkv)
    return list(res[:n]),res[n],res[n+1]
def attention_backward(table, lengths, order, qkv, grads, part_out, out_t, lse, heads, depth, tile):
    n=len(grads); rows=grads[0].shape[0]; total=n*rows; width=heads*depth
    block=total//order.shape[1]
    meta=(len(qkv),n,heads,depth,tile,block)
    f32=jnp.float32; b16=jnp.bfloat16
    return pl.pallas_call(functools.partial(bwd_kernel,meta),
        out_shape=jax.ShapeDtypeStruct((n,rows,4*width),b16),
        in_specs=[SM,SM,SM]+[VM]*(len(qkv)+n+3), out_specs=VM,
        scratch_shapes=[pltpu.VMEM((heads,total,width),b16),pltpu.VMEM((total,width),b16),pltpu.VMEM((total,width),b16),pltpu.VMEM((heads,total,width),b16),
          pltpu.VMEM((width,total),b16),pltpu.VMEM((heads,total),f32),pltpu.VMEM((width,total),f32),pltpu.VMEM((total,width),b16),pltpu.VMEM((total,width),f32),pltpu.VMEM((total,width),f32)],
        cost_estimate=cost(18),
        compiler_params=pltpu.CompilerParams(vmem_limit_bytes=VMEM_BWD),
        name="attention_backward")(table,lengths,order,*qkv,*grads,part_out,out_t,lse)


def tn(left, right):
    return lax.dot_general(left, right, (((0,), (0,)), ((), ())), preferred_element_type=jnp.float32)


def low(value):
    return value.astype(jnp.bfloat16)


def wide(value):
    return value.astype(jnp.float32)


def at(start, size):
    return pl.ds(pl.multiple_of(start, size), size)


def cost(microseconds):
    return pl.CostEstimate(flops=0, bytes_accessed=int(microseconds * 3.4e6), transcendentals=0)


def room(arrays, extra):
    total = 0
    for array in arrays:
        dims = [1, 1] + list(array.shape)
        rows, lanes = -(-dims[-2] // 16) * 16, -(-dims[-1] // 128) * 128
        total += math.prod(dims[:-2]) * rows * lanes * jnp.dtype(array.dtype).itemsize
    return pltpu.CompilerParams(vmem_limit_bytes=min(60 << 20, total + (extra << 20)))


def call(name, kernel, out, inputs, scratch=(), time=2.0, extra=8):
    return list(
        pl.pallas_call(
            kernel,
            out_shape=list(out),
            in_specs=[SM] + [VM] * (len(inputs) - 1),
            out_specs=[VM] * len(out),
            scratch_shapes=list(scratch),
            cost_estimate=cost(time),
            compiler_params=room(list(inputs[1:]) + list(out) + list(scratch), extra),
            name=name,
        )(*inputs)
    )


def shape(dims, dtype=jnp.bfloat16):
    return jax.ShapeDtypeStruct(tuple(dims), dtype)


def slice_kernel(own_width, table, w_ref, one_ref, two_ref, out_ref):
    shard, total = w_ref.shape
    for part in range(3):
        out_ref[0:shard, part * own_width : (part + 1) * own_width] = w_ref[
            :, at(part * (total // 3) + table[0, 0] * own_width, own_width)
        ]
    out_ref[shard : shard + 8, :] = gain_rows(wide(one_ref[...]), wide(two_ref[...]), 3 * own_width)


def gain_rows(one, two, lanes):
    shard = one.shape[1]
    if lanes > shard:
        rest = jnp.zeros((1, lanes - shard), jnp.float32)
        one, two = jnp.concatenate([one, rest], axis=1), jnp.concatenate([two, rest], axis=1)
    number = lax.broadcasted_iota(jnp.int32, (8, lanes), 0)
    return low(jnp.where(number == 0, one, jnp.where(number == 1, two, 0.0)))


def full_gain(table, n, pieces, row, gain_ref):
    shard = gain_ref.shape[1] // len(pieces)
    for slot, piece in enumerate(pieces):
        lines = wide(piece[pl.ds(piece.shape[0] - 8, 8), 0:shard])
        gain_ref[0:1, at(table[0, n + slot] * shard, shard)] = lines[row : row + 1]


def split_kernel(n, table, w_ref, *refs):
    outs, parts_ref = refs[:-1], refs[-1]
    count = len(outs)
    hidden = w_ref.shape[1] // (2 * count)
    for part in range(count):
        parts_ref[part, :, 0:hidden] = w_ref[:, part * hidden : (part + 1) * hidden]
        parts_ref[part, :, hidden:] = w_ref[:, (count + part) * hidden : (count + part + 1) * hidden]
    for slot in range(count):
        outs[slot][...] = parts_ref[table[0, n + slot]]


def project_kernel(n, table, rows_ref, *refs):
    pieces, attn_ref, qkv_ref, gain_ref, weight_ref = refs[:-4], refs[-4], refs[-3], refs[-2], refs[-1]
    shard = rows_ref.shape[1] // len(pieces)
    full_gain(table, n, pieces, 0, gain_ref)
    for slot, piece in enumerate(pieces):
        weight_ref[at(table[0, n + slot] * shard, shard), :] = piece[pl.ds(0, shard), :]
    value = wide(rows_ref[...])
    inverse = lax.rsqrt(jnp.mean(value * value, axis=1, keepdims=True) + EPS)
    attn_in = low(value * inverse * gain_ref[0:1, :])
    attn_ref[...] = attn_in
    qkv_ref[...] = low(nn(attn_in, weight_ref[...]))


def stage_rows(table, n, pieces, weight_ref):
    shard = pieces[0].shape[0]
    for slot, piece in enumerate(pieces):
        weight_ref[at(table[0, n + slot] * shard, shard), :] = piece[...]


def leave_kernel(n, count, table, tokens_ref, *refs):
    parts, outs, slices = refs[:n], refs[n : n + count], refs[n + count : n + 2 * count]
    resid_ref, ffn_ref, gain_ref, weight_ref = refs[n + 2 * count :]
    own_width = parts[0].shape[1]
    full_gain(table, n, slices, 1, gain_ref)
    stage_rows(table, n, outs, weight_ref)
    rows = tokens_ref.shape[0]
    attn = jnp.concatenate([parts[k][...] for k in range(n)], axis=1)
    ordered = jnp.concatenate([weight_ref[at(table[0, k] * own_width, own_width), :] for k in range(n)], axis=0)
    resid = wide(tokens_ref[...]) + nn(attn, ordered)
    resid_ref[...] = resid
    inverse = lax.rsqrt(jnp.mean(resid * resid, axis=1, keepdims=True) + EPS)
    ffn_ref[...] = low(resid * inverse * gain_ref[0:1, :])


def ffn_kernel(n, count, slots, table, *refs):
    ffn, cot = refs[:slots], refs[slots : 2 * slots]
    pieces, down_ref = refs[2 * slots : 2 * slots + count], refs[2 * slots + count]
    rest = refs[2 * slots + count + 1 :]
    terms, outs, hidden_ref, grad_ref = rest[:slots], rest[slots : 2 * slots], rest[2 * slots], rest[2 * slots + 1]
    gate_ref, up_ref, values_ref, cots_ref = rest[2 * slots + 2 :]
    hidden = down_ref.shape[0]
    shard = pieces[0].shape[0]
    rows = ffn[0].shape[0]
    for slot, piece in enumerate(pieces):
        place = at(table[0, n + slot] * shard, shard)
        gate_ref[place, :] = piece[:, 0:hidden]
        up_ref[place, :] = piece[:, hidden:]
    for slot in range(slots):
        values_ref[slot] = ffn[slot][...]
        cots_ref[slot] = cot[slot][...]

    def one(number, unused):
        value = values_ref[number]
        gate = nn(value, gate_ref[...])
        upward = nn(value, up_ref[...])
        grad_hidden = nt(cots_ref[number], down_ref[...])
        sigma = jax.nn.sigmoid(gate)
        active = gate * sigma
        hidden_low = low(active * upward)
        grad_gate = low(grad_hidden * upward * (sigma + active * (1.0 - sigma)))
        grad_up = low(grad_hidden * active)
        place = at(number * rows, rows)
        hidden_ref[place, :] = hidden_low
        grad_ref[place, 0:hidden] = grad_gate
        grad_ref[place, hidden:] = grad_up
        values_ref[number] = low(nt(grad_gate, gate_ref[...]) + nt(grad_up, up_ref[...]))
        cots_ref[number] = low(nn(hidden_low, down_ref[...]))
        return 0

    lax.fori_loop(0, slots, one, 0)
    for slot in range(slots):
        terms[slot][...] = values_ref[slot]
        outs[slot][...] = cots_ref[slot]


def ffn_weight_kernel(n, count, table, *refs):
    ffn, cot, rest = refs[:count], refs[count : 2 * count], refs[2 * count :]
    hiddens, grads, rest = rest[: count // 2], rest[count // 2 : count], rest[count:]
    outs, (value_ref, turned_ref) = rest[:-2], rest[-2:]
    hidden = hiddens[0].shape[1]
    half = n // 2
    shard = ffn[0].shape[1] // count
    sub = shard // n
    lines = count * sub
    cut = outs[half].shape[0]
    hidden_all = jnp.concatenate([r[...] for r in hiddens], axis=0)
    grad_all = jnp.concatenate([r[...] for r in grads], axis=0)

    def one(f, unused):
        lanes = at(f * shard, shard)
        ffn_all = jnp.concatenate([r[:, lanes] for r in ffn], axis=0)
        value_ref[f] = low(tn(ffn_all, grad_all))
        cot_all = jnp.concatenate([r[:, lanes] for r in cot], axis=0)
        turned_ref[f] = low(tn(cot_all, hidden_all))
        return 0

    lax.fori_loop(0, count, one, 0)

    def store(slot, row, lanes, value):
        if slot != half:
            outs[slot if slot < half else slot + 1][row : row + sub, lanes] = value
        elif row < cut:
            outs[half][row : row + sub, lanes] = value
        else:
            outs[half + 1][row - cut : row - cut + sub, lanes] = value

    for f in range(count):
        side, line = f // (count // 2), lines + (f % (count // 2)) * sub
        for slot in range(n):
            mine = at(table[0, slot] * sub, sub)
            store(slot, f * sub, slice(0, 2 * hidden), value_ref[f, mine, :])
            store(slot, line, slice(side * hidden, (side + 1) * hidden), turned_ref[f, mine, :])


def branch_kernel(n, count, got, table, resid_ref, cot_ref, *refs):
    terms, outs, slices = refs[:got], refs[got : got + count], refs[got + count : got + 2 * count]
    rest = refs[got + 2 * count :]
    grad_ref, branch_ref, parts = rest[0], rest[1], rest[2 : 2 + n]
    gain_ref, weight_ref = rest[2 + n :]
    own_width = parts[0].shape[1]
    full_gain(table, n, slices, 1, gain_ref)
    stage_rows(table, n, outs, weight_ref)
    resid = resid_ref[...]
    inverse = lax.rsqrt(jnp.mean(resid * resid, axis=1, keepdims=True) + EPS)
    normed = resid * inverse
    grad = wide(terms[0][...])
    for term in terms[1:]:
        grad = grad + wide(term[...])
    scaled = grad * gain_ref[0:1, :]
    inner = jnp.mean(scaled * normed, axis=1, keepdims=True)
    grad_resid = wide(cot_ref[...]) + inverse * (scaled - normed * inner)
    grad_ref[...] = grad_resid
    branch = low(grad_resid)
    branch_ref[...] = branch
    for k in range(n):
        parts[k][...] = low(nt(branch, weight_ref[at(table[0, k] * own_width, own_width), :]))


def out_weight_kernel(n, count, table, branch_ref, *refs):
    parts, outs, whole_ref = refs[:n], refs[n : n + count], refs[-1]
    own_width = parts[0].shape[1]
    shard = outs[0].shape[1]
    branch = branch_ref[...]
    for k in range(n):
        whole_ref[at(table[0, k] * own_width, own_width), :] = low(tn(parts[k][...], branch))
    for slot in range(count):
        lines = whole_ref[at(table[0, n + slot] * shard, shard), :]
        for owner in range(n):
            outs[slot][owner] = lines[:, owner * own_width : (owner + 1) * own_width]


def qkv_weight_kernel(given, n, count, table, *refs):
    attn, grads_ref, outs, whole_ref = refs[:given], refs[given], refs[given + 1 : -1], refs[-1]
    shard = outs[0].shape[0]
    used = outs[0].shape[1]
    grad_all = jnp.concatenate([grads_ref[table[0, k], :, 0:used] for k in range(n)], axis=0)

    def one(f, unused):
        attn_all = jnp.concatenate([r[:, at(f * shard, shard)] for r in attn], axis=0)
        whole_ref[f] = low(tn(attn_all, grad_all))
        return 0

    lax.fori_loop(0, count, one, 0)
    for slot in range(count):
        outs[slot][...] = whole_ref[table[0, n + slot]]


def tail_kernel(n, count, table, tokens_ref, grad_ref, parts_ref, *refs):
    weights, slices = refs[:count], refs[count : 2 * count]
    out_ref, gain_ref, sum_ref, grads_ref = refs[2 * count :]
    own_width = parts_ref.shape[2] // 4
    width = tokens_ref.shape[1]
    shard = width // count
    full_gain(table, n, slices, 0, gain_ref)
    for owner in range(n):
        for part in range(3):
            start = part * width + owner * own_width
            grads_ref[:, start : start + own_width] = parts_ref[owner, :, part * own_width : (part + 1) * own_width]
    sum_ref[...] = jnp.zeros_like(sum_ref)

    def one(part, unused):
        lanes = at(part * width, width)
        for slot in range(count):
            place = at(table[0, n + slot] * shard, shard)
            sum_ref[:, place] += nt(grads_ref[:, lanes], weights[slot][:, lanes])
        return 0

    lax.fori_loop(0, 3, one, 0)
    value = wide(tokens_ref[...])
    inverse = lax.rsqrt(jnp.mean(value * value, axis=1, keepdims=True) + EPS)
    normed = value * inverse
    scaled = sum_ref[...] * gain_ref[0:1, :]
    inner = jnp.mean(scaled * normed, axis=1, keepdims=True)
    out_ref[...] = low(grad_ref[...] + inverse * (scaled - normed * inner))


def row_sums(product):
    rows, lanes = product.shape
    total = product[:, 0:128]
    for i in range(1, lanes // 128):
        total = total + product[:, i * 128 : (i + 1) * 128]
    return jnp.sum(jnp.transpose(total), axis=0, keepdims=True)


def final_kernel(n, count, factor, aligned, table, gate_up_ref, gain_two_ref, w_qkv_ref, gain_one_ref, *refs):
    pieces, others = refs[: n + 1], refs[n + 1 : 2 * n + 2]
    outs, gain_outs, whole, sem = refs[2 * n + 2 : 2 * n + 6], refs[2 * n + 6 : 2 * n + 8], refs[2 * n + 8 : -1], refs[-1]
    gu_ref, down_ref, qkv_ref, out_ref, turned_ref, pieces_ref, others_ref = whole
    hidden, width = down_ref.shape
    sub = gu_ref.shape[0] // n
    own_width = others[0].shape[1] // 4
    half = n // 2
    copies = []

    def leave(number):
        copy = pltpu.make_async_copy(whole[number], outs[number], sem.at[number])
        copy.start()
        copies.append(copy)

    def stack(parts, whole_ref):
        for number, part in enumerate(parts):
            k = number if number <= half else number - 1
            row = parts[half].shape[0] if number == half + 1 else 0
            whole_ref[k, row : row + part.shape[0], :] = part[...]

    stack(pieces, pieces_ref)
    stack(others, others_ref)

    def one(k, unused):
        start = table[0, k] * sub
        for part in range(count):
            lines = wide(pieces_ref[k, part * sub : (part + 1) * sub, :]) * factor
            gu_ref[at(start, sub), part * hidden : (part + 1) * hidden] = lines[:, 0:hidden]
            gu_ref[at(start, sub), (count + part) * hidden : (count + part + 1) * hidden] = lines[:, hidden:]
            side, line = part // (count // 2), (count + part % (count // 2)) * sub
            turned = wide(pieces_ref[k, line : line + sub, :])[:, side * hidden : (side + 1) * hidden] * factor
            turned_ref[at(part * (n * sub) + start, sub), :] = turned
        return 0

    lax.fori_loop(0, n, one, 0)
    leave(0)

    def other(k, owner):
        for part in range(4):
            value = wide(others_ref[k, :, part * own_width : (part + 1) * own_width]) * factor
            target = out_ref if part == 3 else qkv_ref
            base = 0 if part == 3 else part * width
            if aligned:
                target[:, at(base + owner * own_width, own_width)] = value
            else:
                target[:, base + k * own_width : base + (k + 1) * own_width] = value
        return 0

    if aligned:
        lax.fori_loop(0, n, lambda k, unused: other(k, table[0, k]), 0)
    else:
        for k in range(n):
            other(k, None)
    leave(2)
    leave(3)
    for i in range(width // 128):
        down_ref[:, i * 128 : (i + 1) * 128] = jnp.transpose(turned_ref[i * 128 : (i + 1) * 128, :])
    leave(1)
    gain_outs[0][...] = row_sums(wide(gate_up_ref[...]) * gu_ref[...]) / wide(gain_two_ref[...])
    gain_outs[1][...] = row_sums(wide(w_qkv_ref[...]) * qkv_ref[...]) / wide(gain_one_ref[...])
    for copy in copies:
        copy.wait()


def cut_kernel(n, table, own_ref, up_ref, down_ref, *refs):
    outs, rest_ref, sum_ref = refs[:-2], refs[-2], refs[-1]
    sum_ref[...] = low(wide(own_ref[...]) + wide(up_ref[...]) + wide(down_ref[...]))
    sub = outs[0].shape[0]
    for slot, out in enumerate(outs):
        out[...] = sum_ref[at(table[0, n + slot] * sub, sub), :]
    rest_ref[...] = sum_ref[len(outs) * sub :, :]


def pack_kernel(n, table, rest_ref, *refs):
    pieces, out_ref = refs[:-1], refs[-1]
    sub = pieces[0].shape[0]
    for slot, piece in enumerate(pieces):
        out_ref[at(table[0, n + slot] * sub, sub), :] = piece[...]
    out_ref[len(pieces) * sub :, :] = rest_ref[...]


def join_kernel(terms, table, *refs):
    qkv, back_ref, out_ref = refs[:terms], refs[terms], refs[-1]
    total = wide(qkv[0][...])
    for term in qkv[1:]:
        total = total + wide(term[...])
    start = total.shape[1]
    out_ref[:, 0:start] = low(total)
    shard = out_ref.shape[0]
    other = wide(back_ref[0, 0:shard, start:])
    for owner in range(1, back_ref.shape[0]):
        other = other + wide(back_ref[owner, 0:shard, start:])
    out_ref[:, start:] = low(other)


def ring_of(count):
    if count % 4 or count < 8:
        return list(range(count))
    across = count // 4
    order = []
    for along in range(4):
        columns = range(1, across) if along % 2 == 0 else range(across - 1, 0, -1)
        order += [along * across + column for column in columns]
    return order + [along * across for along in reversed(range(4))]


def ring_shift(value, ring, step):
    count = len(ring)
    return lax.ppermute(
        value, "ctx", [(ring[i], ring[(i + step) % count]) for i in range(count)]
    )


def tie(*values):
    return lax.optimization_barrier(values)


class Gather:
    def __init__(self, value, ring):
        self.ring, self.half, self.step = ring, len(ring) // 2, 1
        self.first, self.ahead, self.behind, self.far = value, [], [], None
        self.up, self.down = tie(ring_shift(value, ring, 1), ring_shift(value, ring, -1))

    def advance(self, *others):
        self.ahead.append(self.down)
        self.behind.append(self.up)
        self.up, self.down, *others = tie(self.up, self.down, *others)
        self.step += 1
        up, down = self.up, self.down
        if self.step == self.half:
            cut = up.shape[0] // 2
            up, down = up[:cut], down[cut:]
        self.up, self.down = tie(ring_shift(up, self.ring, 1), ring_shift(down, self.ring, -1))
        return others

    def slots(self):
        while self.step < self.half:
            self.advance()
        return [self.first] + self.ahead + [self.up, self.down] + self.behind[::-1]


class Scatter:
    def __init__(self, terms, ring):
        self.ring, self.half, self.terms = ring, len(ring) // 2, terms
        self.up, self.down = terms[self.half : self.half + 2]
        self.step = self.half
        self.send()

    def send(self):
        self.up, self.down = tie(ring_shift(self.up, self.ring, 1), ring_shift(self.down, self.ring, -1))

    def advance(self, *others):
        self.up, self.down, *others = tie(self.up, self.down, *others)
        up, down, cut = self.terms[self.step - 1], self.terms[len(self.ring) + 2 - self.step], self.up.shape[0]
        if self.step == self.half:
            rows = up.shape[0]
            self.up = low(wide(up) + jnp.pad(wide(self.up), ((0, rows - cut), (0, 0))))
            self.down = low(wide(down) + jnp.pad(wide(self.down), ((rows - cut, 0), (0, 0))))
        else:
            self.up, self.down = add_low(up, self.up), add_low(down, self.down)
        self.up, self.down, *others = tie(self.up, self.down, *others)
        self.step -= 1
        self.send()
        return others

    def sums(self):
        while self.step > 1:
            self.advance()
        return [self.terms[0], self.up, self.down]


def ring_exchange(slots, ring):
    count = len(ring)
    result = [slots[0]] + [None] * (count - 1)
    for k in range(1, count):
        result[count - k] = ring_shift(slots[k], ring, k)
    return result


def exchange(array):
    return lax.all_to_all(array, "ctx", 0, 0, tiled=True)


def partner(value, count):
    return lax.ppermute(value, "fsdp", [(i, i ^ 1) for i in range(count)])


def chip_shift(value, count, step):
    return lax.ppermute(value, "fsdp", [(i, (i + 2 * step) % count) for i in range(count)])


def far_gather(value, count):
    return [value] + [chip_shift(value, count, -step) for step in range(1, count // 2)]


def near_gather(nears, count):
    slots = []
    for near in nears:
        slots += [near, partner(near, count)]
    return slots


def near_scatter(terms, count):
    return [add_low(terms[i], partner(terms[i + 1], count)) for i in range(0, count, 2)]


def far_scatter(nears, count):
    return [nears[0]] + [chip_shift(nears[step], count, step) for step in range(1, count // 2)]


def side_exchange(pieces, count, slots=None):
    chips = count // 2
    received = []
    for slot in range(count) if slots is None else slots:
        step, flip = (chips - slot // 2) % chips, slot % 2
        piece = pieces[2 * step + flip]
        if step or flip:
            pairs = [(i, ((i + 2 * step) % count) ^ flip) for i in range(count)]
            piece = lax.ppermute(piece, "fsdp", pairs)
        received.append(piece)
    return received


def add_low(left, right):
    return low(wide(left) + wide(right))


def total_of(terms):
    total = wide(terms[0])
    for term in terms[1:]:
        total = total + wide(term)
    return total


def body(
    tokens, cotangent, gain_attn, w_qkv, w_out, gain_ffn, w_gate_up, w_down, lengths, block_order
):
    rows, width = tokens.shape
    heads = HEADS
    depth = width // heads
    ctx = lax.axis_size("ctx")
    fsdp = lax.axis_size("fsdp")
    factor = 1.0 / math.sqrt(rows * ctx * fsdp)
    shard = width // fsdp
    hidden = w_down.shape[0]
    own_heads = heads // ctx
    own_width = own_heads * depth
    aligned = own_width % 128 == 0
    half = ctx // 2
    sub = shard // ctx
    lines = fsdp * sub
    ring = ring_of(ctx)
    chips = fsdp // 2
    entries = []
    for c in range(ctx):
        me = ring.index(c)
        for f in range(fsdp):
            owners = [ring[(me + k) % ctx] for k in range(ctx)]
            sides = [((f // 2 + s) % chips) * 2 + ((f % 2) ^ k) for s in range(chips) for k in (0, 1)]
            entries.append(owners + sides)
    device = lax.axis_index("ctx") * fsdp + lax.axis_index("fsdp")
    table = lax.dynamic_slice_in_dim(jnp.asarray(entries, jnp.int32), device, 1, 0)
    gain_one, gain_two = gain_attn.reshape(1, shard), gain_ffn.reshape(1, shard)
    f32 = jnp.float32
    gain_scratch = pltpu.VMEM((8, width), f32)
    square_scratch = pltpu.VMEM((width, width), jnp.bfloat16)

    going = Gather(tokens, ring)
    if aligned:
        (piece,) = call(
            "slice", functools.partial(slice_kernel, own_width),
            [shape((shard + 8, 3 * own_width))], [table, w_qkv, gain_one, gain_two],
            time=2.2,
        )
    else:
        mine = [
            lax.dynamic_slice(w_qkv, (0, part * width + table[0, 0] * own_width), (shard, own_width))
            for part in range(3)
        ]
        piece = jnp.concatenate(
            [jnp.concatenate(mine, axis=1), gain_rows(wide(gain_one), wide(gain_two), 3 * own_width)], axis=0
        )
    slices = far_gather(piece, fsdp)
    gate_pieces = call(
        "split", functools.partial(split_kernel, ctx),
        [shape((shard, 2 * hidden))] * fsdp, [table, w_gate_up],
        scratch=[pltpu.VMEM((fsdp, shard, 2 * hidden), jnp.bfloat16)],
        time=4,
    )
    sent = gate_pieces
    gate_pieces = [sent[0]] + side_exchange(sent, fsdp, range(1, 3)) + [None] * (fsdp - 3)
    slices, sent = going.advance(slices, sent)
    slices = near_gather(slices, fsdp)

    def project(slot):
        return call(
            "project", functools.partial(project_kernel, ctx),
            [shape(slot.shape), shape((slot.shape[0], 3 * own_width))], [table, slot] + slices,
            scratch=[gain_scratch, pltpu.VMEM((width, 3 * own_width), jnp.bfloat16)],
            time=2.6,
        )

    first = project(tokens)
    ahead, behind = [project(going.ahead[0])], [project(going.behind[0])]
    first, ahead[0], behind[0], gate_pieces[1:3] = going.advance(first, ahead[0], behind[0], gate_pieces[1:3])
    for step in range(1, half - 1):
        ahead.append(project(going.ahead[step]))
        behind.append(project(going.behind[step]))
        if step == 1:
            sent, unused = tie(sent, gate_pieces[1:3])
            gate_pieces[3:] = side_exchange(sent, fsdp, range(3, fsdp))
        if going.step < half:
            ahead[step], behind[step] = going.advance(ahead[step], behind[step])
    *far, ahead, behind, gate_pieces[3:] = tie(going.up, going.down, ahead, behind, gate_pieces[3:])
    far = [project(value) for value in far]
    later_out, far = tie(w_out, far)
    outs = far_gather(later_out, fsdp)
    pairs = [first] + ahead + far + behind[::-1]
    attn_slots, qkv = [pair[0] for pair in pairs], [pair[1] for pair in pairs]

    out_slots, out_t, log_total = attention_forward(
        table, lengths, block_order, qkv, ctx, own_heads, depth, TILE
    )
    out_slots, outs, gate_pieces = tie(out_slots, outs, gate_pieces)
    later_cot, out_slots = tie(cotangent, out_slots)
    cots = far_gather(later_cot, fsdp)
    attn_parts = ring_exchange(out_slots, ring)
    outs = near_gather(outs, fsdp)
    attn_parts, outs, cots = tie(attn_parts, outs, cots)
    cots = near_gather(cots, fsdp)
    resid, ffn_in = call(
        "leave", functools.partial(leave_kernel, ctx, fsdp),
        [shape((rows, width), f32), shape((rows, width))],
        [table, tokens] + attn_parts + outs + slices,
        scratch=[gain_scratch, square_scratch],
        time=4.1,
    )

    nears = far_gather(ffn_in, fsdp)
    ffns, grad_terms, out_terms, hiddens, grads = [], [], [], [], []
    for chip in range(chips):
        ffn_pair = [nears[chip], partner(nears[chip], fsdp)]
        result = call(
            "feed_forward", functools.partial(ffn_kernel, ctx, fsdp, 2),
            [shape((rows, width))] * 4 + [shape((2 * rows, hidden)), shape((2 * rows, 2 * hidden))],
            [table] + ffn_pair + cots[2 * chip : 2 * chip + 2] + gate_pieces + [w_down],
            scratch=[pltpu.VMEM((width, hidden), jnp.bfloat16)] * 2 + [pltpu.VMEM((2, rows, width), jnp.bfloat16)] * 2,
            time=9.5,
        )
        if chip == 0:
            result, nears[1:] = tie(result, nears[1:])
        ffns += ffn_pair
        grad_terms += result[0:2]
        out_terms += result[2:4]
        hiddens.append(result[4])
        grads.append(result[5])
    grad_nears = near_scatter(grad_terms, fsdp)
    hiddens, grad_nears = tie(hiddens, grad_nears)
    grad_parts = far_scatter(grad_nears, fsdp)
    terms_ffn = call(
        "feed_forward_weights", functools.partial(ffn_weight_kernel, ctx, fsdp),
        [shape((lines + lines // 2, 2 * hidden))] * half
        + [shape(((lines + lines // 2) // 2, 2 * hidden))] * 2
        + [shape((lines + lines // 2, 2 * hidden))] * (half - 1),
        [table] + ffns + cots + hiddens + grads,
        scratch=[pltpu.VMEM((fsdp, shard, 2 * hidden), jnp.bfloat16), pltpu.VMEM((fsdp, shard, hidden), jnp.bfloat16)],
        time=12,
    )
    grad_parts, unused = tie(grad_parts, terms_ffn[0])
    ffn_sums = Scatter(terms_ffn, ring)
    grad_resid, branch, *grad_attn = call(
        "branch", functools.partial(branch_kernel, ctx, fsdp, len(grad_parts)),
        [shape((rows, width), f32), shape((rows, width))] + [shape((rows, own_width))] * ctx,
        [table, resid, cotangent] + grad_parts + outs + slices,
        scratch=[gain_scratch, square_scratch],
        time=5,
    )
    grad_attn, branch, ffn_sums.up, ffn_sums.down = tie(grad_attn, branch, ffn_sums.up, ffn_sums.down)
    grad_slots = ring_exchange(grad_attn, ring)
    out_sides = call(
        "out_weights", functools.partial(out_weight_kernel, ctx, fsdp),
        [shape((ctx, shard, own_width))] * fsdp, [table, branch] + attn_parts,
        scratch=[square_scratch],
        time=3.3,
    )
    out_nears = near_scatter(out_sides, fsdp)

    out_parts = far_scatter(out_nears, fsdp)
    part_out = low(total_of(out_parts))
    grad_slots, part_out = ffn_sums.advance(grad_slots, part_out)
    grad_qkv = attention_backward(
        table, lengths, block_order, qkv, grad_slots, part_out, out_t, log_total, own_heads, depth, TILE
    )
    (grad_qkv,) = ffn_sums.advance(grad_qkv)
    qkv_sides = call(
        "qkv_weights", functools.partial(qkv_weight_kernel, len(attn_slots), ctx, fsdp),
        [shape((shard, 3 * own_width))] * fsdp, [table] + attn_slots + [grad_qkv],
        scratch=[pltpu.VMEM((fsdp, shard, 3 * own_width), jnp.bfloat16)],
        time=6,
    )
    if ffn_sums.step > 1:
        grad_qkv, qkv_sides = ffn_sums.advance(grad_qkv, qkv_sides)
    grad_back = exchange(grad_qkv)
    later_qkv, unused = tie(w_qkv, qkv_sides[0])
    qkv_nears = far_gather(later_qkv, fsdp)
    qkv_sum = far_scatter(near_scatter(qkv_sides, fsdp), fsdp)

    qkv_sum = ffn_sums.advance(qkv_sum)[0] if ffn_sums.step > 1 else qkv_sum
    own_sum, ffn_up, ffn_down = ffn_sums.sums()
    *gate_sides, rest = call(
        "cut", functools.partial(cut_kernel, ctx),
        [shape((sub, 2 * hidden))] * fsdp + [shape((lines // 2, 2 * hidden))],
        [table, own_sum, ffn_up, ffn_down],
        scratch=[pltpu.VMEM((lines + lines // 2, 2 * hidden), jnp.bfloat16)],
        time=3,
    )
    (joined,) = call(
        "join", functools.partial(join_kernel, len(qkv_sum)),
        [shape((shard, 4 * own_width))], [table] + qkv_sum + [grad_back],
        time=2.5,
    )
    gate_sides = side_exchange(gate_sides, fsdp)
    gate_sides, joined = tie(gate_sides, joined)
    (packed,) = call(
        "pack", functools.partial(pack_kernel, ctx),
        [shape((lines + lines // 2, 2 * hidden))], [table, rest] + gate_sides,
        time=2,
    )
    ffn_going = Gather(packed, ring)
    attn_going = Gather(joined, ring)
    weights = near_gather(qkv_nears, fsdp)
    (grad_tokens,) = call(
        "tail", functools.partial(tail_kernel, ctx, fsdp),
        [shape((rows, width))], [table, tokens, grad_resid, grad_back] + weights + slices,
        scratch=[gain_scratch, pltpu.VMEM((rows, width), f32), pltpu.VMEM((rows, 3 * width), jnp.bfloat16)],
        time=8,
    )
    ffn_going.advance()
    (grad_tokens,) = ffn_going.advance(grad_tokens)
    results = [
        shape((shard, 2 * hidden * fsdp), f32), shape((hidden, width), f32),
        shape((shard, 3 * width), f32), shape((shard, width), f32),
    ]
    inputs = [table, w_gate_up, gain_two, w_qkv if aligned else unmixed(relative(w_qkv, table, ctx), ctx, own_width), gain_one]
    inputs += ffn_going.slots() + attn_going.slots()
    scratch = [pltpu.VMEM(x.shape, f32) for x in results] + [pltpu.VMEM((width, hidden), f32)]
    scratch += [pltpu.VMEM((ctx,) + packed.shape, jnp.bfloat16), pltpu.VMEM((ctx,) + joined.shape, jnp.bfloat16)]
    *results, grad_gain_ffn, grad_gain_attn = pl.pallas_call(
        functools.partial(final_kernel, ctx, fsdp, factor, aligned),
        out_shape=results + [shape((1, shard), f32)] * 2,
        in_specs=[SM] + [VM] * (len(inputs) - 1),
        out_specs=[pl.BlockSpec(memory_space=pltpu.HBM)] * 4 + [VM] * 2,
        scratch_shapes=scratch + [pltpu.SemaphoreType.DMA((4,))],
        compiler_params=room(inputs[1:] + scratch, 8),
        cost_estimate=cost(6),
        name="final",
    )(*inputs)
    grad_w_gate_up, grad_w_down, grad_w_qkv, grad_w_out = results
    if not aligned:
        grad_w_qkv, grad_w_out = ordered(grad_w_qkv, table, 3, ctx), ordered(grad_w_out, table, 1, ctx)
    output = low(resid + total_of(far_scatter(near_scatter(out_terms, fsdp), fsdp)))
    return (
        output,
        grad_tokens,
        grad_gain_attn.reshape(shard),
        grad_w_qkv,
        grad_w_out,
        grad_gain_ffn.reshape(shard),
        grad_w_gate_up,
        grad_w_down,
    )


def relative(weight, table, ctx):
    rows = weight.shape[0]
    parts = weight.reshape(rows, 3, ctx, -1)
    slots = [lax.dynamic_index_in_dim(parts, table[0, k], 2, keepdims=False) for k in range(ctx)]
    return jnp.concatenate([slot.reshape(rows, -1) for slot in slots], axis=1)


def unmixed(weight, ctx, own_width):
    rows = weight.shape[0]
    return weight.reshape(rows, ctx, 3, own_width).transpose(0, 2, 1, 3).reshape(rows, -1)


def ordered(array, table, parts, ctx):
    rows = array.shape[0]
    split = array.reshape(rows, parts, ctx, -1)
    result = jnp.zeros_like(split)
    for k in range(ctx):
        result = lax.dynamic_update_slice(result, split[:, :, k : k + 1], (0, 0, table[0, k], 0))
    return result.reshape(rows, -1)


def solution(mesh):
    in_specs = (
        P(("fsdp", "ctx"), None),
        P(("fsdp", "ctx"), None),
        P("fsdp"),
        P("fsdp", None),
        P("fsdp", None),
        P("fsdp"),
        P("fsdp", None),
        P("fsdp", None),
        P("fsdp", None),
        P("fsdp", None),
    )
    out_specs = (
        P(("fsdp", "ctx"), None),
        P(("fsdp", "ctx"), None),
        P("fsdp"),
        P("fsdp", None),
        P("fsdp", None),
        P("fsdp"),
        P("fsdp", None),
        P("fsdp", None),
    )
    return jax.shard_map(body, mesh=mesh, in_specs=in_specs, out_specs=out_specs, check_vma=False)
```

```python
import functools
import math

import jax
import jax.numpy as jnp
from jax import lax
from jax.experimental import pallas as pl
from jax.experimental.pallas import tpu as pltpu
from jax.sharding import PartitionSpec as P

HEADS = 16
TILE = 256
VMEM_FWD = 26 << 20
VMEM_BWD = 34 << 20


EPS = 1e-05
MASKED=-1e30
def nt(a,b): return lax.dot_general(a,b,(((1,),(1,)),((),())),preferred_element_type=jnp.float32)
def nn(a,b): return lax.dot_general(a,b,(((1,),(0,)),((),())),preferred_element_type=jnp.float32)

def ends_of(lengths_ref):
    ends = [lengths_ref[0, 0]]
    for i in range(1, lengths_ref.shape[1]):
        ends.append(ends[-1] + lengths_ref[0, i])
    return ends

def first_tile(ends, position, tile):
    start = jnp.int32(0)
    for end in ends[:-1]:
        start = jnp.where(end <= position, end, start)
    return start // tile

def last_tile(ends, position, tile):
    last = ends[-1]
    for end in reversed(ends[:-1]):
        last = jnp.where(end > position, end, last)
    return (last - 1) // tile

def seen(ends, query_start, key_start, queries, keys):
    pos_query = query_start + lax.broadcasted_iota(jnp.int32, (1, queries), 1)
    start = jnp.zeros((1, queries), jnp.int32)
    for end in ends[:-1]:
        start = jnp.where(pos_query >= end, end, start)
    pos_key = key_start + lax.broadcasted_iota(jnp.int32, (keys, queries), 0)
    return (pos_key <= pos_query) & (pos_key >= start)

def head_lanes(x, head, heads, depth):
    if heads == 1:
        return x
    lane = lax.broadcasted_iota(jnp.int32, x.shape, 1)
    return jnp.where((lane >= head * depth) & (lane < (head + 1) * depth), x, jnp.zeros_like(x))

def placed(slots, block, table, order_ref, per):
    number = 0
    for slot in slots:
        for row in range(0, slot.shape[0], block):
            position = order_ref[0, table[0, number // per] * per + number % per] * block
            yield slot, pl.ds(row, block), pl.ds(pl.multiple_of(position, block), block)
            number += 1

def stored(owners, block, order_ref, per):
    for owner in range(owners):
        for b in range(per):
            position = order_ref[0, owner * per + b] * block
            yield owner, pl.ds(b * block, block), pl.ds(pl.multiple_of(position, block), block)

def fwd_kernel(meta, table, lengths_ref, order_ref, *refs):
    given, n, heads, depth, tile, block = meta
    qkv_refs, out_refs = refs[:given], refs[given:given+n]
    out_t_ref, lse_ref = refs[given+n], refs[given+n+1]
    q_ref, k_ref, v_ref, o_ref = refs[given+n+2:]
    ends = ends_of(lengths_ref)
    width = heads*depth
    scale = depth ** (-0.5)
    per = out_refs[0].shape[0] // block
    for slot, src, dst in placed(qkv_refs, block, table, order_ref, per):
        q = slot[src, 0:width].astype(jnp.float32)*scale
        for h in range(heads):
            q_ref[h, dst, :] = head_lanes(q, h, heads, depth).astype(jnp.bfloat16)
        k_ref[dst, :] = slot[src, width:2*width]
        v_ref[dst, :] = slot[src, 2*width:]
    wide_tile = 2 * tile
    tiles = q_ref.shape[1] // wide_tile
    def one_query(t, _):
        rows = pl.ds(pl.multiple_of(t*wide_tile, wide_tile), wide_tile)
        qs = [q_ref[h, rows, :] for h in range(heads)]
        def one_key(j, carry):
            keys = pl.ds(pl.multiple_of(j*tile, tile), tile)
            k = k_ref[keys, :]
            v_t = jnp.transpose(v_ref[keys, :].astype(jnp.float32)).astype(jnp.bfloat16)
            mask = seen(ends, t*wide_tile, j*tile, wide_tile, tile)
            new = []
            for h in range(heads):
                m, l, acc = carry[h]
                s = jnp.where(mask, nt(k, qs[h]), MASKED)
                m_new = jnp.maximum(m, jnp.max(s, axis=0, keepdims=True))
                e = jnp.exp(s - m_new)
                alpha = jnp.exp(m - m_new)
                l = l*alpha + jnp.sum(e, axis=0, keepdims=True)
                acc = acc*alpha + nn(v_t[h*depth:(h+1)*depth], e.astype(jnp.bfloat16))
                new.append((m_new, l, acc))
            return tuple(new)
        init = tuple((jnp.full((1,wide_tile),MASKED,jnp.float32), jnp.zeros((1,wide_tile),jnp.float32), jnp.zeros((depth,wide_tile),jnp.float32)) for _ in range(heads))
        final = lax.fori_loop(first_tile(ends, t*wide_tile, tile), 2*t+2, one_key, init)
        outs = []
        for h in range(heads):
            m, l, acc = final[h]
            outs.append(acc / l)
            lse_ref[h:h+1, rows] = m + jnp.log(l)
        out_t = jnp.concatenate(outs, axis=0) if heads > 1 else outs[0]
        out_t_ref[:, rows] = out_t
        o_ref[rows, :] = jnp.transpose(out_t).astype(jnp.bfloat16)
        return 0
    lax.fori_loop(0, tiles, one_query, 0)
    for slot, dst, src in placed(out_refs, block, table, order_ref, per):
        slot[dst, :] = o_ref[src, :]

def bwd_kernel(meta, table, lengths_ref, order_ref, *refs):
    given, n, heads, depth, tile, block = meta
    qkv_refs, grad_refs = refs[:given], refs[given:given+n]
    refs = refs[n:]
    part_out_ref, out_t_ref, lse_ref, dqkv_ref = refs[given:given+4]
    ends = ends_of(lengths_ref)
    q_ref, k_ref, v_ref, g_ref, k_t_ref, delta_ref, dq_t_ref, dq_ref, dk_ref, dv_ref = refs[given+4:]
    width = heads*depth
    scale = depth ** (-0.5)
    per = dqkv_ref.shape[1] // block
    total = k_ref.shape[0]
    for slot, src, dst in placed(qkv_refs, block, table, order_ref, per):
        q = slot[src, 0:width].astype(jnp.float32)*scale
        for h in range(heads):
            q_ref[h, dst, :] = head_lanes(q, h, heads, depth).astype(jnp.bfloat16)
        k_ref[dst, :] = slot[src, width:2*width]
        v_ref[dst, :] = slot[src, 2*width:]
    for slot, src, dst in placed(grad_refs, block, table, order_ref, per):
        g = slot[src, :].astype(jnp.float32)
        for h in range(heads):
            g_ref[h, dst, :] = head_lanes(g, h, heads, depth).astype(jnp.bfloat16)
    tiles = total // tile
    def prepare(t, _):
        rows = pl.ds(pl.multiple_of(t*tile, tile), tile)
        k_t_ref[:, rows] = jnp.transpose(k_ref[rows, :].astype(jnp.float32)).astype(jnp.bfloat16)
        g = g_ref[0, rows, :].astype(jnp.float32)
        for h in range(1, heads):
            g = g + g_ref[h, rows, :].astype(jnp.float32)
        prod = jnp.transpose(g) * out_t_ref[:, rows]
        for h in range(heads):
            delta_ref[h:h+1, rows] = jnp.sum(prod[h*depth:(h+1)*depth], axis=0, keepdims=True)
        dq_t_ref[:, rows] = jnp.zeros((width, tile), jnp.float32)
        return 0
    lax.fori_loop(0, tiles, prepare, 0)
    wide_tile = 2 * tile
    def one_key(j, _):
        keys = pl.ds(pl.multiple_of(j*tile, tile), tile)
        k = k_ref[keys, :]
        v = v_ref[keys, :]
        k_t = k_t_ref[:, keys]
        dk_ref[keys, :] = jnp.zeros((tile, width), jnp.float32)
        dv_ref[keys, :] = jnp.zeros((tile, width), jnp.float32)
        def one_query(t, _):
            rows = pl.ds(pl.multiple_of(t*wide_tile, wide_tile), wide_tile)
            mask = seen(ends, t*wide_tile, j*tile, wide_tile, tile)
            dk = dk_ref[keys, :]
            dv = dv_ref[keys, :]
            for h in range(heads):
                q = q_ref[h, rows, :]
                g = g_ref[h, rows, :]
                s = nt(k, q)
                p = jnp.where(mask, jnp.exp(s - lse_ref[h:h+1, rows]), 0.0)
                dp = nt(v, g)
                ds = (p*(dp - delta_ref[h:h+1, rows])).astype(jnp.bfloat16)
                dv = dv + nn(p.astype(jnp.bfloat16), g)
                dk = dk + nn(ds, q)
                part = pl.ds(h*depth, depth)
                dq_t_ref[part, rows] = dq_t_ref[part, rows] + nn(k_t[h*depth:(h+1)*depth], ds)
            dk_ref[keys, :] = dk
            dv_ref[keys, :] = dv
            return 0
        lax.fori_loop(j//2, last_tile(ends, j*tile + tile - 1, wide_tile) + 1, one_query, 0)
        return 0
    lax.fori_loop(0, tiles, one_key, 0)
    def finish(t, _):
        rows = pl.ds(pl.multiple_of(t*tile, tile), tile)
        dq_ref[rows, :] = (jnp.transpose(dq_t_ref[:, rows])*scale).astype(jnp.bfloat16)
        return 0
    lax.fori_loop(0, tiles, finish, 0)
    for owner, dst, src in stored(n, block, order_ref, per):
        dqkv_ref[owner, dst, 0:width] = dq_ref[src, :]
        dqkv_ref[owner, dst, width:2*width] = dk_ref[src, :].astype(jnp.bfloat16)
        dqkv_ref[owner, dst, 2*width:3*width] = dv_ref[src, :].astype(jnp.bfloat16)
    shard = part_out_ref.shape[1]
    rows = dqkv_ref.shape[1]
    for owner in range(n):
        dqkv_ref[owner, 0:shard, 3*width:] = part_out_ref[owner]
        if shard < rows:
            dqkv_ref[owner, shard:, 3*width:] = jnp.zeros((rows-shard, width), jnp.bfloat16)

SM=pl.BlockSpec(memory_space=pltpu.SMEM)
VM=pl.BlockSpec(memory_space=pltpu.VMEM)
def attention_forward(table, lengths, order, qkv, n, heads, depth, tile):
    total=sum(x.shape[0] for x in qkv); rows=total//n; width=heads*depth
    block=total//order.shape[1]
    meta=(len(qkv),n,heads,depth,tile,block)
    res=pl.pallas_call(functools.partial(fwd_kernel,meta),
        out_shape=[jax.ShapeDtypeStruct((rows,width),jnp.bfloat16)]*n+[jax.ShapeDtypeStruct((width,total),jnp.float32),jax.ShapeDtypeStruct((heads,total),jnp.float32)],
        in_specs=[SM,SM,SM]+[VM]*len(qkv), out_specs=[VM]*(n+2),
        scratch_shapes=[pltpu.VMEM((heads,total,width),jnp.bfloat16)]+[pltpu.VMEM((total,width),jnp.bfloat16)]*3,
        cost_estimate=cost(17),
        compiler_params=pltpu.CompilerParams(vmem_limit_bytes=VMEM_FWD),
        name="attention_forward")(table,lengths,order,*qkv)
    return list(res[:n]),res[n],res[n+1]
def attention_backward(table, lengths, order, qkv, grads, part_out, out_t, lse, heads, depth, tile):
    n=len(grads); rows=grads[0].shape[0]; total=n*rows; width=heads*depth
    block=total//order.shape[1]
    meta=(len(qkv),n,heads,depth,tile,block)
    f32=jnp.float32; b16=jnp.bfloat16
    return pl.pallas_call(functools.partial(bwd_kernel,meta),
        out_shape=jax.ShapeDtypeStruct((n,rows,4*width),b16),
        in_specs=[SM,SM,SM]+[VM]*(len(qkv)+n+3), out_specs=VM,
        scratch_shapes=[pltpu.VMEM((heads,total,width),b16),pltpu.VMEM((total,width),b16),pltpu.VMEM((total,width),b16),pltpu.VMEM((heads,total,width),b16),
          pltpu.VMEM((width,total),b16),pltpu.VMEM((heads,total),f32),pltpu.VMEM((width,total),f32),pltpu.VMEM((total,width),b16),pltpu.VMEM((total,width),f32),pltpu.VMEM((total,width),f32)],
        cost_estimate=cost(18),
        compiler_params=pltpu.CompilerParams(vmem_limit_bytes=VMEM_BWD),
        name="attention_backward")(table,lengths,order,*qkv,*grads,part_out,out_t,lse)


def tn(left, right):
    return lax.dot_general(left, right, (((0,), (0,)), ((), ())), preferred_element_type=jnp.float32)


def low(value):
    return value.astype(jnp.bfloat16)


def wide(value):
    return value.astype(jnp.float32)


def at(start, size):
    return pl.ds(pl.multiple_of(start, size), size)


def cost(microseconds):
    return pl.CostEstimate(flops=0, bytes_accessed=int(microseconds * 3.4e6), transcendentals=0)


def room(arrays, extra):
    total = 0
    for array in arrays:
        dims = [1, 1] + list(array.shape)
        rows, lanes = -(-dims[-2] // 16) * 16, -(-dims[-1] // 128) * 128
        total += math.prod(dims[:-2]) * rows * lanes * jnp.dtype(array.dtype).itemsize
    return pltpu.CompilerParams(vmem_limit_bytes=min(60 << 20, total + (extra << 20)))


def call(name, kernel, out, inputs, scratch=(), time=2.0, extra=8):
    return list(
        pl.pallas_call(
            kernel,
            out_shape=list(out),
            in_specs=[SM] + [VM] * (len(inputs) - 1),
            out_specs=[VM] * len(out),
            scratch_shapes=list(scratch),
            cost_estimate=cost(time),
            compiler_params=room(list(inputs[1:]) + list(out) + list(scratch), extra),
            name=name,
        )(*inputs)
    )


def shape(dims, dtype=jnp.bfloat16):
    return jax.ShapeDtypeStruct(tuple(dims), dtype)


def slice_kernel(own_width, table, w_ref, one_ref, two_ref, out_ref):
    shard, total = w_ref.shape
    for part in range(3):
        out_ref[0:shard, part * own_width : (part + 1) * own_width] = w_ref[
            :, at(part * (total // 3) + table[0, 0] * own_width, own_width)
        ]
    out_ref[shard : shard + 8, :] = gain_rows(wide(one_ref[...]), wide(two_ref[...]), 3 * own_width)


def gain_rows(one, two, lanes):
    shard = one.shape[1]
    if lanes > shard:
        rest = jnp.zeros((1, lanes - shard), jnp.float32)
        one, two = jnp.concatenate([one, rest], axis=1), jnp.concatenate([two, rest], axis=1)
    number = lax.broadcasted_iota(jnp.int32, (8, lanes), 0)
    return low(jnp.where(number == 0, one, jnp.where(number == 1, two, 0.0)))


def full_gain(table, n, pieces, row, gain_ref):
    shard = gain_ref.shape[1] // len(pieces)
    for slot, piece in enumerate(pieces):
        lines = wide(piece[pl.ds(piece.shape[0] - 8, 8), 0:shard])
        gain_ref[0:1, at(table[0, n + slot] * shard, shard)] = lines[row : row + 1]


def split_kernel(n, table, w_ref, *refs):
    outs, parts_ref = refs[:-1], refs[-1]
    count = len(outs)
    hidden = w_ref.shape[1] // (2 * count)
    for part in range(count):
        parts_ref[part, :, 0:hidden] = w_ref[:, part * hidden : (part + 1) * hidden]
        parts_ref[part, :, hidden:] = w_ref[:, (count + part) * hidden : (count + part + 1) * hidden]
    for slot in range(count):
        outs[slot][...] = parts_ref[table[0, n + slot]]


def project_kernel(n, table, rows_ref, *refs):
    pieces, attn_ref, qkv_ref, gain_ref, weight_ref = refs[:-4], refs[-4], refs[-3], refs[-2], refs[-1]
    shard = rows_ref.shape[1] // len(pieces)
    full_gain(table, n, pieces, 0, gain_ref)
    for slot, piece in enumerate(pieces):
        weight_ref[at(table[0, n + slot] * shard, shard), :] = piece[pl.ds(0, shard), :]
    value = wide(rows_ref[...])
    inverse = lax.rsqrt(jnp.mean(value * value, axis=1, keepdims=True) + EPS)
    attn_in = low(value * inverse * gain_ref[0:1, :])
    attn_ref[...] = attn_in
    qkv_ref[...] = low(nn(attn_in, weight_ref[...]))


def stage_rows(table, n, pieces, weight_ref):
    shard = pieces[0].shape[0]
    for slot, piece in enumerate(pieces):
        weight_ref[at(table[0, n + slot] * shard, shard), :] = piece[...]


def leave_kernel(n, count, table, tokens_ref, *refs):
    parts, outs, slices = refs[:n], refs[n : n + count], refs[n + count : n + 2 * count]
    resid_ref, ffn_ref, gain_ref, weight_ref = refs[n + 2 * count :]
    own_width = parts[0].shape[1]
    full_gain(table, n, slices, 1, gain_ref)
    stage_rows(table, n, outs, weight_ref)
    rows = tokens_ref.shape[0]
    attn = jnp.concatenate([parts[k][...] for k in range(n)], axis=1)
    ordered = jnp.concatenate([weight_ref[at(table[0, k] * own_width, own_width), :] for k in range(n)], axis=0)
    resid = wide(tokens_ref[...]) + nn(attn, ordered)
    resid_ref[...] = resid
    inverse = lax.rsqrt(jnp.mean(resid * resid, axis=1, keepdims=True) + EPS)
    ffn_ref[...] = low(resid * inverse * gain_ref[0:1, :])


def ffn_kernel(n, count, slots, table, *refs):
    ffn, cot = refs[:slots], refs[slots : 2 * slots]
    pieces, down_ref = refs[2 * slots : 2 * slots + count], refs[2 * slots + count]
    rest = refs[2 * slots + count + 1 :]
    terms, outs, hidden_ref, grad_ref = rest[:slots], rest[slots : 2 * slots], rest[2 * slots], rest[2 * slots + 1]
    gate_ref, up_ref, values_ref, cots_ref = rest[2 * slots + 2 :]
    hidden = down_ref.shape[0]
    shard = pieces[0].shape[0]
    rows = ffn[0].shape[0]
    for slot, piece in enumerate(pieces):
        place = at(table[0, n + slot] * shard, shard)
        gate_ref[place, :] = piece[:, 0:hidden]
        up_ref[place, :] = piece[:, hidden:]
    for slot in range(slots):
        values_ref[slot] = ffn[slot][...]
        cots_ref[slot] = cot[slot][...]

    def one(number, unused):
        value = values_ref[number]
        gate = nn(value, gate_ref[...])
        upward = nn(value, up_ref[...])
        grad_hidden = nt(cots_ref[number], down_ref[...])
        sigma = jax.nn.sigmoid(gate)
        active = gate * sigma
        hidden_low = low(active * upward)
        grad_gate = low(grad_hidden * upward * (sigma + active * (1.0 - sigma)))
        grad_up = low(grad_hidden * active)
        place = at(number * rows, rows)
        hidden_ref[place, :] = hidden_low
        grad_ref[place, 0:hidden] = grad_gate
        grad_ref[place, hidden:] = grad_up
        values_ref[number] = low(nt(grad_gate, gate_ref[...]) + nt(grad_up, up_ref[...]))
        cots_ref[number] = low(nn(hidden_low, down_ref[...]))
        return 0

    lax.fori_loop(0, slots, one, 0)
    for slot in range(slots):
        terms[slot][...] = values_ref[slot]
        outs[slot][...] = cots_ref[slot]


def ffn_weight_kernel(n, count, table, *refs):
    ffn, cot, rest = refs[:count], refs[count : 2 * count], refs[2 * count :]
    hiddens, grads, rest = rest[: count // 2], rest[count // 2 : count], rest[count:]
    outs, (value_ref, turned_ref) = rest[:-2], rest[-2:]
    hidden = hiddens[0].shape[1]
    half = n // 2
    shard = ffn[0].shape[1] // count
    sub = shard // n
    lines = count * sub
    cut = outs[half].shape[0]
    hidden_all = jnp.concatenate([r[...] for r in hiddens], axis=0)
    grad_all = jnp.concatenate([r[...] for r in grads], axis=0)

    def one(f, unused):
        lanes = at(f * shard, shard)
        ffn_all = jnp.concatenate([r[:, lanes] for r in ffn], axis=0)
        value_ref[f] = low(tn(ffn_all, grad_all))
        cot_all = jnp.concatenate([r[:, lanes] for r in cot], axis=0)
        turned_ref[f] = low(tn(cot_all, hidden_all))
        return 0

    lax.fori_loop(0, count, one, 0)

    def store(slot, row, lanes, value):
        if slot != half:
            outs[slot if slot < half else slot + 1][row : row + sub, lanes] = value
        elif row < cut:
            outs[half][row : row + sub, lanes] = value
        else:
            outs[half + 1][row - cut : row - cut + sub, lanes] = value

    for f in range(count):
        side, line = f // (count // 2), lines + (f % (count // 2)) * sub
        for slot in range(n):
            mine = at(table[0, slot] * sub, sub)
            store(slot, f * sub, slice(0, 2 * hidden), value_ref[f, mine, :])
            store(slot, line, slice(side * hidden, (side + 1) * hidden), turned_ref[f, mine, :])


def branch_kernel(n, count, got, table, resid_ref, cot_ref, *refs):
    terms, outs, slices = refs[:got], refs[got : got + count], refs[got + count : got + 2 * count]
    rest = refs[got + 2 * count :]
    grad_ref, branch_ref, parts = rest[0], rest[1], rest[2 : 2 + n]
    gain_ref, weight_ref = rest[2 + n :]
    own_width = parts[0].shape[1]
    full_gain(table, n, slices, 1, gain_ref)
    stage_rows(table, n, outs, weight_ref)
    resid = resid_ref[...]
    inverse = lax.rsqrt(jnp.mean(resid * resid, axis=1, keepdims=True) + EPS)
    normed = resid * inverse
    grad = wide(terms[0][...])
    for term in terms[1:]:
        grad = grad + wide(term[...])
    scaled = grad * gain_ref[0:1, :]
    inner = jnp.mean(scaled * normed, axis=1, keepdims=True)
    grad_resid = wide(cot_ref[...]) + inverse * (scaled - normed * inner)
    grad_ref[...] = grad_resid
    branch = low(grad_resid)
    branch_ref[...] = branch
    for k in range(n):
        parts[k][...] = low(nt(branch, weight_ref[at(table[0, k] * own_width, own_width), :]))


def out_weight_kernel(n, count, table, branch_ref, *refs):
    parts, outs, whole_ref = refs[:n], refs[n : n + count], refs[-1]
    own_width = parts[0].shape[1]
    shard = outs[0].shape[1]
    branch = branch_ref[...]
    for k in range(n):
        whole_ref[at(table[0, k] * own_width, own_width), :] = low(tn(parts[k][...], branch))
    for slot in range(count):
        lines = whole_ref[at(table[0, n + slot] * shard, shard), :]
        for owner in range(n):
            outs[slot][owner] = lines[:, owner * own_width : (owner + 1) * own_width]


def qkv_weight_kernel(given, n, count, table, *refs):
    attn, grads_ref, outs, whole_ref = refs[:given], refs[given], refs[given + 1 : -1], refs[-1]
    shard = outs[0].shape[0]
    used = outs[0].shape[1]
    grad_all = jnp.concatenate([grads_ref[table[0, k], :, 0:used] for k in range(n)], axis=0)

    def one(f, unused):
        attn_all = jnp.concatenate([r[:, at(f * shard, shard)] for r in attn], axis=0)
        whole_ref[f] = low(tn(attn_all, grad_all))
        return 0

    lax.fori_loop(0, count, one, 0)
    for slot in range(count):
        outs[slot][...] = whole_ref[table[0, n + slot]]


def tail_kernel(n, count, table, tokens_ref, grad_ref, parts_ref, *refs):
    weights, slices = refs[:count], refs[count : 2 * count]
    out_ref, gain_ref, sum_ref, grads_ref = refs[2 * count :]
    own_width = parts_ref.shape[2] // 4
    width = tokens_ref.shape[1]
    shard = width // count
    full_gain(table, n, slices, 0, gain_ref)
    for owner in range(n):
        for part in range(3):
            start = part * width + owner * own_width
            grads_ref[:, start : start + own_width] = parts_ref[owner, :, part * own_width : (part + 1) * own_width]
    sum_ref[...] = jnp.zeros_like(sum_ref)

    def one(part, unused):
        lanes = at(part * width, width)
        for slot in range(count):
            place = at(table[0, n + slot] * shard, shard)
            sum_ref[:, place] += nt(grads_ref[:, lanes], weights[slot][:, lanes])
        return 0

    lax.fori_loop(0, 3, one, 0)
    value = wide(tokens_ref[...])
    inverse = lax.rsqrt(jnp.mean(value * value, axis=1, keepdims=True) + EPS)
    normed = value * inverse
    scaled = sum_ref[...] * gain_ref[0:1, :]
    inner = jnp.mean(scaled * normed, axis=1, keepdims=True)
    out_ref[...] = low(grad_ref[...] + inverse * (scaled - normed * inner))


def row_sums(product):
    rows, lanes = product.shape
    total = product[:, 0:128]
    for i in range(1, lanes // 128):
        total = total + product[:, i * 128 : (i + 1) * 128]
    return jnp.sum(jnp.transpose(total), axis=0, keepdims=True)


def final_kernel(n, count, factor, aligned, table, gate_up_ref, gain_two_ref, w_qkv_ref, gain_one_ref, *refs):
    pieces, others = refs[: n + 1], refs[n + 1 : 2 * n + 2]
    outs, gain_outs, whole, sem = refs[2 * n + 2 : 2 * n + 6], refs[2 * n + 6 : 2 * n + 8], refs[2 * n + 8 : -1], refs[-1]
    gu_ref, down_ref, qkv_ref, out_ref, turned_ref, pieces_ref, others_ref = whole
    hidden, width = down_ref.shape
    sub = gu_ref.shape[0] // n
    own_width = others[0].shape[1] // 4
    half = n // 2
    copies = []

    def leave(number):
        copy = pltpu.make_async_copy(whole[number], outs[number], sem.at[number])
        copy.start()
        copies.append(copy)

    def stack(parts, whole_ref):
        for number, part in enumerate(parts):
            k = number if number <= half else number - 1
            row = parts[half].shape[0] if number == half + 1 else 0
            whole_ref[k, row : row + part.shape[0], :] = part[...]

    stack(pieces, pieces_ref)
    stack(others, others_ref)

    def one(k, unused):
        start = table[0, k] * sub
        for part in range(count):
            lines = wide(pieces_ref[k, part * sub : (part + 1) * sub, :]) * factor
            gu_ref[at(start, sub), part * hidden : (part + 1) * hidden] = lines[:, 0:hidden]
            gu_ref[at(start, sub), (count + part) * hidden : (count + part + 1) * hidden] = lines[:, hidden:]
            side, line = part // (count // 2), (count + part % (count // 2)) * sub
            turned_ref[at(part * (n * sub) + start, sub), :] = pieces_ref[k, line : line + sub, side * hidden : (side + 1) * hidden]
        return 0

    lax.fori_loop(0, n, one, 0)
    leave(0)

    def other(k, owner):
        for part in range(4):
            value = wide(others_ref[k, :, part * own_width : (part + 1) * own_width]) * factor
            target = out_ref if part == 3 else qkv_ref
            base = 0 if part == 3 else part * width
            if aligned:
                target[:, at(base + owner * own_width, own_width)] = value
            else:
                target[:, base + k * own_width : base + (k + 1) * own_width] = value
        return 0

    if aligned:
        lax.fori_loop(0, n, lambda k, unused: other(k, table[0, k]), 0)
    else:
        for k in range(n):
            other(k, None)
    leave(2)
    leave(3)
    for i in range(width // 128):
        down_ref[:, i * 128 : (i + 1) * 128] = wide(jnp.transpose(turned_ref[i * 128 : (i + 1) * 128, :])) * factor
    leave(1)
    gain_outs[0][...] = row_sums(wide(gate_up_ref[...]) * gu_ref[...]) / wide(gain_two_ref[...])
    gain_outs[1][...] = row_sums(wide(w_qkv_ref[...]) * qkv_ref[...]) / wide(gain_one_ref[...])
    for copy in copies:
        copy.wait()


def cut_kernel(n, table, own_ref, up_ref, down_ref, *refs):
    outs, rest_ref, sum_ref = refs[:-2], refs[-2], refs[-1]
    sum_ref[...] = low(wide(own_ref[...]) + wide(up_ref[...]) + wide(down_ref[...]))
    sub = outs[0].shape[0]
    for slot, out in enumerate(outs):
        out[...] = sum_ref[at(table[0, n + slot] * sub, sub), :]
    rest_ref[...] = sum_ref[len(outs) * sub :, :]


def pack_kernel(n, table, rest_ref, *refs):
    pieces, out_ref = refs[:-1], refs[-1]
    sub = pieces[0].shape[0]
    for slot, piece in enumerate(pieces):
        out_ref[at(table[0, n + slot] * sub, sub), :] = piece[...]
    out_ref[len(pieces) * sub :, :] = rest_ref[...]


def join_kernel(terms, table, *refs):
    qkv, back_ref, out_ref = refs[:terms], refs[terms], refs[-1]
    total = wide(qkv[0][...])
    for term in qkv[1:]:
        total = total + wide(term[...])
    start = total.shape[1]
    out_ref[:, 0:start] = low(total)
    shard = out_ref.shape[0]
    other = wide(back_ref[0, 0:shard, start:])
    for owner in range(1, back_ref.shape[0]):
        other = other + wide(back_ref[owner, 0:shard, start:])
    out_ref[:, start:] = low(other)


def ring_of(count):
    if count % 4 or count < 8:
        return list(range(count))
    across = count // 4
    order = []
    for along in range(4):
        columns = range(1, across) if along % 2 == 0 else range(across - 1, 0, -1)
        order += [along * across + column for column in columns]
    return order + [along * across for along in reversed(range(4))]


def ring_shift(value, ring, step):
    count = len(ring)
    return lax.ppermute(
        value, "ctx", [(ring[i], ring[(i + step) % count]) for i in range(count)]
    )


def tie(*values):
    return lax.optimization_barrier(values)


class Gather:
    def __init__(self, value, ring):
        self.ring, self.half, self.step = ring, len(ring) // 2, 1
        self.first, self.ahead, self.behind, self.far = value, [], [], None
        self.up, self.down = tie(ring_shift(value, ring, 1), ring_shift(value, ring, -1))

    def advance(self, *others):
        self.ahead.append(self.down)
        self.behind.append(self.up)
        self.up, self.down, *others = tie(self.up, self.down, *others)
        self.step += 1
        up, down = self.up, self.down
        if self.step == self.half:
            cut = up.shape[0] // 2
            up, down = up[:cut], down[cut:]
        self.up, self.down = tie(ring_shift(up, self.ring, 1), ring_shift(down, self.ring, -1))
        return others

    def slots(self):
        while self.step < self.half:
            self.advance()
        return [self.first] + self.ahead + [self.up, self.down] + self.behind[::-1]


class Scatter:
    def __init__(self, terms, ring):
        self.ring, self.half, self.terms = ring, len(ring) // 2, terms
        self.up, self.down = terms[self.half : self.half + 2]
        self.step = self.half
        self.send()

    def send(self):
        self.up, self.down = tie(ring_shift(self.up, self.ring, 1), ring_shift(self.down, self.ring, -1))

    def advance(self, *others):
        self.up, self.down, *others = tie(self.up, self.down, *others)
        up, down, cut = self.terms[self.step - 1], self.terms[len(self.ring) + 2 - self.step], self.up.shape[0]
        if self.step == self.half:
            rows = up.shape[0]
            self.up = low(wide(up) + jnp.pad(wide(self.up), ((0, rows - cut), (0, 0))))
            self.down = low(wide(down) + jnp.pad(wide(self.down), ((rows - cut, 0), (0, 0))))
        else:
            self.up, self.down = add_low(up, self.up), add_low(down, self.down)
        self.up, self.down, *others = tie(self.up, self.down, *others)
        self.step -= 1
        self.send()
        return others

    def sums(self):
        while self.step > 1:
            self.advance()
        return [self.terms[0], self.up, self.down]


def ring_exchange(slots, ring):
    count = len(ring)
    result = [slots[0]] + [None] * (count - 1)
    for k in range(1, count):
        result[count - k] = ring_shift(slots[k], ring, k)
    return result


def exchange(array):
    return lax.all_to_all(array, "ctx", 0, 0, tiled=True)


def partner(value, count):
    return lax.ppermute(value, "fsdp", [(i, i ^ 1) for i in range(count)])


def chip_shift(value, count, step):
    return lax.ppermute(value, "fsdp", [(i, (i + 2 * step) % count) for i in range(count)])


def far_gather(value, count):
    return [value] + [chip_shift(value, count, -step) for step in range(1, count // 2)]


def near_gather(nears, count):
    slots = []
    for near in nears:
        slots += [near, partner(near, count)]
    return slots


def near_scatter(terms, count):
    return [add_low(terms[i], partner(terms[i + 1], count)) for i in range(0, count, 2)]


def far_scatter(nears, count):
    return [nears[0]] + [chip_shift(nears[step], count, step) for step in range(1, count // 2)]


def side_exchange(pieces, count, slots=None):
    chips = count // 2
    received = []
    for slot in range(count) if slots is None else slots:
        step, flip = (chips - slot // 2) % chips, slot % 2
        piece = pieces[2 * step + flip]
        if step or flip:
            pairs = [(i, ((i + 2 * step) % count) ^ flip) for i in range(count)]
            piece = lax.ppermute(piece, "fsdp", pairs)
        received.append(piece)
    return received


def add_low(left, right):
    return low(wide(left) + wide(right))


def total_of(terms):
    total = wide(terms[0])
    for term in terms[1:]:
        total = total + wide(term)
    return total


def body(
    tokens, cotangent, gain_attn, w_qkv, w_out, gain_ffn, w_gate_up, w_down, lengths, block_order
):
    rows, width = tokens.shape
    heads = HEADS
    depth = width // heads
    ctx = lax.axis_size("ctx")
    fsdp = lax.axis_size("fsdp")
    factor = 1.0 / math.sqrt(rows * ctx * fsdp)
    shard = width // fsdp
    hidden = w_down.shape[0]
    own_heads = heads // ctx
    own_width = own_heads * depth
    aligned = own_width % 128 == 0
    half = ctx // 2
    sub = shard // ctx
    lines = fsdp * sub
    ring = ring_of(ctx)
    chips = fsdp // 2
    entries = []
    for c in range(ctx):
        me = ring.index(c)
        for f in range(fsdp):
            owners = [ring[(me + k) % ctx] for k in range(ctx)]
            sides = [((f // 2 + s) % chips) * 2 + ((f % 2) ^ k) for s in range(chips) for k in (0, 1)]
            entries.append(owners + sides)
    device = lax.axis_index("ctx") * fsdp + lax.axis_index("fsdp")
    table = lax.dynamic_slice_in_dim(jnp.asarray(entries, jnp.int32), device, 1, 0)
    gain_one, gain_two = gain_attn.reshape(1, shard), gain_ffn.reshape(1, shard)
    f32 = jnp.float32
    gain_scratch = pltpu.VMEM((8, width), f32)
    square_scratch = pltpu.VMEM((width, width), jnp.bfloat16)

    going = Gather(tokens, ring)
    if aligned:
        (piece,) = call(
            "slice", functools.partial(slice_kernel, own_width),
            [shape((shard + 8, 3 * own_width))], [table, w_qkv, gain_one, gain_two],
            time=2.2,
        )
    else:
        mine = [
            lax.dynamic_slice(w_qkv, (0, part * width + table[0, 0] * own_width), (shard, own_width))
            for part in range(3)
        ]
        piece = jnp.concatenate(
            [jnp.concatenate(mine, axis=1), gain_rows(wide(gain_one), wide(gain_two), 3 * own_width)], axis=0
        )
    slices = far_gather(piece, fsdp)
    gate_pieces = call(
        "split", functools.partial(split_kernel, ctx),
        [shape((shard, 2 * hidden))] * fsdp, [table, w_gate_up],
        scratch=[pltpu.VMEM((fsdp, shard, 2 * hidden), jnp.bfloat16)],
        time=4,
    )
    sent = gate_pieces
    gate_pieces = [sent[0]] + side_exchange(sent, fsdp, range(1, 3)) + [None] * (fsdp - 3)
    slices, sent = going.advance(slices, sent)
    slices = near_gather(slices, fsdp)

    def project(slot):
        return call(
            "project", functools.partial(project_kernel, ctx),
            [shape(slot.shape), shape((slot.shape[0], 3 * own_width))], [table, slot] + slices,
            scratch=[gain_scratch, pltpu.VMEM((width, 3 * own_width), jnp.bfloat16)],
            time=2.6,
        )

    first = project(tokens)
    ahead, behind = [project(going.ahead[0])], [project(going.behind[0])]
    first, ahead[0], behind[0], gate_pieces[1:3] = going.advance(first, ahead[0], behind[0], gate_pieces[1:3])
    for step in range(1, half - 1):
        ahead.append(project(going.ahead[step]))
        behind.append(project(going.behind[step]))
        if step == 1:
            sent, unused = tie(sent, gate_pieces[1:3])
            gate_pieces[3:] = side_exchange(sent, fsdp, range(3, fsdp))
        if going.step < half:
            ahead[step], behind[step] = going.advance(ahead[step], behind[step])
    *far, ahead, behind, gate_pieces[3:] = tie(going.up, going.down, ahead, behind, gate_pieces[3:])
    far = [project(value) for value in far]
    later_out, far = tie(w_out, far)
    outs = far_gather(later_out, fsdp)
    pairs = [first] + ahead + far + behind[::-1]
    attn_slots, qkv = [pair[0] for pair in pairs], [pair[1] for pair in pairs]

    out_slots, out_t, log_total = attention_forward(
        table, lengths, block_order, qkv, ctx, own_heads, depth, TILE
    )
    near_out = partner(w_out, fsdp)
    out_slots, outs, near_out, gate_pieces = tie(out_slots, outs, near_out, gate_pieces)
    attn_parts = ring_exchange(out_slots, ring)
    later_cot, outs, unused = tie(cotangent, outs, attn_parts[-1])
    cots = far_gather(later_cot, fsdp)
    outs = [outs[0], near_out] + near_gather(outs[1:], fsdp)
    resid, ffn_in = call(
        "leave", functools.partial(leave_kernel, ctx, fsdp),
        [shape((rows, width), f32), shape((rows, width))],
        [table, tokens] + attn_parts + outs + slices,
        scratch=[gain_scratch, square_scratch],
        time=4.1,
    )

    ffn_in, cots = tie(ffn_in, cots)
    cots = near_gather(cots, fsdp)

    nears = far_gather(ffn_in, fsdp)
    ffns, grad_terms, out_terms, hiddens, grads = [], [], [], [], []
    for chip in range(chips):
        ffn_pair = [nears[chip], partner(nears[chip], fsdp)]
        result = call(
            "feed_forward", functools.partial(ffn_kernel, ctx, fsdp, 2),
            [shape((rows, width))] * 4 + [shape((2 * rows, hidden)), shape((2 * rows, 2 * hidden))],
            [table] + ffn_pair + cots[2 * chip : 2 * chip + 2] + gate_pieces + [w_down],
            scratch=[pltpu.VMEM((width, hidden), jnp.bfloat16)] * 2 + [pltpu.VMEM((2, rows, width), jnp.bfloat16)] * 2,
            time=9.5,
        )
        if chip == 0:
            result, nears[1:] = tie(result, nears[1:])
        ffns += ffn_pair
        grad_terms += result[0:2]
        out_terms += result[2:4]
        hiddens.append(result[4])
        grads.append(result[5])
    grad_nears = near_scatter(grad_terms, fsdp)
    hiddens, grad_nears = tie(hiddens, grad_nears)
    grad_parts = far_scatter(grad_nears, fsdp)
    terms_ffn = call(
        "feed_forward_weights", functools.partial(ffn_weight_kernel, ctx, fsdp),
        [shape((lines + lines // 2, 2 * hidden))] * half
        + [shape(((lines + lines // 2) // 2, 2 * hidden))] * 2
        + [shape((lines + lines // 2, 2 * hidden))] * (half - 1),
        [table] + ffns + cots + hiddens + grads,
        scratch=[pltpu.VMEM((fsdp, shard, 2 * hidden), jnp.bfloat16), pltpu.VMEM((fsdp, shard, hidden), jnp.bfloat16)],
        time=12,
    )
    grad_parts, unused = tie(grad_parts, terms_ffn[0])
    ffn_sums = Scatter(terms_ffn, ring)
    grad_resid, branch, *grad_attn = call(
        "branch", functools.partial(branch_kernel, ctx, fsdp, len(grad_parts)),
        [shape((rows, width), f32), shape((rows, width))] + [shape((rows, own_width))] * ctx,
        [table, resid, cotangent] + grad_parts + outs + slices,
        scratch=[gain_scratch, square_scratch],
        time=5,
    )
    grad_slots = ring_exchange(grad_attn, ring)
    out_sides = call(
        "out_weights", functools.partial(out_weight_kernel, ctx, fsdp),
        [shape((ctx, shard, own_width))] * fsdp, [table, branch] + attn_parts,
        scratch=[square_scratch],
        time=3.3,
    )
    out_nears = near_scatter(out_sides, fsdp)

    out_parts = far_scatter(out_nears, fsdp)
    part_out = low(total_of(out_parts))
    grad_slots, part_out = ffn_sums.advance(grad_slots, part_out)
    grad_qkv = attention_backward(
        table, lengths, block_order, qkv, grad_slots, part_out, out_t, log_total, own_heads, depth, TILE
    )
    (grad_qkv,) = ffn_sums.advance(grad_qkv)
    qkv_sides = call(
        "qkv_weights", functools.partial(qkv_weight_kernel, len(attn_slots), ctx, fsdp),
        [shape((shard, 3 * own_width))] * fsdp, [table] + attn_slots + [grad_qkv],
        scratch=[pltpu.VMEM((fsdp, shard, 3 * own_width), jnp.bfloat16)],
        time=6,
    )
    if ffn_sums.step > 1:
        grad_qkv, qkv_sides = ffn_sums.advance(grad_qkv, qkv_sides)
    grad_back = exchange(grad_qkv)
    later_qkv, unused = tie(w_qkv, qkv_sides[0])
    qkv_nears = far_gather(later_qkv, fsdp)
    qkv_sum = far_scatter(near_scatter(qkv_sides, fsdp), fsdp)

    qkv_sum = ffn_sums.advance(qkv_sum)[0] if ffn_sums.step > 1 else qkv_sum
    own_sum, ffn_up, ffn_down = ffn_sums.sums()
    *gate_sides, rest = call(
        "cut", functools.partial(cut_kernel, ctx),
        [shape((sub, 2 * hidden))] * fsdp + [shape((lines // 2, 2 * hidden))],
        [table, own_sum, ffn_up, ffn_down],
        scratch=[pltpu.VMEM((lines + lines // 2, 2 * hidden), jnp.bfloat16)],
        time=3,
    )
    (joined,) = call(
        "join", functools.partial(join_kernel, len(qkv_sum)),
        [shape((shard, 4 * own_width))], [table] + qkv_sum + [grad_back],
        time=2.5,
    )
    gate_sides = side_exchange(gate_sides, fsdp)
    gate_sides, joined = tie(gate_sides, joined)
    (packed,) = call(
        "pack", functools.partial(pack_kernel, ctx),
        [shape((lines + lines // 2, 2 * hidden))], [table, rest] + gate_sides,
        time=2,
    )
    ffn_going = Gather(packed, ring)
    attn_going = Gather(joined, ring)
    weights = near_gather(qkv_nears, fsdp)
    (grad_tokens,) = call(
        "tail", functools.partial(tail_kernel, ctx, fsdp),
        [shape((rows, width))], [table, tokens, grad_resid, grad_back] + weights + slices,
        scratch=[gain_scratch, pltpu.VMEM((rows, width), f32), pltpu.VMEM((rows, 3 * width), jnp.bfloat16)],
        time=8,
    )
    ffn_going.advance()
    (grad_tokens,) = ffn_going.advance(grad_tokens)
    results = [
        shape((shard, 2 * hidden * fsdp), f32), shape((hidden, width), f32),
        shape((shard, 3 * width), f32), shape((shard, width), f32),
    ]
    inputs = [table, w_gate_up, gain_two, w_qkv if aligned else unmixed(relative(w_qkv, table, ctx), ctx, own_width), gain_one]
    inputs += ffn_going.slots() + attn_going.slots()
    scratch = [pltpu.VMEM(x.shape, f32) for x in results] + [pltpu.VMEM((width, hidden), jnp.bfloat16)]
    scratch += [pltpu.VMEM((ctx,) + packed.shape, jnp.bfloat16), pltpu.VMEM((ctx,) + joined.shape, jnp.bfloat16)]
    *results, grad_gain_ffn, grad_gain_attn = pl.pallas_call(
        functools.partial(final_kernel, ctx, fsdp, factor, aligned),
        out_shape=results + [shape((1, shard), f32)] * 2,
        in_specs=[SM] + [VM] * (len(inputs) - 1),
        out_specs=[pl.BlockSpec(memory_space=pltpu.HBM)] * 4 + [VM] * 2,
        scratch_shapes=scratch + [pltpu.SemaphoreType.DMA((4,))],
        compiler_params=room(inputs[1:] + scratch, 8),
        cost_estimate=cost(6),
        name="final",
    )(*inputs)
    grad_w_gate_up, grad_w_down, grad_w_qkv, grad_w_out = results
    if not aligned:
        grad_w_qkv, grad_w_out = ordered(grad_w_qkv, table, 3, ctx), ordered(grad_w_out, table, 1, ctx)
    output = low(resid + total_of(far_scatter(near_scatter(out_terms, fsdp), fsdp)))
    return (
        output,
        grad_tokens,
        grad_gain_attn.reshape(shard),
        grad_w_qkv,
        grad_w_out,
        grad_gain_ffn.reshape(shard),
        grad_w_gate_up,
        grad_w_down,
    )


def relative(weight, table, ctx):
    rows = weight.shape[0]
    parts = weight.reshape(rows, 3, ctx, -1)
    slots = [lax.dynamic_index_in_dim(parts, table[0, k], 2, keepdims=False) for k in range(ctx)]
    return jnp.concatenate([slot.reshape(rows, -1) for slot in slots], axis=1)


def unmixed(weight, ctx, own_width):
    rows = weight.shape[0]
    return weight.reshape(rows, ctx, 3, own_width).transpose(0, 2, 1, 3).reshape(rows, -1)


def ordered(array, table, parts, ctx):
    rows = array.shape[0]
    split = array.reshape(rows, parts, ctx, -1)
    result = jnp.zeros_like(split)
    for k in range(ctx):
        result = lax.dynamic_update_slice(result, split[:, :, k : k + 1], (0, 0, table[0, k], 0))
    return result.reshape(rows, -1)


def solution(mesh):
    in_specs = (
        P(("fsdp", "ctx"), None),
        P(("fsdp", "ctx"), None),
        P("fsdp"),
        P("fsdp", None),
        P("fsdp", None),
        P("fsdp"),
        P("fsdp", None),
        P("fsdp", None),
        P("fsdp", None),
        P("fsdp", None),
    )
    out_specs = (
        P(("fsdp", "ctx"), None),
        P(("fsdp", "ctx"), None),
        P("fsdp"),
        P("fsdp", None),
        P("fsdp", None),
        P("fsdp"),
        P("fsdp", None),
        P("fsdp", None),
    )
    return jax.shard_map(body, mesh=mesh, in_specs=in_specs, out_specs=out_specs, check_vma=False)
```

```python
import functools
import math

import jax
import jax.numpy as jnp
from jax import lax
from jax.experimental import pallas as pl
from jax.experimental.pallas import tpu as pltpu
from jax.sharding import PartitionSpec as P

HEADS = 16
TILE = 256
VMEM_FWD = 26 << 20
VMEM_BWD = 34 << 20


EPS = 1e-05
MASKED=-1e30
def nt(a,b): return lax.dot_general(a,b,(((1,),(1,)),((),())),preferred_element_type=jnp.float32)
def nn(a,b): return lax.dot_general(a,b,(((1,),(0,)),((),())),preferred_element_type=jnp.float32)

def ends_of(lengths_ref):
    ends = [lengths_ref[0, 0]]
    for i in range(1, lengths_ref.shape[1]):
        ends.append(ends[-1] + lengths_ref[0, i])
    return ends

def first_tile(ends, position, tile):
    start = jnp.int32(0)
    for end in ends[:-1]:
        start = jnp.where(end <= position, end, start)
    return start // tile

def last_tile(ends, position, tile):
    last = ends[-1]
    for end in reversed(ends[:-1]):
        last = jnp.where(end > position, end, last)
    return (last - 1) // tile

def seen(ends, query_start, key_start, queries, keys):
    pos_query = query_start + lax.broadcasted_iota(jnp.int32, (1, queries), 1)
    start = jnp.zeros((1, queries), jnp.int32)
    for end in ends[:-1]:
        start = jnp.where(pos_query >= end, end, start)
    pos_key = key_start + lax.broadcasted_iota(jnp.int32, (keys, queries), 0)
    return (pos_key <= pos_query) & (pos_key >= start)

def head_lanes(x, head, heads, depth):
    if heads == 1:
        return x
    lane = lax.broadcasted_iota(jnp.int32, x.shape, 1)
    return jnp.where((lane >= head * depth) & (lane < (head + 1) * depth), x, jnp.zeros_like(x))

def placed(slots, block, table, order_ref, per):
    number = 0
    for slot in slots:
        for row in range(0, slot.shape[0], block):
            position = order_ref[0, table[0, number // per] * per + number % per] * block
            yield slot, pl.ds(row, block), pl.ds(pl.multiple_of(position, block), block)
            number += 1

def stored(owners, block, order_ref, per):
    for owner in range(owners):
        for b in range(per):
            position = order_ref[0, owner * per + b] * block
            yield owner, pl.ds(b * block, block), pl.ds(pl.multiple_of(position, block), block)

def fwd_kernel(meta, table, lengths_ref, order_ref, *refs):
    given, n, heads, depth, tile, block = meta
    qkv_refs, out_refs = refs[:given], refs[given:given+n]
    out_t_ref, lse_ref = refs[given+n], refs[given+n+1]
    q_ref, k_ref, v_ref, o_ref = refs[given+n+2:]
    ends = ends_of(lengths_ref)
    width = heads*depth
    scale = depth ** (-0.5)
    per = out_refs[0].shape[0] // block
    for slot, src, dst in placed(qkv_refs, block, table, order_ref, per):
        q = slot[src, 0:width].astype(jnp.float32)*scale
        for h in range(heads):
            q_ref[h, dst, :] = head_lanes(q, h, heads, depth).astype(jnp.bfloat16)
        k_ref[dst, :] = slot[src, width:2*width]
        v_ref[dst, :] = slot[src, 2*width:]
    wide_tile = 2 * tile
    tiles = q_ref.shape[1] // wide_tile
    def one_query(t, _):
        rows = pl.ds(pl.multiple_of(t*wide_tile, wide_tile), wide_tile)
        qs = [q_ref[h, rows, :] for h in range(heads)]
        def one_key(j, carry):
            keys = pl.ds(pl.multiple_of(j*tile, tile), tile)
            k = k_ref[keys, :]
            v_t = jnp.transpose(v_ref[keys, :].astype(jnp.float32)).astype(jnp.bfloat16)
            mask = seen(ends, t*wide_tile, j*tile, wide_tile, tile)
            new = []
            for h in range(heads):
                m, l, acc = carry[h]
                s = jnp.where(mask, nt(k, qs[h]), MASKED)
                m_new = jnp.maximum(m, jnp.max(s, axis=0, keepdims=True))
                e = jnp.exp(s - m_new)
                alpha = jnp.exp(m - m_new)
                l = l*alpha + jnp.sum(e, axis=0, keepdims=True)
                acc = acc*alpha + nn(v_t[h*depth:(h+1)*depth], e.astype(jnp.bfloat16))
                new.append((m_new, l, acc))
            return tuple(new)
        init = tuple((jnp.full((1,wide_tile),MASKED,jnp.float32), jnp.zeros((1,wide_tile),jnp.float32), jnp.zeros((depth,wide_tile),jnp.float32)) for _ in range(heads))
        final = lax.fori_loop(first_tile(ends, t*wide_tile, tile), 2*t+2, one_key, init)
        outs = []
        for h in range(heads):
            m, l, acc = final[h]
            outs.append(acc / l)
            lse_ref[h:h+1, rows] = m + jnp.log(l)
        out_t = jnp.concatenate(outs, axis=0) if heads > 1 else outs[0]
        out_t_ref[:, rows] = out_t
        o_ref[rows, :] = jnp.transpose(out_t).astype(jnp.bfloat16)
        return 0
    lax.fori_loop(0, tiles, one_query, 0)
    for slot, dst, src in placed(out_refs, block, table, order_ref, per):
        slot[dst, :] = o_ref[src, :]

def bwd_kernel(meta, table, lengths_ref, order_ref, *refs):
    given, n, heads, depth, tile, block = meta
    qkv_refs, grad_refs = refs[:given], refs[given:given+n]
    refs = refs[n:]
    part_out_ref, out_t_ref, lse_ref, dqkv_ref = refs[given:given+4]
    ends = ends_of(lengths_ref)
    q_ref, k_ref, v_ref, g_ref, k_t_ref, delta_ref, dq_t_ref, dq_ref, dk_ref, dv_ref = refs[given+4:]
    width = heads*depth
    scale = depth ** (-0.5)
    per = dqkv_ref.shape[1] // block
    total = k_ref.shape[0]
    for slot, src, dst in placed(qkv_refs, block, table, order_ref, per):
        q = slot[src, 0:width].astype(jnp.float32)*scale
        for h in range(heads):
            q_ref[h, dst, :] = head_lanes(q, h, heads, depth).astype(jnp.bfloat16)
        k_ref[dst, :] = slot[src, width:2*width]
        v_ref[dst, :] = slot[src, 2*width:]
    for slot, src, dst in placed(grad_refs, block, table, order_ref, per):
        g = slot[src, :].astype(jnp.float32)
        for h in range(heads):
            g_ref[h, dst, :] = head_lanes(g, h, heads, depth).astype(jnp.bfloat16)
    tiles = total // tile
    def prepare(t, _):
        rows = pl.ds(pl.multiple_of(t*tile, tile), tile)
        k_t_ref[:, rows] = jnp.transpose(k_ref[rows, :].astype(jnp.float32)).astype(jnp.bfloat16)
        g = g_ref[0, rows, :].astype(jnp.float32)
        for h in range(1, heads):
            g = g + g_ref[h, rows, :].astype(jnp.float32)
        prod = jnp.transpose(g) * out_t_ref[:, rows]
        for h in range(heads):
            delta_ref[h:h+1, rows] = jnp.sum(prod[h*depth:(h+1)*depth], axis=0, keepdims=True)
        dq_t_ref[:, rows] = jnp.zeros((width, tile), jnp.float32)
        return 0
    lax.fori_loop(0, tiles, prepare, 0)
    wide_tile = 2 * tile
    def one_key(j, _):
        keys = pl.ds(pl.multiple_of(j*tile, tile), tile)
        k = k_ref[keys, :]
        v = v_ref[keys, :]
        k_t = k_t_ref[:, keys]
        dk_ref[keys, :] = jnp.zeros((tile, width), jnp.float32)
        dv_ref[keys, :] = jnp.zeros((tile, width), jnp.float32)
        def one_query(t, _):
            rows = pl.ds(pl.multiple_of(t*wide_tile, wide_tile), wide_tile)
            mask = seen(ends, t*wide_tile, j*tile, wide_tile, tile)
            dk = dk_ref[keys, :]
            dv = dv_ref[keys, :]
            for h in range(heads):
                q = q_ref[h, rows, :]
                g = g_ref[h, rows, :]
                s = nt(k, q)
                p = jnp.where(mask, jnp.exp(s - lse_ref[h:h+1, rows]), 0.0)
                dp = nt(v, g)
                ds = (p*(dp - delta_ref[h:h+1, rows])).astype(jnp.bfloat16)
                dv = dv + nn(p.astype(jnp.bfloat16), g)
                dk = dk + nn(ds, q)
                part = pl.ds(h*depth, depth)
                dq_t_ref[part, rows] = dq_t_ref[part, rows] + nn(k_t[h*depth:(h+1)*depth], ds)
            dk_ref[keys, :] = dk
            dv_ref[keys, :] = dv
            return 0
        lax.fori_loop(j//2, last_tile(ends, j*tile + tile - 1, wide_tile) + 1, one_query, 0)
        return 0
    lax.fori_loop(0, tiles, one_key, 0)
    def finish(t, _):
        rows = pl.ds(pl.multiple_of(t*tile, tile), tile)
        dq_ref[rows, :] = (jnp.transpose(dq_t_ref[:, rows])*scale).astype(jnp.bfloat16)
        return 0
    lax.fori_loop(0, tiles, finish, 0)
    for owner, dst, src in stored(n, block, order_ref, per):
        dqkv_ref[owner, dst, 0:width] = dq_ref[src, :]
        dqkv_ref[owner, dst, width:2*width] = dk_ref[src, :].astype(jnp.bfloat16)
        dqkv_ref[owner, dst, 2*width:3*width] = dv_ref[src, :].astype(jnp.bfloat16)
    shard = part_out_ref.shape[1]
    rows = dqkv_ref.shape[1]
    for owner in range(n):
        dqkv_ref[owner, 0:shard, 3*width:] = part_out_ref[owner]
        if shard < rows:
            dqkv_ref[owner, shard:, 3*width:] = jnp.zeros((rows-shard, width), jnp.bfloat16)

SM=pl.BlockSpec(memory_space=pltpu.SMEM)
VM=pl.BlockSpec(memory_space=pltpu.VMEM)
def attention_forward(table, lengths, order, qkv, n, heads, depth, tile):
    total=sum(x.shape[0] for x in qkv); rows=total//n; width=heads*depth
    block=total//order.shape[1]
    meta=(len(qkv),n,heads,depth,tile,block)
    res=pl.pallas_call(functools.partial(fwd_kernel,meta),
        out_shape=[jax.ShapeDtypeStruct((rows,width),jnp.bfloat16)]*n+[jax.ShapeDtypeStruct((width,total),jnp.float32),jax.ShapeDtypeStruct((heads,total),jnp.float32)],
        in_specs=[SM,SM,SM]+[VM]*len(qkv), out_specs=[VM]*(n+2),
        scratch_shapes=[pltpu.VMEM((heads,total,width),jnp.bfloat16)]+[pltpu.VMEM((total,width),jnp.bfloat16)]*3,
        cost_estimate=cost(17),
        compiler_params=pltpu.CompilerParams(vmem_limit_bytes=VMEM_FWD),
        name="attention_forward")(table,lengths,order,*qkv)
    return list(res[:n]),res[n],res[n+1]
def attention_backward(table, lengths, order, qkv, grads, part_out, out_t, lse, heads, depth, tile):
    n=len(grads); rows=grads[0].shape[0]; total=n*rows; width=heads*depth
    block=total//order.shape[1]
    meta=(len(qkv),n,heads,depth,tile,block)
    f32=jnp.float32; b16=jnp.bfloat16
    return pl.pallas_call(functools.partial(bwd_kernel,meta),
        out_shape=jax.ShapeDtypeStruct((n,rows,4*width),b16),
        in_specs=[SM,SM,SM]+[VM]*(len(qkv)+n+3), out_specs=VM,
        scratch_shapes=[pltpu.VMEM((heads,total,width),b16),pltpu.VMEM((total,width),b16),pltpu.VMEM((total,width),b16),pltpu.VMEM((heads,total,width),b16),
          pltpu.VMEM((width,total),b16),pltpu.VMEM((heads,total),f32),pltpu.VMEM((width,total),f32),pltpu.VMEM((total,width),b16),pltpu.VMEM((total,width),f32),pltpu.VMEM((total,width),f32)],
        cost_estimate=cost(18),
        compiler_params=pltpu.CompilerParams(vmem_limit_bytes=VMEM_BWD),
        name="attention_backward")(table,lengths,order,*qkv,*grads,part_out,out_t,lse)


def tn(left, right):
    return lax.dot_general(left, right, (((0,), (0,)), ((), ())), preferred_element_type=jnp.float32)


def low(value):
    return value.astype(jnp.bfloat16)


def wide(value):
    return value.astype(jnp.float32)


def at(start, size):
    return pl.ds(pl.multiple_of(start, size), size)


def cost(microseconds):
    return pl.CostEstimate(flops=0, bytes_accessed=int(microseconds * 3.4e6), transcendentals=0)


def room(arrays, extra):
    total = 0
    for array in arrays:
        dims = [1, 1] + list(array.shape)
        rows, lanes = -(-dims[-2] // 16) * 16, -(-dims[-1] // 128) * 128
        total += math.prod(dims[:-2]) * rows * lanes * jnp.dtype(array.dtype).itemsize
    return pltpu.CompilerParams(vmem_limit_bytes=min(60 << 20, total + (extra << 20)))


def call(name, kernel, out, inputs, scratch=(), time=2.0, extra=8):
    return list(
        pl.pallas_call(
            kernel,
            out_shape=list(out),
            in_specs=[SM] + [VM] * (len(inputs) - 1),
            out_specs=[VM] * len(out),
            scratch_shapes=list(scratch),
            cost_estimate=cost(time),
            compiler_params=room(list(inputs[1:]) + list(out) + list(scratch), extra),
            name=name,
        )(*inputs)
    )


def shape(dims, dtype=jnp.bfloat16):
    return jax.ShapeDtypeStruct(tuple(dims), dtype)


def slice_kernel(own_width, table, w_ref, one_ref, two_ref, out_ref):
    shard, total = w_ref.shape
    for part in range(3):
        out_ref[0:shard, part * own_width : (part + 1) * own_width] = w_ref[
            :, at(part * (total // 3) + table[0, 0] * own_width, own_width)
        ]
    out_ref[shard : shard + 8, :] = gain_rows(wide(one_ref[...]), wide(two_ref[...]), 3 * own_width)


def gain_rows(one, two, lanes):
    shard = one.shape[1]
    if lanes > shard:
        rest = jnp.zeros((1, lanes - shard), jnp.float32)
        one, two = jnp.concatenate([one, rest], axis=1), jnp.concatenate([two, rest], axis=1)
    number = lax.broadcasted_iota(jnp.int32, (8, lanes), 0)
    return low(jnp.where(number == 0, one, jnp.where(number == 1, two, 0.0)))


def full_gain(table, n, pieces, row, gain_ref):
    shard = gain_ref.shape[1] // len(pieces)
    for slot, piece in enumerate(pieces):
        lines = wide(piece[pl.ds(piece.shape[0] - 8, 8), 0:shard])
        gain_ref[0:1, at(table[0, n + slot] * shard, shard)] = lines[row : row + 1]


def split_kernel(n, table, w_ref, *refs):
    outs, parts_ref = refs[:-1], refs[-1]
    count = len(outs)
    hidden = w_ref.shape[1] // (2 * count)
    step = w_ref.shape[0] // 4

    def one(i, unused):
        lines = at(i * step, step)
        for part in range(count):
            parts_ref[part, lines, 0:hidden] = w_ref[lines, part * hidden : (part + 1) * hidden]
            parts_ref[part, lines, hidden:] = w_ref[lines, (count + part) * hidden : (count + part + 1) * hidden]
        for slot in range(count):
            outs[slot][lines, :] = parts_ref[table[0, n + slot], lines, :]
        return 0

    lax.fori_loop(0, 4, one, 0)


def project_kernel(n, table, rows_ref, *refs):
    pieces, attn_ref, qkv_ref, gain_ref, weight_ref = refs[:-4], refs[-4], refs[-3], refs[-2], refs[-1]
    shard = rows_ref.shape[1] // len(pieces)
    full_gain(table, n, pieces, 0, gain_ref)
    for slot, piece in enumerate(pieces):
        weight_ref[at(table[0, n + slot] * shard, shard), :] = piece[pl.ds(0, shard), :]
    value = wide(rows_ref[...])
    inverse = lax.rsqrt(jnp.mean(value * value, axis=1, keepdims=True) + EPS)
    attn_in = low(value * inverse * gain_ref[0:1, :])
    attn_ref[...] = attn_in
    qkv_ref[...] = low(nn(attn_in, weight_ref[...]))


def stage_rows(table, n, pieces, weight_ref):
    shard = pieces[0].shape[0]
    for slot, piece in enumerate(pieces):
        weight_ref[at(table[0, n + slot] * shard, shard), :] = piece[...]


def leave_kernel(n, count, table, tokens_ref, *refs):
    parts, outs, slices = refs[:n], refs[n : n + count], refs[n + count : n + 2 * count]
    resid_ref, ffn_ref, gain_ref, weight_ref = refs[n + 2 * count :]
    own_width = parts[0].shape[1]
    full_gain(table, n, slices, 1, gain_ref)
    stage_rows(table, n, outs, weight_ref)
    rows = tokens_ref.shape[0]
    attn = jnp.concatenate([parts[k][...] for k in range(n)], axis=1)
    ordered = jnp.concatenate([weight_ref[at(table[0, k] * own_width, own_width), :] for k in range(n)], axis=0)
    resid = wide(tokens_ref[...]) + nn(attn, ordered)
    resid_ref[...] = resid
    inverse = lax.rsqrt(jnp.mean(resid * resid, axis=1, keepdims=True) + EPS)
    ffn_ref[...] = low(resid * inverse * gain_ref[0:1, :])


def ffn_kernel(n, count, slots, table, *refs):
    ffn, cot = refs[:slots], refs[slots : 2 * slots]
    pieces, down_ref = refs[2 * slots : 2 * slots + count], refs[2 * slots + count]
    rest = refs[2 * slots + count + 1 :]
    terms, outs, hidden_ref, grad_ref = rest[:slots], rest[slots : 2 * slots], rest[2 * slots], rest[2 * slots + 1]
    gate_ref, up_ref, values_ref, cots_ref = rest[2 * slots + 2 :]
    hidden = down_ref.shape[0]
    shard = pieces[0].shape[0]
    rows = ffn[0].shape[0]
    for slot, piece in enumerate(pieces):
        place = at(table[0, n + slot] * shard, shard)
        gate_ref[place, :] = piece[:, 0:hidden]
        up_ref[place, :] = piece[:, hidden:]
    for slot in range(slots):
        values_ref[slot] = ffn[slot][...]
        cots_ref[slot] = cot[slot][...]

    def one(number, unused):
        value = values_ref[number]
        gate = nn(value, gate_ref[...])
        upward = nn(value, up_ref[...])
        grad_hidden = nt(cots_ref[number], down_ref[...])
        sigma = jax.nn.sigmoid(gate)
        active = gate * sigma
        hidden_low = low(active * upward)
        grad_gate = low(grad_hidden * upward * (sigma + active * (1.0 - sigma)))
        grad_up = low(grad_hidden * active)
        place = at(number * rows, rows)
        hidden_ref[place, :] = hidden_low
        grad_ref[place, 0:hidden] = grad_gate
        grad_ref[place, hidden:] = grad_up
        values_ref[number] = low(nt(grad_gate, gate_ref[...]) + nt(grad_up, up_ref[...]))
        cots_ref[number] = low(nn(hidden_low, down_ref[...]))
        return 0

    lax.fori_loop(0, slots, one, 0)
    for slot in range(slots):
        terms[slot][...] = values_ref[slot]
        outs[slot][...] = cots_ref[slot]


def ffn_weight_kernel(n, count, table, *refs):
    ffn, cot, rest = refs[:count], refs[count : 2 * count], refs[2 * count :]
    hiddens, grads, rest = rest[: count // 2], rest[count // 2 : count], rest[count:]
    outs, (value_ref, turned_ref) = rest[:-2], rest[-2:]
    hidden = hiddens[0].shape[1]
    half = n // 2
    shard = ffn[0].shape[1] // count
    sub = shard // n
    lines = count * sub
    cut = outs[half].shape[0]
    hidden_all = jnp.concatenate([r[...] for r in hiddens], axis=0)
    grad_all = jnp.concatenate([r[...] for r in grads], axis=0)

    def one(f, unused):
        lanes = at(f * shard, shard)
        ffn_all = jnp.concatenate([r[:, lanes] for r in ffn], axis=0)
        value_ref[f] = low(tn(ffn_all, grad_all))
        cot_all = jnp.concatenate([r[:, lanes] for r in cot], axis=0)
        turned_ref[f] = low(tn(cot_all, hidden_all))
        return 0

    lax.fori_loop(0, count, one, 0)

    def store(slot, row, lanes, value):
        if slot != half:
            outs[slot if slot < half else slot + 1][row : row + sub, lanes] = value
        elif row < cut:
            outs[half][row : row + sub, lanes] = value
        else:
            outs[half + 1][row - cut : row - cut + sub, lanes] = value

    for f in range(count):
        side, line = f // (count // 2), lines + (f % (count // 2)) * sub
        for slot in range(n):
            mine = at(table[0, slot] * sub, sub)
            store(slot, f * sub, slice(0, 2 * hidden), value_ref[f, mine, :])
            store(slot, line, slice(side * hidden, (side + 1) * hidden), turned_ref[f, mine, :])


def branch_kernel(n, count, got, table, resid_ref, cot_ref, *refs):
    terms, outs, slices = refs[:got], refs[got : got + count], refs[got + count : got + 2 * count]
    rest = refs[got + 2 * count :]
    grad_ref, branch_ref, parts = rest[0], rest[1], rest[2 : 2 + n]
    gain_ref, weight_ref = rest[2 + n :]
    own_width = parts[0].shape[1]
    full_gain(table, n, slices, 1, gain_ref)
    stage_rows(table, n, outs, weight_ref)
    resid = resid_ref[...]
    inverse = lax.rsqrt(jnp.mean(resid * resid, axis=1, keepdims=True) + EPS)
    normed = resid * inverse
    grad = wide(terms[0][...])
    for term in terms[1:]:
        grad = grad + wide(term[...])
    scaled = grad * gain_ref[0:1, :]
    inner = jnp.mean(scaled * normed, axis=1, keepdims=True)
    grad_resid = wide(cot_ref[...]) + inverse * (scaled - normed * inner)
    grad_ref[...] = grad_resid
    branch = low(grad_resid)
    branch_ref[...] = branch
    for k in range(n):
        parts[k][...] = low(nt(branch, weight_ref[at(table[0, k] * own_width, own_width), :]))


def out_weight_kernel(n, count, table, branch_ref, *refs):
    parts, outs, whole_ref = refs[:n], refs[n : n + count], refs[-1]
    own_width = parts[0].shape[1]
    shard = outs[0].shape[1]
    branch = branch_ref[...]
    for k in range(n):
        whole_ref[at(table[0, k] * own_width, own_width), :] = low(tn(parts[k][...], branch))
    for slot in range(count):
        lines = whole_ref[at(table[0, n + slot] * shard, shard), :]
        for owner in range(n):
            outs[slot][owner] = lines[:, owner * own_width : (owner + 1) * own_width]


def qkv_weight_kernel(given, n, count, table, *refs):
    attn, grads_ref, outs, whole_ref = refs[:given], refs[given], refs[given + 1 : -1], refs[-1]
    shard = outs[0].shape[0]
    used = outs[0].shape[1]
    grad_all = jnp.concatenate([grads_ref[table[0, k], :, 0:used] for k in range(n)], axis=0)

    def one(f, unused):
        attn_all = jnp.concatenate([r[:, at(f * shard, shard)] for r in attn], axis=0)
        whole_ref[f] = low(tn(attn_all, grad_all))
        return 0

    lax.fori_loop(0, count, one, 0)
    for slot in range(count):
        outs[slot][...] = whole_ref[table[0, n + slot]]


def tail_kernel(n, count, table, tokens_ref, grad_ref, parts_ref, *refs):
    weights, slices = refs[: 2 * count], refs[2 * count : 3 * count]
    out_ref, gain_ref, sum_ref, grads_ref = refs[3 * count :]
    own_width = parts_ref.shape[2] // 4
    width = tokens_ref.shape[1]
    shard = width // count
    full_gain(table, n, slices, 0, gain_ref)
    for owner in range(n):
        for part in range(3):
            start = part * width + owner * own_width
            grads_ref[:, start : start + own_width] = parts_ref[owner, :, part * own_width : (part + 1) * own_width]
    sum_ref[...] = jnp.zeros_like(sum_ref)

    def one(part, unused):
        lanes = at(part * width, width)
        for slot in range(count):
            place = at(table[0, n + slot] * shard, shard)
            both = jnp.concatenate([weights[2 * slot + piece][:, lanes] for piece in range(2)], axis=0)
            sum_ref[:, place] += nt(grads_ref[:, lanes], both)
        return 0

    lax.fori_loop(0, 3, one, 0)
    value = wide(tokens_ref[...])
    inverse = lax.rsqrt(jnp.mean(value * value, axis=1, keepdims=True) + EPS)
    normed = value * inverse
    scaled = sum_ref[...] * gain_ref[0:1, :]
    inner = jnp.mean(scaled * normed, axis=1, keepdims=True)
    out_ref[...] = low(grad_ref[...] + inverse * (scaled - normed * inner))


def row_sums(product):
    rows, lanes = product.shape
    total = product[:, 0:128]
    for i in range(1, lanes // 128):
        total = total + product[:, i * 128 : (i + 1) * 128]
    return jnp.sum(jnp.transpose(total), axis=0, keepdims=True)


def final_kernel(n, count, factor, aligned, table, gate_up_ref, gain_two_ref, w_qkv_ref, gain_one_ref, *refs):
    pieces, others = refs[: n + 1], refs[n + 1 : 2 * n + 2]
    outs, gain_outs, whole, sem = refs[2 * n + 2 : 2 * n + 6], refs[2 * n + 6 : 2 * n + 8], refs[2 * n + 8 : -1], refs[-1]
    gu_ref, down_ref, qkv_ref, out_ref, turned_ref, pieces_ref, others_ref = whole
    hidden, width = down_ref.shape
    sub = gu_ref.shape[0] // n
    own_width = others[0].shape[1] // 4
    half = n // 2
    copies = []

    def leave(number):
        copy = pltpu.make_async_copy(whole[number], outs[number], sem.at[number])
        copy.start()
        copies.append(copy)

    def stack(parts, whole_ref):
        for number, part in enumerate(parts):
            k = number if number <= half else number - 1
            row = parts[half].shape[0] if number == half + 1 else 0
            whole_ref[k, row : row + part.shape[0], :] = part[...]

    stack(pieces, pieces_ref)
    stack(others, others_ref)

    def one(k, unused):
        start = table[0, k] * sub
        for part in range(count):
            lines = wide(pieces_ref[k, part * sub : (part + 1) * sub, :]) * factor
            gu_ref[at(start, sub), part * hidden : (part + 1) * hidden] = lines[:, 0:hidden]
            gu_ref[at(start, sub), (count + part) * hidden : (count + part + 1) * hidden] = lines[:, hidden:]
            side, line = part // (count // 2), (count + part % (count // 2)) * sub
            turned_ref[at(part * (n * sub) + start, sub), :] = pieces_ref[k, line : line + sub, side * hidden : (side + 1) * hidden]
        return 0

    lax.fori_loop(0, n, one, 0)
    leave(0)

    def other(k, owner):
        for part in range(4):
            value = wide(others_ref[k, :, part * own_width : (part + 1) * own_width]) * factor
            target = out_ref if part == 3 else qkv_ref
            base = 0 if part == 3 else part * width
            if aligned:
                target[:, at(base + owner * own_width, own_width)] = value
            else:
                target[:, base + k * own_width : base + (k + 1) * own_width] = value
        return 0

    if aligned:
        lax.fori_loop(0, n, lambda k, unused: other(k, table[0, k]), 0)
    else:
        for k in range(n):
            other(k, None)
    leave(2)
    leave(3)
    for i in range(width // 128):
        down_ref[:, i * 128 : (i + 1) * 128] = wide(jnp.transpose(turned_ref[i * 128 : (i + 1) * 128, :])) * factor
    leave(1)
    gain_outs[0][...] = row_sums(wide(gate_up_ref[...]) * gu_ref[...]) / wide(gain_two_ref[...])
    gain_outs[1][...] = row_sums(wide(w_qkv_ref[...]) * qkv_ref[...]) / wide(gain_one_ref[...])
    for copy in copies:
        copy.wait()


def cut_kernel(n, table, own_ref, up_ref, down_ref, *refs):
    outs, rest_ref, sum_ref = refs[:-2], refs[-2], refs[-1]
    sum_ref[...] = low(wide(own_ref[...]) + wide(up_ref[...]) + wide(down_ref[...]))
    sub = outs[0].shape[0]
    for slot, out in enumerate(outs):
        out[...] = sum_ref[at(table[0, n + slot] * sub, sub), :]
    rest_ref[...] = sum_ref[len(outs) * sub :, :]


def pack_kernel(n, table, rest_ref, *refs):
    pieces, out_ref = refs[:-1], refs[-1]
    sub = pieces[0].shape[0]
    for slot, piece in enumerate(pieces):
        out_ref[at(table[0, n + slot] * sub, sub), :] = piece[...]
    out_ref[len(pieces) * sub :, :] = rest_ref[...]


def join_kernel(terms, table, *refs):
    qkv, back_ref, out_ref = refs[:terms], refs[terms], refs[-1]
    total = wide(qkv[0][...])
    for term in qkv[1:]:
        total = total + wide(term[...])
    start = total.shape[1]
    out_ref[:, 0:start] = low(total)
    shard = out_ref.shape[0]
    other = wide(back_ref[0, 0:shard, start:])
    for owner in range(1, back_ref.shape[0]):
        other = other + wide(back_ref[owner, 0:shard, start:])
    out_ref[:, start:] = low(other)


def ring_of(count):
    if count % 4 or count < 8:
        return list(range(count))
    across = count // 4
    order = []
    for along in range(4):
        columns = range(1, across) if along % 2 == 0 else range(across - 1, 0, -1)
        order += [along * across + column for column in columns]
    return order + [along * across for along in reversed(range(4))]


def ring_shift(value, ring, step):
    count = len(ring)
    return lax.ppermute(
        value, "ctx", [(ring[i], ring[(i + step) % count]) for i in range(count)]
    )


def tie(*values):
    return lax.optimization_barrier(values)


class Gather:
    def __init__(self, value, ring):
        self.ring, self.half, self.step = ring, len(ring) // 2, 1
        self.first, self.ahead, self.behind, self.far = value, [], [], None
        self.up, self.down = tie(ring_shift(value, ring, 1), ring_shift(value, ring, -1))

    def advance(self, *others):
        self.ahead.append(self.down)
        self.behind.append(self.up)
        self.up, self.down, *others = tie(self.up, self.down, *others)
        self.step += 1
        up, down = self.up, self.down
        if self.step == self.half:
            cut = up.shape[0] // 2
            up, down = up[:cut], down[cut:]
        self.up, self.down = tie(ring_shift(up, self.ring, 1), ring_shift(down, self.ring, -1))
        return others

    def slots(self):
        while self.step < self.half:
            self.advance()
        return [self.first] + self.ahead + [self.up, self.down] + self.behind[::-1]


class Scatter:
    def __init__(self, terms, ring):
        self.ring, self.half, self.terms = ring, len(ring) // 2, terms
        self.up, self.down = terms[self.half : self.half + 2]
        self.step = self.half
        self.send()

    def send(self):
        self.up, self.down = tie(ring_shift(self.up, self.ring, 1), ring_shift(self.down, self.ring, -1))

    def advance(self, *others):
        self.up, self.down, *others = tie(self.up, self.down, *others)
        up, down, cut = self.terms[self.step - 1], self.terms[len(self.ring) + 2 - self.step], self.up.shape[0]
        if self.step == self.half:
            rows = up.shape[0]
            self.up = low(wide(up) + jnp.pad(wide(self.up), ((0, rows - cut), (0, 0))))
            self.down = low(wide(down) + jnp.pad(wide(self.down), ((rows - cut, 0), (0, 0))))
        else:
            self.up, self.down = add_low(up, self.up), add_low(down, self.down)
        self.up, self.down, *others = tie(self.up, self.down, *others)
        self.step -= 1
        self.send()
        return others

    def sums(self):
        while self.step > 1:
            self.advance()
        return [self.terms[0], self.up, self.down]


def ring_exchange(slots, ring):
    count = len(ring)
    result = [slots[0]] + [None] * (count - 1)
    for k in range(1, count):
        result[count - k] = ring_shift(slots[k], ring, k)
    return result


def exchange(array):
    return lax.all_to_all(array, "ctx", 0, 0, tiled=True)


def partner(value, count):
    return lax.ppermute(value, "fsdp", [(i, i ^ 1) for i in range(count)])


def chip_shift(value, count, step):
    return lax.ppermute(value, "fsdp", [(i, (i + 2 * step) % count) for i in range(count)])


def far_gather(value, count):
    return [value] + [chip_shift(value, count, -step) for step in range(1, count // 2)]


def near_gather(nears, count):
    slots = []
    for near in nears:
        slots += [near, partner(near, count)]
    return slots


def near_scatter(terms, count):
    return [add_low(terms[i], partner(terms[i + 1], count)) for i in range(0, count, 2)]


def far_scatter(nears, count):
    return [nears[0]] + [chip_shift(nears[step], count, step) for step in range(1, count // 2)]


def side_exchange(pieces, count, slots=None):
    chips = count // 2
    received = []
    for slot in range(count) if slots is None else slots:
        step, flip = (chips - slot // 2) % chips, slot % 2
        piece = pieces[2 * step + flip]
        if step or flip:
            pairs = [(i, ((i + 2 * step) % count) ^ flip) for i in range(count)]
            piece = lax.ppermute(piece, "fsdp", pairs)
        received.append(piece)
    return received


def add_low(left, right):
    return low(wide(left) + wide(right))


def total_of(terms):
    total = wide(terms[0])
    for term in terms[1:]:
        total = total + wide(term)
    return total


def body(
    tokens, cotangent, gain_attn, w_qkv, w_out, gain_ffn, w_gate_up, w_down, lengths, block_order
):
    rows, width = tokens.shape
    heads = HEADS
    depth = width // heads
    ctx = lax.axis_size("ctx")
    fsdp = lax.axis_size("fsdp")
    factor = 1.0 / math.sqrt(rows * ctx * fsdp)
    shard = width // fsdp
    hidden = w_down.shape[0]
    own_heads = heads // ctx
    own_width = own_heads * depth
    aligned = own_width % 128 == 0
    half = ctx // 2
    sub = shard // ctx
    lines = fsdp * sub
    ring = ring_of(ctx)
    chips = fsdp // 2
    entries = []
    for c in range(ctx):
        me = ring.index(c)
        for f in range(fsdp):
            owners = [ring[(me + k) % ctx] for k in range(ctx)]
            sides = [((f // 2 + s) % chips) * 2 + ((f % 2) ^ k) for s in range(chips) for k in (0, 1)]
            entries.append(owners + sides)
    device = lax.axis_index("ctx") * fsdp + lax.axis_index("fsdp")
    table = lax.dynamic_slice_in_dim(jnp.asarray(entries, jnp.int32), device, 1, 0)
    gain_one, gain_two = gain_attn.reshape(1, shard), gain_ffn.reshape(1, shard)
    f32 = jnp.float32
    gain_scratch = pltpu.VMEM((8, width), f32)
    square_scratch = pltpu.VMEM((width, width), jnp.bfloat16)

    going = Gather(tokens, ring)
    if aligned:
        (piece,) = call(
            "slice", functools.partial(slice_kernel, own_width),
            [shape((shard + 8, 3 * own_width))], [table, w_qkv, gain_one, gain_two],
            time=2.2,
        )
    else:
        mine = [
            lax.dynamic_slice(w_qkv, (0, part * width + table[0, 0] * own_width), (shard, own_width))
            for part in range(3)
        ]
        piece = jnp.concatenate(
            [jnp.concatenate(mine, axis=1), gain_rows(wide(gain_one), wide(gain_two), 3 * own_width)], axis=0
        )
    slices = far_gather(piece, fsdp)
    gate_pieces = call(
        "split", functools.partial(split_kernel, ctx),
        [shape((shard, 2 * hidden))] * fsdp, [table, w_gate_up],
        scratch=[pltpu.VMEM((fsdp, shard, 2 * hidden), jnp.bfloat16)],
        time=4,
    )
    sent = gate_pieces
    gate_pieces = [sent[0]] + side_exchange(sent, fsdp, range(1, 3)) + [None] * (fsdp - 3)
    slices, sent = going.advance(slices, sent)
    slices = near_gather(slices, fsdp)

    def project(slot):
        return call(
            "project", functools.partial(project_kernel, ctx),
            [shape(slot.shape), shape((slot.shape[0], 3 * own_width))], [table, slot] + slices,
            scratch=[gain_scratch, pltpu.VMEM((width, 3 * own_width), jnp.bfloat16)],
            time=2.6,
        )

    first = project(tokens)
    ahead, behind = [project(going.ahead[0])], [project(going.behind[0])]
    first, ahead[0], behind[0], gate_pieces[1:3] = going.advance(first, ahead[0], behind[0], gate_pieces[1:3])
    for step in range(1, half - 1):
        ahead.append(project(going.ahead[step]))
        behind.append(project(going.behind[step]))
        if step == 1:
            sent, unused = tie(sent, gate_pieces[1:3])
            gate_pieces[3:] = side_exchange(sent, fsdp, range(3, fsdp))
        if going.step < half:
            ahead[step], behind[step] = going.advance(ahead[step], behind[step])
    *far, ahead, behind, gate_pieces[3:] = tie(going.up, going.down, ahead, behind, gate_pieces[3:])
    far = [project(value) for value in far]
    later_out, far = tie(w_out, far)
    outs = far_gather(later_out, fsdp)
    pairs = [first] + ahead + far + behind[::-1]
    attn_slots, qkv = [pair[0] for pair in pairs], [pair[1] for pair in pairs]

    out_slots, out_t, log_total = attention_forward(
        table, lengths, block_order, qkv, ctx, own_heads, depth, TILE
    )
    near_out = partner(w_out, fsdp)
    out_slots, outs, near_out, gate_pieces = tie(out_slots, outs, near_out, gate_pieces)
    attn_parts = ring_exchange(out_slots, ring)
    later_cot, unused = tie(cotangent, out_slots[0])
    cots = far_gather(later_cot, fsdp)
    outs = [outs[0], near_out] + near_gather(outs[1:], fsdp)
    resid, ffn_in = call(
        "leave", functools.partial(leave_kernel, ctx, fsdp),
        [shape((rows, width), f32), shape((rows, width))],
        [table, tokens] + attn_parts + outs + slices,
        scratch=[gain_scratch, square_scratch],
        time=4.1,
    )

    ffn_in, cots = tie(ffn_in, cots)
    cots = near_gather(cots, fsdp)

    nears = far_gather(ffn_in, fsdp)
    ffns, grad_terms, out_terms, hiddens, grads = [], [], [], [], []
    for chip in range(chips):
        ffn_pair = [nears[chip], partner(nears[chip], fsdp)]
        result = call(
            "feed_forward", functools.partial(ffn_kernel, ctx, fsdp, 2),
            [shape((rows, width))] * 4 + [shape((2 * rows, hidden)), shape((2 * rows, 2 * hidden))],
            [table] + ffn_pair + cots[2 * chip : 2 * chip + 2] + gate_pieces + [w_down],
            scratch=[pltpu.VMEM((width, hidden), jnp.bfloat16)] * 2 + [pltpu.VMEM((2, rows, width), jnp.bfloat16)] * 2,
            time=9.5,
        )
        if chip == 0:
            result, nears[1:] = tie(result, nears[1:])
        ffns += ffn_pair
        grad_terms += result[0:2]
        out_terms += result[2:4]
        hiddens.append(result[4])
        grads.append(result[5])
    grad_nears = near_scatter(grad_terms, fsdp)
    hiddens, grad_nears = tie(hiddens, grad_nears)
    grad_parts = far_scatter(grad_nears, fsdp)
    terms_ffn = call(
        "feed_forward_weights", functools.partial(ffn_weight_kernel, ctx, fsdp),
        [shape((lines + lines // 2, 2 * hidden))] * half
        + [shape(((lines + lines // 2) // 2, 2 * hidden))] * 2
        + [shape((lines + lines // 2, 2 * hidden))] * (half - 1),
        [table] + ffns + cots + hiddens + grads,
        scratch=[pltpu.VMEM((fsdp, shard, 2 * hidden), jnp.bfloat16), pltpu.VMEM((fsdp, shard, hidden), jnp.bfloat16)],
        time=12,
    )
    grad_parts, unused = tie(grad_parts, terms_ffn[0])
    ffn_sums = Scatter(terms_ffn, ring)
    grad_resid, branch, *grad_attn = call(
        "branch", functools.partial(branch_kernel, ctx, fsdp, len(grad_parts)),
        [shape((rows, width), f32), shape((rows, width))] + [shape((rows, own_width))] * ctx,
        [table, resid, cotangent] + grad_parts + outs + slices,
        scratch=[gain_scratch, square_scratch],
        time=5,
    )
    grad_slots = ring_exchange(grad_attn, ring)
    out_sides = call(
        "out_weights", functools.partial(out_weight_kernel, ctx, fsdp),
        [shape((ctx, shard, own_width))] * fsdp, [table, branch] + attn_parts,
        scratch=[square_scratch],
        time=3.3,
    )
    out_nears = near_scatter(out_sides, fsdp)

    out_parts = far_scatter(out_nears, fsdp)
    part_out = low(total_of(out_parts))
    grad_slots, part_out = ffn_sums.advance(grad_slots, part_out)
    grad_qkv = attention_backward(
        table, lengths, block_order, qkv, grad_slots, part_out, out_t, log_total, own_heads, depth, TILE
    )
    first_half, second_half = w_qkv[: shard // 2], w_qkv[shard // 2 :]
    first_half, unused = tie(first_half, part_out)
    first_half = far_gather(first_half, fsdp)
    grad_qkv, first_half = ffn_sums.advance(grad_qkv, first_half)
    second_half, unused = tie(second_half, grad_qkv)
    second_half = far_gather(second_half, fsdp)
    qkv_sides = call(
        "qkv_weights", functools.partial(qkv_weight_kernel, len(attn_slots), ctx, fsdp),
        [shape((shard, 3 * own_width))] * fsdp, [table] + attn_slots + [grad_qkv],
        scratch=[pltpu.VMEM((fsdp, shard, 3 * own_width), jnp.bfloat16)],
        time=6,
    )
    if ffn_sums.step > 1:
        grad_qkv, qkv_sides = ffn_sums.advance(grad_qkv, qkv_sides)
    qkv_sum = far_scatter(near_scatter(qkv_sides, fsdp), fsdp)

    qkv_sum = ffn_sums.advance(qkv_sum)[0] if ffn_sums.step > 1 else qkv_sum
    own_sum, ffn_up, ffn_down = ffn_sums.sums()
    ffn_up, ffn_down, grad_qkv, qkv_sum, second_half = tie(ffn_up, ffn_down, grad_qkv, qkv_sum, second_half)
    first_half, second_half = near_gather(first_half, fsdp), near_gather(second_half, fsdp)
    grad_back = exchange(grad_qkv)
    *gate_sides, rest = call(
        "cut", functools.partial(cut_kernel, ctx),
        [shape((sub, 2 * hidden))] * fsdp + [shape((lines // 2, 2 * hidden))],
        [table, own_sum, ffn_up, ffn_down],
        scratch=[pltpu.VMEM((lines + lines // 2, 2 * hidden), jnp.bfloat16)],
        time=3,
    )
    gate_sides = side_exchange(gate_sides, fsdp)
    (packed,) = call(
        "pack", functools.partial(pack_kernel, ctx),
        [shape((lines + lines // 2, 2 * hidden))], [table, rest] + gate_sides,
        time=2,
    )
    ffn_going = Gather(packed, ring)
    (joined,) = call(
        "join", functools.partial(join_kernel, len(qkv_sum)),
        [shape((shard, 4 * own_width))], [table] + qkv_sum + [grad_back],
        time=2.5,
    )
    (joined,) = ffn_going.advance(joined)
    attn_going = Gather(joined, ring)
    weights = [piece for pair in zip(first_half, second_half) for piece in pair]
    (grad_tokens,) = call(
        "tail", functools.partial(tail_kernel, ctx, fsdp),
        [shape((rows, width))], [table, tokens, grad_resid, grad_back] + weights + slices,
        scratch=[gain_scratch, pltpu.VMEM((rows, width), f32), pltpu.VMEM((rows, 3 * width), jnp.bfloat16)],
        time=8,
    )
    (grad_tokens,) = ffn_going.advance(grad_tokens)
    results = [
        shape((shard, 2 * hidden * fsdp), f32), shape((hidden, width), f32),
        shape((shard, 3 * width), f32), shape((shard, width), f32),
    ]
    inputs = [table, w_gate_up, gain_two, w_qkv if aligned else unmixed(relative(w_qkv, table, ctx), ctx, own_width), gain_one]
    inputs += ffn_going.slots() + attn_going.slots()
    scratch = [pltpu.VMEM(x.shape, f32) for x in results] + [pltpu.VMEM((width, hidden), jnp.bfloat16)]
    scratch += [pltpu.VMEM((ctx,) + packed.shape, jnp.bfloat16), pltpu.VMEM((ctx,) + joined.shape, jnp.bfloat16)]
    *results, grad_gain_ffn, grad_gain_attn = pl.pallas_call(
        functools.partial(final_kernel, ctx, fsdp, factor, aligned),
        out_shape=results + [shape((1, shard), f32)] * 2,
        in_specs=[SM] + [VM] * (len(inputs) - 1),
        out_specs=[pl.BlockSpec(memory_space=pltpu.HBM)] * 4 + [VM] * 2,
        scratch_shapes=scratch + [pltpu.SemaphoreType.DMA((4,))],
        compiler_params=room(inputs[1:] + scratch, 8),
        cost_estimate=cost(6),
        name="final",
    )(*inputs)
    grad_w_gate_up, grad_w_down, grad_w_qkv, grad_w_out = results
    if not aligned:
        grad_w_qkv, grad_w_out = ordered(grad_w_qkv, table, 3, ctx), ordered(grad_w_out, table, 1, ctx)
    output = low(resid + total_of(far_scatter(near_scatter(out_terms, fsdp), fsdp)))
    return (
        output,
        grad_tokens,
        grad_gain_attn.reshape(shard),
        grad_w_qkv,
        grad_w_out,
        grad_gain_ffn.reshape(shard),
        grad_w_gate_up,
        grad_w_down,
    )


def relative(weight, table, ctx):
    rows = weight.shape[0]
    parts = weight.reshape(rows, 3, ctx, -1)
    slots = [lax.dynamic_index_in_dim(parts, table[0, k], 2, keepdims=False) for k in range(ctx)]
    return jnp.concatenate([slot.reshape(rows, -1) for slot in slots], axis=1)


def unmixed(weight, ctx, own_width):
    rows = weight.shape[0]
    return weight.reshape(rows, ctx, 3, own_width).transpose(0, 2, 1, 3).reshape(rows, -1)


def ordered(array, table, parts, ctx):
    rows = array.shape[0]
    split = array.reshape(rows, parts, ctx, -1)
    result = jnp.zeros_like(split)
    for k in range(ctx):
        result = lax.dynamic_update_slice(result, split[:, :, k : k + 1], (0, 0, table[0, k], 0))
    return result.reshape(rows, -1)


def solution(mesh):
    in_specs = (
        P(("fsdp", "ctx"), None),
        P(("fsdp", "ctx"), None),
        P("fsdp"),
        P("fsdp", None),
        P("fsdp", None),
        P("fsdp"),
        P("fsdp", None),
        P("fsdp", None),
        P("fsdp", None),
        P("fsdp", None),
    )
    out_specs = (
        P(("fsdp", "ctx"), None),
        P(("fsdp", "ctx"), None),
        P("fsdp"),
        P("fsdp", None),
        P("fsdp", None),
        P("fsdp"),
        P("fsdp", None),
        P("fsdp", None),
    )
    return jax.shard_map(body, mesh=mesh, in_specs=in_specs, out_specs=out_specs, check_vma=False)
```
